32 devices in a mesh: groups: 2 (over y), rel: 4 (over z), bin: 2 (over x), rep: 2 (over core).
Axes of the slice: x: 2, y: 2, z: 4, core: 2. Of those that a mesh axis runs over, the one named last changes fastest.
Arguments:
- footprint: bfloat16 [192, 128, 128], P(('groups', 'rel', 'bin', 'rep')), parts along dimension 0, as said below
- block_tile: int32 [192], P(('groups', 'rel', 'bin', 'rep')), parts along dimension 0, may hold values from 0 to 31, as said below
- log_release: float32 [1024, 32], P(('groups', 'rel')), parts along dimension 0, may hold values from -4 to 4
- prior_mean: float32 [1024, 32], P(('groups', 'rel')), parts along dimension 0, may hold values from -4 to 4
- prior_weight: float32 [1024, 32], P(('groups', 'rel')), parts along dimension 0, may hold values from 0.5 to 2
- observed: float32 [256, 32, 128], P(('groups', 'rel', 'bin', 'rep')), parts along dimension 0, may hold values from -6 to 6
- noise_weight: float32 [256, 32, 128], P(('groups', 'rel', 'bin', 'rep')), parts along dimension 0, may hold values from 0.5 to 2
- pixel_mask: int32 [256, 128], P(('groups', 'rel', 'bin', 'rep')), parts along dimension 0, may hold values 0 or 1
Outputs:
- release_new: float32 [1024, 32], P(('groups', 'rel'), ('bin', 'rep')), parts along dimension 0
- residual: float32 [256, 32, 128], P(('groups', 'rel', 'bin', 'rep')), parts along dimension 0
The draws below stay inside these ranges and needn't reach their ends.
There are 2 independent parts, one for each index of `groups`. The reference program is written for one: setup_inputs(seed, part) draws one part's arguments, and reference() takes and returns one part's arrays. A program takes and returns all parts, laid end to end along the dimension named above; each array names one. Nothing has to cross between parts.
Inputs may be any that keep to these rules, and one draw needn't show every extreme that they name: `footprint`: Real-valued sensitivities. `block_tile`: values are indices among the 32 swath tiles of the devices with the same bin and rep indices: owner value // 8 along rel, local tile value % 8. A device's list is grouped by owner in ascending order; at most 2 entries name one owner, and those name different tiles. In every group of devices with equal bin and rep indices, one owner is named 2 times by every device of the group.
All inputs are finite; a program needn't handle non-finite values. No bound on the sum of `pixel_mask` on one device may be relied on, other than what follows from the above.
Results may differ from the reference program's by a relative error of at most 0.002.
Values may be sent and summed in bfloat16 or wider, within the bound.
No kernel may reach another device: no remote copies, remote signals or barrier semaphores. Data moves between devices by JAX's collectives and lax.ppermute only.
A program may use at most 64 MiB of HBM per device.

```python
import math
import jax
import jax.numpy as jnp
from jax import lax

BINS = 32
REL_DEV = 128
TILE = 128
CAP = 2
TILE_DEV = 8
OWNERS = 4
PLANES = 4
KB = 6
SLOTS = 8
BLOCKS = 96
TILES = 128
RELEASES = 512


def correlation_tables(key):
    devices = OWNERS * PLANES
    hot_owner = jax.random.randint(jax.random.fold_in(key, 11), (PLANES,), 0, OWNERS)
    device_keys = jax.random.split(jax.random.fold_in(key, 12), devices)
    offsets = jax.random.randint(jax.random.fold_in(key, 13), (devices, OWNERS), 0, TILE_DEV)
    slot_owner = jnp.arange(SLOTS, dtype=jnp.int32) // CAP
    within = jnp.arange(CAP, dtype=jnp.int32)

    def one_device(device_key, device, offset_row):
        plane = device % PLANES
        scores = jax.random.permutation(device_key, SLOTS).astype(jnp.int32)
        scores = jnp.where(slot_owner == hot_owner[plane], -1, scores)
        ranked = jnp.argsort(scores, stable=True)
        taken = jnp.zeros((SLOTS,), jnp.int32).at[ranked[:KB]].set(1)
        counts = taken.reshape(OWNERS, CAP).sum(axis=1)
        local = (offset_row[:, None] + within[None, :]) % TILE_DEV
        return jnp.where(within[None, :] < counts[:, None], local, -1).astype(jnp.int32)
    return jax.vmap(one_device)(device_keys, jnp.arange(devices, dtype=jnp.int32), offsets)


def draw_footprint(key, part):
    sigma = (TILE * KB * PLANES / 4.0) ** (-0.5)
    width = REL_DEV / 8.0
    noise = jnp.clip(jax.random.normal(jax.random.fold_in(key, 21), (BLOCKS, REL_DEV, TILE), jnp.float32), -5.0, 5.0)
    signs = (jax.random.randint(jax.random.fold_in(key, 22), (BLOCKS,), 0, 2) * 2 - 1).astype(jnp.float32)
    pattern = jnp.exp(jax.random.uniform(jax.random.fold_in(key, 23), (BLOCKS, TILE), jnp.float32, -1.1, 1.1)) * signs[:, None]
    centre = jax.random.uniform(jax.random.fold_in(key, 24), (BLOCKS,), jnp.float32, 0.0, REL_DEV * 1.0)
    place = jnp.arange(REL_DEV, dtype=jnp.float32)
    apart = jnp.abs(place[None, :] - centre[:, None])
    apart = jnp.minimum(apart, REL_DEV - apart)
    bump = jnp.exp(-0.5 * (apart / width) ** 2)
    rough = jax.random.uniform(jax.random.fold_in(key, 25), (BLOCKS, REL_DEV), jnp.float32, 0.5, 1.5)
    profile = rough * bump
    values = sigma * (noise + profile[:, :, None] * pattern[:, None, :])
    return values.astype(jnp.bfloat16)


def draw_block_tile(key, part):
    tables = correlation_tables(jax.random.fold_in(key, 5))
    owner_ids = jnp.arange(OWNERS, dtype=jnp.int32)[None, :, None]
    values = jnp.where(tables >= 0, owner_ids * TILE_DEV + tables, -1)
    flat = values.reshape(OWNERS * PLANES, SLOTS)
    order = jnp.argsort((flat < 0).astype(jnp.int32), axis=1, stable=True)[:, :KB]
    picked = jnp.take_along_axis(flat, order, axis=1)
    return picked.reshape(BLOCKS).astype(jnp.int32)


def place_ends(values, own_key, smallest, high):
    longest = values.shape.index(max(values.shape))
    spots = []
    for shift in (0, 1):
        where = [jax.random.randint(jax.random.fold_in(own_key, axis), (), 0, length) for axis, length in enumerate(values.shape)]
        where[longest] = (where[longest] + shift) % values.shape[longest]
        spots.append(tuple(where))
    return values.at[spots[0]].set(smallest).at[spots[1]].set(high)


def block_levels(stream_key, extent, cuts, low, top_value):
    gain, own = 1.0, jax.random.fold_in(stream_key, 6)
    for dim, blocks in cuts:
        heights = jnp.exp(jax.random.uniform(jax.random.fold_in(own, dim), (blocks,), jnp.float32, low / len(cuts), top_value / len(cuts)))
        gain = gain * jnp.repeat(heights, extent[dim] // blocks).reshape([-1 if axis == dim else 1 for axis in range(len(extent))])
    return gain


def bell_draw(own_key, shape, deviation, reach, shards=(), kind=jnp.bfloat16):
    array = jax.random.normal(own_key, shape, jnp.float32) * deviation
    if len(shards) > 0:
        array = block_levels(own_key, shape, shards, -0.22, 0.18) * array
    return jnp.clip(array, min=-reach, max=reach).astype(kind)


def setup_inputs(seed: int = 0, part: int = 0) -> dict:
    splits = jax.random.split(jax.random.key(seed), 9)
    own_keys = jax.random.split(jax.random.fold_in(splits[8], part), 9)
    return {
        "footprint": draw_footprint(jax.random.fold_in(jax.random.fold_in(splits[8], part), 71), part),
        "block_tile": draw_block_tile(jax.random.fold_in(jax.random.fold_in(splits[8], part), 71), part),
        "log_release": bell_draw(own_keys[2], (RELEASES, BINS), 1.0, 4.0, ((0, 4),), jnp.float32),
        "prior_mean": bell_draw(own_keys[3], (RELEASES, BINS), 1.0, 4.0, ((0, 4),), jnp.float32),
        "prior_weight": jnp.clip(jnp.exp(math.log(2.0) - 1.3862944 * jax.random.uniform(own_keys[4], (RELEASES, BINS), jnp.float32) ** block_levels(own_keys[4], (RELEASES, BINS), ((0, 4),), -0.2, 0.2)), 0.5, 2.0),
        "observed": bell_draw(own_keys[5], (TILES, BINS, TILE), 1.0, 6.0, ((0, 16),), jnp.float32),
        "noise_weight": jnp.clip(jnp.exp(math.log(2.0) - 1.3862944 * jax.random.uniform(own_keys[6], (TILES, BINS, TILE), jnp.float32) ** block_levels(own_keys[6], (TILES, BINS, TILE), ((0, 16),), -0.2, 0.2)), 0.5, 2.0),
        "pixel_mask": place_ends((jax.random.randint(own_keys[7], (TILES, TILE), 0, 10) < 7).astype(jnp.int32), jax.random.fold_in(own_keys[7], 1), 0, 1),
    }


def newton_update(gram_sum, gradient, release_part, mean_part, weight_part):
    slopes = jax.nn.sigmoid(release_part).T
    prior_diag = weight_part.T
    matrix = slopes[:, :, None] * gram_sum * slopes[:, None, :]
    matrix = 0.5 * (matrix + jnp.swapaxes(matrix, 1, 2))
    identity = jnp.eye(matrix.shape[1], dtype=jnp.float32)
    matrix = matrix + prior_diag[:, :, None] * identity[None]
    right_side = slopes * gradient - prior_diag * (release_part - mean_part).T
    factor = jnp.linalg.cholesky(matrix)
    partial_sol = jax.scipy.linalg.solve_triangular(factor, right_side[:, :, None], lower=True)
    update_step = jax.scipy.linalg.solve_triangular(factor, partial_sol, lower=True, trans=1)[:, :, 0]
    return release_part + update_step.T

def reference(footprint, block_tile, log_release, prior_mean, prior_weight, observed, noise_weight, pixel_mask):
    per_owner = KB * PLANES
    block_plane = jnp.arange(BLOCKS, dtype=jnp.int32) // KB % PLANES
    tile_of = (block_tile // TILE_DEV * PLANES + block_plane) * TILE_DEV + block_tile % TILE_DEV
    rates = jax.nn.softplus(log_release).astype(jnp.bfloat16)
    prints = footprint.reshape(OWNERS, per_owner, REL_DEV, TILE)
    tile_ids = tile_of.reshape(OWNERS, per_owner).astype(jnp.int32)
    owner_rates = rates.reshape(OWNERS, REL_DEV, BINS)

    def add_owner(running, pieces):
        block_prints, block_tiles, block_rates = pieces
        emission = jnp.einsum('rb,krp->kbp', block_rates.astype(jnp.float32), block_prints.astype(jnp.float32))
        return (running + jax.ops.segment_sum(emission, block_tiles, num_segments=TILES), None)
    predicted, _ = lax.scan(add_owner, jnp.zeros((TILES, BINS, TILE), jnp.float32), (prints, tile_ids, owner_rates))
    weight = pixel_mask[:, None, :].astype(jnp.float32) * noise_weight
    residual = weight * (observed - predicted)
    resid_half = residual.astype(jnp.bfloat16)
    weight_half = weight.astype(jnp.bfloat16)
    group = math.gcd(per_owner, 16)

    def solve_owner(pieces):
        block_prints, block_tiles, release_part, mean_part, weight_part = pieces
        prints_wide = block_prints.astype(jnp.float32)
        resid_rows = resid_half[block_tiles].astype(jnp.float32)
        weight_rows = weight_half[block_tiles]
        gradient = jnp.einsum('kbp,krp->br', resid_rows, prints_wide)

        def add_group(counter, running):
            start = (counter * group).astype(jnp.int32)
            group_prints = lax.dynamic_slice_in_dim(prints_wide, start, group, 0)
            group_weights = lax.dynamic_slice_in_dim(weight_rows, start, group, 0).astype(jnp.float32)
            scaled = (group_prints[:, None, :, :] * group_weights[:, :, None, :]).astype(jnp.bfloat16)
            scaled = lax.optimization_barrier(scaled).astype(jnp.float32)
            return running + jnp.einsum('kbrp,ksp->brs', scaled, group_prints)
        gram_sum = lax.fori_loop(0, per_owner // group, add_group, jnp.zeros((BINS, REL_DEV, REL_DEV), jnp.float32))
        return newton_update(gram_sum, gradient, release_part, mean_part, weight_part)
    release_new = lax.map(solve_owner, (prints, tile_ids, log_release.reshape(OWNERS, REL_DEV, BINS), prior_mean.reshape(OWNERS, REL_DEV, BINS), prior_weight.reshape(OWNERS, REL_DEV, BINS)))
    return (release_new.reshape(RELEASES, BINS), residual)
```

```python
import functools
import math

import jax
import jax.numpy as jnp
from jax import lax
from jax.experimental import pallas as pl
from jax.experimental.pallas import tpu as pltpu
from jax.sharding import PartitionSpec as P

PIVOTS = 8
ROWS = 8
LIMIT = 48 << 20
F32 = jnp.float32
BF16 = jnp.bfloat16


def emission_kernel(tiles, capacity, group, tile_of, release, prints, sent, message):
    blocks, releases, pixels = prints.shape
    slots, padded, _ = sent.shape
    bins = padded - ROWS
    value = release[...]
    rates = (jnp.maximum(value, 0.0) + jnp.log1p(jnp.exp(-jnp.abs(value)))).astype(BF16)
    sent[...] = jnp.full(sent.shape, -1.0, F32)
    owner, rank = None, None
    targets = []
    for k in range(blocks):
        mine = lax.div(tile_of[k], tiles)
        rank = jnp.where(mine == owner, rank + 1, 0) if k else 0
        owner = mine
        target = owner * capacity + rank
        emission = lax.dot_general(
            rates, prints[k], (((0,), (0,)), ((), ())), preferred_element_type=F32
        )
        local = lax.rem(tile_of[k], tiles).astype(F32)
        sent[target, :bins, :] = emission
        sent[target, bins:, :] = jnp.full((ROWS, pixels), local, F32)
        targets.append(jnp.full((1, pixels), target.astype(F32), F32))
    for chunk in range(blocks // group):
        first = chunk * group
        for j in range(group):
            message[chunk, j * releases : (j + 1) * releases, :] = prints[first + j]
        rows = targets[first : first + group]
        rows.append(jnp.full((2 * ROWS - group, pixels), -1.0, F32))
        message[chunk, group * releases :, :] = jnp.concatenate(rows, 0).astype(BF16)


def residual_kernel(planes, capacity, arrived, observed, noise, mask, residual, weights, back):
    slots, padded, pixels = arrived.shape
    tiles, bins, _ = observed.shape
    share = bins // planes
    owners = slots // capacity

    def one_tile(t):
        def add(s, running):
            match = arrived[s, bins : bins + 1, :] == t.astype(F32)
            return running + jnp.where(match, arrived[s, :bins, :], 0.0)

        predicted = lax.fori_loop(0, slots, add, jnp.zeros((bins, pixels), F32), unroll=slots <= 8)
        weight = mask[pl.ds(t, 1), :].astype(F32) * noise[t]
        weights[t] = weight
        residual[t] = weight * (observed[t] - predicted)

    pl.loop(0, tiles, unroll=True)(one_tile)

    def one_owner(c):
        pieces = []
        for rank in range(capacity):
            s = c * capacity + rank
            place = arrived[s, bins : bins + 1, :]
            misfit = jnp.zeros((bins, pixels), F32)
            weight = jnp.zeros((bins, pixels), F32)
            for t in range(tiles):
                match = place == float(t)
                misfit = jnp.where(match, residual[t], misfit)
                weight = jnp.where(match, weights[t], weight)
            pieces.append((misfit, weight))
        for e in range(planes):
            rows = slice(e * share, (e + 1) * share)
            parts = [part[rows] for pair in pieces for part in pair]
            back[c * planes + e] = jnp.concatenate(parts, 0).astype(BF16)

    pl.loop(0, owners, unroll=owners <= 4)(one_owner)


def three_parts(values):
    high = values.astype(BF16).astype(F32)
    rest = values - high
    middle = rest.astype(BF16).astype(F32)
    return high, middle, rest - middle


def pivot_rows(rows, base, lane):
    width = lane.shape[1]
    inside = (lane >= base) & (lane < base + PIVOTS)
    out = [
        jnp.where(inside, jnp.where(lane == base + t, 1.0, 0.0), rows[t]) for t in range(PIVOTS)
    ]
    turned = [pltpu.roll(row, width - base, 1) for row in rows]
    block = [
        [jnp.broadcast_to(row[:, u : u + 1], lane.shape) for u in range(PIVOTS)] for row in turned
    ]
    for j in range(PIVOTS):
        inverse = 1.0 / block[j][j]
        out[j] = out[j] * inverse
        for u in range(j + 1, PIVOTS):
            block[j][u] = block[j][u] * inverse
        for i in range(PIVOTS):
            if i != j:
                factor = block[i][j]
                out[i] = out[i] - factor * out[j]
                for u in range(j + 1, PIVOTS):
                    block[i][u] = block[i][u] - factor * block[j][u]
    return [jnp.where(inside, -row, row) for row in out]


def sweep(matrix, panel, width):
    lane = lax.broadcasted_iota(jnp.int32, (ROWS, width), 1)
    thin = lax.broadcasted_iota(jnp.int32, (1, width), 1)

    def one_panel(step, carry):
        base = pl.multiple_of(step * PIVOTS, PIVOTS)
        rows = [matrix[pl.ds(base + t, ROWS, stride=width), :] for t in range(PIVOTS)]
        old = [matrix[pl.ds(b * width + base, PIVOTS), :] for b in range(ROWS)]
        new = pivot_rows(rows, base, lane)
        for t in range(PIVOTS):
            panel[pl.ds(t, ROWS, stride=PIVOTS), :] = new[t]
        inside = (thin >= base) & (thin < base + PIVOTS)
        mine = [panel[b * PIVOTS : (b + 1) * PIVOTS, :] for b in range(ROWS)]
        for b in range(ROWS):
            a1, a2, a3 = three_parts(old[b])
            b1, b2, b3 = three_parts(mine[b])
            left = jnp.concatenate([a1, a1, a2, a2, a1, a3], 0).astype(BF16)
            right = jnp.concatenate([b1, b2, b1, b2, b3, b1], 0).astype(BF16)
            change = lax.dot_general(
                left, right, (((0,), (0,)), ((), ())), preferred_element_type=F32
            )
            whole = slice(b * width, (b + 1) * width)
            matrix[whole, :] = jnp.where(inside, 0.0, matrix[whole, :]) - change
        for b in range(ROWS):
            matrix[pl.ds(b * width + base, PIVOTS), :] = mine[b]
        return carry

    lax.fori_loop(0, width // PIVOTS, one_panel, 0)


def minus_product(matrix, vector, width):
    total = [jnp.zeros(vector.shape, F32) for _ in range(4)]
    for k in range(width):
        factor = jnp.broadcast_to(vector[:, k : k + 1], vector.shape)
        total[k % 4] = total[k % 4] - factor * matrix[pl.ds(k, ROWS, stride=width), :]
    return (total[0] + total[1]) + (total[2] + total[3])


def newton_kernel(
    planes, capacity, group, plane, prints, back, release, mean, prior, out, left, gram, panel
):
    _, chunks, height, pixels = prints.shape
    sources, depth, _ = back.shape
    owners = sources // planes
    bins = release.shape[1]
    releases = release.shape[0]
    share = bins // planes
    pair = 2 * share
    top = share * releases
    gram[...] = jnp.zeros(gram.shape, F32)

    def one_chunk(step, carry):
        e, chunk = lax.div(step, chunks), lax.rem(step, chunks)
        targets = prints[e, chunk, group * releases :, :].astype(F32)
        values = []
        for o in range(owners):
            block = back[o * planes + e].astype(F32)
            values.extend(block[r * pair : (r + 1) * pair] for r in range(capacity))
        for j in range(group):
            picked = jnp.zeros((pair, pixels), F32)
            for s, value in enumerate(values):
                picked = jnp.where(targets[j : j + 1] == float(s), value, picked)
            columns = slice(j * pixels, (j + 1) * pixels)
            block = prints[e, chunk, j * releases : (j + 1) * releases, :]
            for b in range(share):
                weight = jnp.broadcast_to(picked[share + b : share + b + 1], (2 * ROWS, pixels))
                weight = weight.astype(BF16)
                for r in range(0, releases, 2 * ROWS):
                    rows = slice(b * releases + r, b * releases + r + 2 * ROWS)
                    left[rows, columns] = block[r : r + 2 * ROWS] * weight
            if pair < 2 * ROWS:
                picked = jnp.concatenate(
                    [picked, jnp.zeros((2 * ROWS - pair, pixels), F32)], 0
                )
            left[top:, columns] = picked.astype(BF16)
        right = jnp.concatenate(
            [prints[e, chunk, j * releases : (j + 1) * releases, :] for j in range(group)], 1
        )
        gram[: top + 2 * ROWS, :] += lax.dot_general(
            left[...], right, (((1,), (1,)), ((), ())), preferred_element_type=F32
        )
        return carry

    lax.fori_loop(0, planes * chunks, one_chunk, 0)

    def own(array):
        rows = array[...].T
        mine = rows[:share]
        for e in range(1, planes):
            mine = jnp.where(plane[0] == e, rows[e * share : (e + 1) * share], mine)
        if share < ROWS:
            mine = jnp.concatenate([mine, jnp.zeros((ROWS - share, releases), F32)], 0)
        return mine

    log_release, prior_mean, prior_weight = own(release), own(mean), own(prior)
    unslope = 1.0 + jnp.exp(-log_release)
    gradient = gram[top : top + ROWS, :]
    right_side = gradient - prior_weight * (log_release - prior_mean) * unslope
    diagonal = prior_weight * unslope * unslope
    row = lax.broadcasted_iota(jnp.int32, (releases, releases), 0)
    column = lax.broadcasted_iota(jnp.int32, (releases, releases), 1)
    for b in range(ROWS):
        block = slice(b * releases, (b + 1) * releases)
        if b < share:
            matrix = gram[block, :]
            matrix = 0.5 * (matrix + matrix.T)
            gram[block, :] = matrix + jnp.where(row == column, diagonal[b : b + 1], 0.0)
        else:
            gram[block, :] = jnp.where(row == column, 1.0, 0.0)
    sweep(gram, panel, releases)
    update = log_release + unslope * minus_product(gram, right_side, releases)
    out[...] = update.T[:, :share]


def params():
    return pltpu.CompilerParams(vmem_limit_bytes=LIMIT)


def body(
    footprint, block_tile, log_release, prior_mean, prior_weight, observed, noise_weight, pixel_mask
):
    blocks, releases, pixels = footprint.shape
    owners = lax.axis_size("rel")
    planes = lax.axis_size(("bin", "rep"))
    tiles, bins, _ = observed.shape
    capacity = blocks * 4 // 3 // owners
    slots = owners * capacity
    share = bins // planes
    group = math.gcd(blocks, 6)
    chunks = blocks // group
    scalars = pl.BlockSpec(memory_space=pltpu.SMEM)
    local = pl.BlockSpec(memory_space=pltpu.VMEM)

    sent, message = pl.pallas_call(
        functools.partial(emission_kernel, tiles, capacity, group),
        out_shape=(
            jax.ShapeDtypeStruct((slots, bins + ROWS, pixels), F32),
            jax.ShapeDtypeStruct((chunks, group * releases + 2 * ROWS, pixels), BF16),
        ),
        in_specs=[scalars, local, local],
        out_specs=(local, local),
        compiler_params=params(),
    )(block_tile, log_release, footprint)
    arrived = lax.all_to_all(sent, "rel", split_axis=0, concat_axis=0, tiled=True)
    prints = lax.all_gather(message, ("bin", "rep"), axis=0, tiled=False)

    residual, _, back = pl.pallas_call(
        functools.partial(residual_kernel, planes, capacity),
        out_shape=(
            jax.ShapeDtypeStruct(observed.shape, F32),
            jax.ShapeDtypeStruct(observed.shape, F32),
            jax.ShapeDtypeStruct((owners * planes, capacity * 2 * share, pixels), BF16),
        ),
        in_specs=[local] * 4,
        out_specs=(local, local, local),
        compiler_params=params(),
    )(arrived, observed, noise_weight, pixel_mask)
    back = lax.all_to_all(back, ("rel", "bin", "rep"), split_axis=0, concat_axis=0, tiled=True)

    plane = lax.axis_index(("bin", "rep")).astype(jnp.int32).reshape(1)
    height = share * releases + 2 * ROWS
    release_new = pl.pallas_call(
        functools.partial(newton_kernel, planes, capacity, group),
        out_shape=jax.ShapeDtypeStruct((releases, share), F32),
        in_specs=[scalars] + [local] * 5,
        out_specs=local,
        scratch_shapes=[
            pltpu.VMEM((height, group * pixels), BF16),
            pltpu.VMEM((max(height, ROWS * releases), releases), F32),
            pltpu.VMEM((ROWS * PIVOTS, releases), F32),
        ],
        compiler_params=params(),
    )(plane, prints, back, log_release, prior_mean, prior_weight)
    return (release_new, residual)


def solution(mesh):
    in_specs = (
        P(("groups", "rel", "bin", "rep"), None, None),
        P(("groups", "rel", "bin", "rep")),
        P(("groups", "rel"), None),
        P(("groups", "rel"), None),
        P(("groups", "rel"), None),
        P(("groups", "rel", "bin", "rep"), None, None),
        P(("groups", "rel", "bin", "rep"), None, None),
        P(("groups", "rel", "bin", "rep"), None),
    )
    out_specs = (
        P(("groups", "rel"), ("bin", "rep")),
        P(("groups", "rel", "bin", "rep"), None, None),
    )
    return jax.shard_map(body, mesh=mesh, in_specs=in_specs, out_specs=out_specs, check_vma=False)
```

```python
import functools
import math

import jax
import jax.numpy as jnp
from jax import lax
from jax.experimental import pallas as pl
from jax.experimental.pallas import tpu as pltpu
from jax.sharding import PartitionSpec as P

PIVOTS = 8
ROWS = 8
LIMIT = 48 << 20
F32 = jnp.float32
BF16 = jnp.bfloat16


def emission_kernel(tiles, capacity, group, tile_of, release, prints, sent, message):
    blocks, releases, pixels = prints.shape
    slots, padded, _ = sent.shape
    bins = padded - ROWS
    value = release[...]
    rates = (jnp.maximum(value, 0.0) + jnp.log1p(jnp.exp(-jnp.abs(value)))).astype(BF16)
    sent[...] = jnp.full(sent.shape, -1.0, F32)
    owner, rank = None, None
    targets = []
    for k in range(blocks):
        mine = lax.div(tile_of[k], tiles)
        rank = jnp.where(mine == owner, rank + 1, 0) if k else 0
        owner = mine
        target = owner * capacity + rank
        emission = lax.dot_general(
            rates, prints[k], (((1,), (0,)), ((), ())), preferred_element_type=F32
        )
        local = lax.rem(tile_of[k], tiles).astype(F32)
        sent[target, :bins, :] = emission
        sent[target, bins:, :] = jnp.full((ROWS, pixels), local, F32)
        targets.append(jnp.full((1, pixels), target.astype(F32), F32))
    for chunk in range(blocks // group):
        first = chunk * group
        for j in range(group):
            message[chunk, j * releases : (j + 1) * releases, :] = prints[first + j]
        rows = targets[first : first + group]
        rows.append(jnp.full((2 * ROWS - group, pixels), -1.0, F32))
        message[chunk, group * releases :, :] = jnp.concatenate(rows, 0).astype(BF16)


def residual_kernel(planes, capacity, arrived, observed, noise, mask, residual, back, weights):
    slots, padded, pixels = arrived.shape
    tiles, bins, _ = observed.shape
    share = bins // planes
    owners = slots // capacity

    def one_tile(t):
        def add(s, running):
            match = arrived[s, bins : bins + 1, :] == t.astype(F32)
            return running + jnp.where(match, arrived[s, :bins, :], 0.0)

        predicted = lax.fori_loop(0, slots, add, jnp.zeros((bins, pixels), F32), unroll=slots <= 8)
        weight = mask[pl.ds(t, 1), :].astype(F32) * noise[t]
        weights[t] = weight
        residual[t] = weight * (observed[t] - predicted)

    pl.loop(0, tiles, unroll=True)(one_tile)

    def one_owner(c):
        pieces = []
        for rank in range(capacity):
            s = c * capacity + rank
            place = arrived[s, bins : bins + 1, :]
            misfit = jnp.zeros((bins, pixels), F32)
            weight = jnp.zeros((bins, pixels), F32)
            for t in range(tiles):
                match = place == float(t)
                misfit = jnp.where(match, residual[t], misfit)
                weight = jnp.where(match, weights[t], weight)
            pieces.append((misfit, weight))
        for e in range(planes):
            rows = slice(e * share, (e + 1) * share)
            parts = [part[rows] for pair in pieces for part in pair]
            back[c * planes + e] = jnp.concatenate(parts, 0).astype(BF16)

    pl.loop(0, owners, unroll=owners <= 4)(one_owner)


def three_parts(values):
    high = values.astype(BF16).astype(F32)
    rest = values - high
    middle = rest.astype(BF16).astype(F32)
    return high, middle, rest - middle


def pivot_rows(rows, base, lane):
    width = lane.shape[1]
    inside = (lane >= base) & (lane < base + PIVOTS)
    out = [
        jnp.where(inside, jnp.where(lane == base + t, 1.0, 0.0), rows[t]) for t in range(PIVOTS)
    ]
    turned = [pltpu.roll(row, width - base, 1) for row in rows]
    block = [
        [jnp.broadcast_to(row[:, u : u + 1], lane.shape) for u in range(PIVOTS)] for row in turned
    ]
    for j in range(PIVOTS):
        inverse = 1.0 / block[j][j]
        out[j] = out[j] * inverse
        for u in range(j + 1, PIVOTS):
            block[j][u] = block[j][u] * inverse
        for i in range(PIVOTS):
            if i != j:
                factor = block[i][j]
                out[i] = out[i] - factor * out[j]
                for u in range(j + 1, PIVOTS):
                    block[i][u] = block[i][u] - factor * block[j][u]
    return [jnp.where(inside, -row, row) for row in out]


def sweep(matrix, panel, width):
    lane = lax.broadcasted_iota(jnp.int32, (ROWS, width), 1)
    thin = lax.broadcasted_iota(jnp.int32, (1, width), 1)

    def one_panel(step, carry):
        base = pl.multiple_of(step * PIVOTS, PIVOTS)
        rows = [matrix[pl.ds(base + t, ROWS, stride=width), :] for t in range(PIVOTS)]
        old = [matrix[pl.ds(b * width + base, PIVOTS), :] for b in range(ROWS)]
        new = pivot_rows(rows, base, lane)
        for t in range(PIVOTS):
            panel[pl.ds(t, ROWS, stride=PIVOTS), :] = new[t]
        inside = (thin >= base) & (thin < base + PIVOTS)
        mine = [panel[b * PIVOTS : (b + 1) * PIVOTS, :] for b in range(ROWS)]
        for b in range(ROWS):
            a1, a2, a3 = three_parts(old[b])
            b1, b2, b3 = three_parts(mine[b])
            left = jnp.concatenate([a1, a1, a2, a2, a1, a3], 0).astype(BF16)
            right = jnp.concatenate([b1, b2, b1, b2, b3, b1], 0).astype(BF16)
            change = lax.dot_general(
                left, right, (((0,), (0,)), ((), ())), preferred_element_type=F32
            )
            whole = slice(b * width, (b + 1) * width)
            matrix[whole, :] = jnp.where(inside, 0.0, matrix[whole, :]) - change
        for b in range(ROWS):
            matrix[pl.ds(b * width + base, PIVOTS), :] = mine[b]
        return carry

    lax.fori_loop(0, width // PIVOTS, one_panel, 0)


def minus_product(matrix, vector, width):
    total = [jnp.zeros(vector.shape, F32) for _ in range(4)]
    for k in range(width):
        factor = jnp.broadcast_to(vector[:, k : k + 1], vector.shape)
        total[k % 4] = total[k % 4] - factor * matrix[pl.ds(k, ROWS, stride=width), :]
    return (total[0] + total[1]) + (total[2] + total[3])


def newton_kernel(shifts, sides, capacity, group, plane, *refs):
    planes = len(shifts)
    messages, (back, release, mean, prior, out, left, gram, panel) = refs[:planes], refs[planes:]
    chunks, _, pixels = messages[0].shape
    owners = back.shape[0] // planes
    bins, releases = release.shape
    share = bins // planes
    pair = 2 * share
    top = share * releases
    gram[...] = jnp.zeros(gram.shape, F32)

    def one_chunk(prints, e, chunk):
        targets = prints[chunk, group * releases :, :].astype(F32)
        values = []
        for o in range(owners):
            block = back[o * planes + e].astype(F32)
            values.extend(block[r * pair : (r + 1) * pair] for r in range(capacity))
        for j in range(group):
            picked = jnp.zeros((pair, pixels), F32)
            for s, value in enumerate(values):
                picked = jnp.where(targets[j : j + 1] == float(s), value, picked)
            columns = slice(j * pixels, (j + 1) * pixels)
            block = prints[chunk, j * releases : (j + 1) * releases, :]
            for b in range(share):
                weight = jnp.broadcast_to(picked[share + b : share + b + 1], (2 * ROWS, pixels))
                weight = weight.astype(BF16)
                for r in range(0, releases, 2 * ROWS):
                    rows = slice(b * releases + r, b * releases + r + 2 * ROWS)
                    left[rows, columns] = block[r : r + 2 * ROWS] * weight
            if pair < 2 * ROWS:
                picked = jnp.concatenate([picked, jnp.zeros((2 * ROWS - pair, pixels), F32)], 0)
            left[top:, columns] = picked.astype(BF16)
        right = jnp.concatenate(
            [prints[chunk, j * releases : (j + 1) * releases, :] for j in range(group)], 1
        )
        gram[: top + 2 * ROWS, :] += lax.dot_general(
            left[...], right, (((1,), (1,)), ((), ())), preferred_element_type=F32
        )

    along, across = lax.div(plane[0], sides[1]), lax.rem(plane[0], sides[1])
    for prints, (far, near) in zip(messages, shifts):
        e = lax.rem(along + far, sides[0]) * sides[1] + lax.rem(across + near, sides[1])
        pl.loop(0, chunks, unroll=chunks == 1)(functools.partial(one_chunk, prints, e))

    def own(array):
        rows = array[...]
        mine = rows[:share]
        for e in range(1, planes):
            mine = jnp.where(plane[0] == e, rows[e * share : (e + 1) * share], mine)
        if share < ROWS:
            mine = jnp.concatenate([mine, jnp.zeros((ROWS - share, releases), F32)], 0)
        return mine

    log_release, prior_mean, prior_weight = own(release), own(mean), own(prior)
    unslope = 1.0 + jnp.exp(-log_release)
    gradient = gram[top : top + ROWS, :]
    right_side = gradient - prior_weight * (log_release - prior_mean) * unslope
    diagonal = prior_weight * unslope * unslope
    row = lax.broadcasted_iota(jnp.int32, (releases, releases), 0)
    column = lax.broadcasted_iota(jnp.int32, (releases, releases), 1)
    for b in range(ROWS):
        block = slice(b * releases, (b + 1) * releases)
        if b < share:
            matrix = gram[block, :]
            matrix = 0.5 * (matrix + matrix.T)
            gram[block, :] = matrix + jnp.where(row == column, diagonal[b : b + 1], 0.0)
        else:
            gram[block, :] = jnp.where(row == column, 1.0, 0.0)
    sweep(gram, panel, releases)
    update = log_release + unslope * minus_product(gram, right_side, releases)
    out[...] = update[:share]


def shifted(array, axis, distance):
    if not distance:
        return array
    size = lax.axis_size(axis)
    return lax.ppermute(array, axis, [((i + distance) % size, i) for i in range(size)])


def params():
    return pltpu.CompilerParams(vmem_limit_bytes=LIMIT)


def body(
    footprint, block_tile, log_release, prior_mean, prior_weight, observed, noise_weight, pixel_mask
):
    blocks, releases, pixels = footprint.shape
    owners = lax.axis_size("rel")
    planes = lax.axis_size(("bin", "rep"))
    tiles, bins, _ = observed.shape
    capacity = blocks * 4 // 3 // owners
    slots = owners * capacity
    share = bins // planes
    group = math.gcd(blocks, 6)
    chunks = blocks // group
    scalars = pl.BlockSpec(memory_space=pltpu.SMEM)
    local = pl.BlockSpec(memory_space=pltpu.VMEM)

    sent, message = pl.pallas_call(
        functools.partial(emission_kernel, tiles, capacity, group),
        out_shape=(
            jax.ShapeDtypeStruct((slots, bins + ROWS, pixels), F32),
            jax.ShapeDtypeStruct((chunks, group * releases + 2 * ROWS, pixels), BF16),
        ),
        in_specs=[scalars, local, local],
        out_specs=(local, local),
        compiler_params=params(),
    )(block_tile, log_release.T, footprint)
    arrived = lax.all_to_all(sent, "rel", split_axis=0, concat_axis=0, tiled=True)
    sides = (lax.axis_size("bin"), lax.axis_size("rep"))
    shifts, messages = [], []
    for far in range(sides[0]):
        moved = shifted(message, "bin", far)
        for near in range(sides[1]):
            shifts.append((far, near))
            messages.append(shifted(moved, "rep", near))

    residual, back = pl.pallas_call(
        functools.partial(residual_kernel, planes, capacity),
        out_shape=(
            jax.ShapeDtypeStruct(observed.shape, F32),
            jax.ShapeDtypeStruct((owners * planes, capacity * 2 * share, pixels), BF16),
        ),
        in_specs=[local] * 4,
        out_specs=(local, local),
        scratch_shapes=[pltpu.VMEM(observed.shape, F32)],
        compiler_params=params(),
    )(arrived, observed, noise_weight, pixel_mask)
    back = lax.all_to_all(back, ("rel", "bin", "rep"), split_axis=0, concat_axis=0, tiled=True)

    plane = lax.axis_index(("bin", "rep")).astype(jnp.int32).reshape(1)
    height = share * releases + 2 * ROWS
    release_new = pl.pallas_call(
        functools.partial(newton_kernel, shifts, sides, capacity, group),
        out_shape=jax.ShapeDtypeStruct((share, releases), F32),
        in_specs=[scalars] + [local] * (planes + 4),
        out_specs=local,
        scratch_shapes=[
            pltpu.VMEM((height, group * pixels), BF16),
            pltpu.VMEM((max(height, ROWS * releases), releases), F32),
            pltpu.VMEM((ROWS * PIVOTS, releases), F32),
        ],
        compiler_params=params(),
    )(plane, *messages, back, log_release.T, prior_mean.T, prior_weight.T)
    return (release_new.T, residual)


def solution(mesh):
    in_specs = (
        P(("groups", "rel", "bin", "rep"), None, None),
        P(("groups", "rel", "bin", "rep")),
        P(("groups", "rel"), None),
        P(("groups", "rel"), None),
        P(("groups", "rel"), None),
        P(("groups", "rel", "bin", "rep"), None, None),
        P(("groups", "rel", "bin", "rep"), None, None),
        P(("groups", "rel", "bin", "rep"), None),
    )
    out_specs = (
        P(("groups", "rel"), ("bin", "rep")),
        P(("groups", "rel", "bin", "rep"), None, None),
    )
    return jax.shard_map(body, mesh=mesh, in_specs=in_specs, out_specs=out_specs, check_vma=False)
```

```python
import functools
import math

import jax
import jax.numpy as jnp
from jax import lax
from jax.experimental import pallas as pl
from jax.experimental.pallas import tpu as pltpu
from jax.sharding import PartitionSpec as P

PIVOTS = 8
ROWS = 8
LIMIT = 48 << 20
F32 = jnp.float32
BF16 = jnp.bfloat16


def emission_kernel(
    tiles, capacity, blocks, tile_source, release_source, print_source, sent, message,
    tile_of, release, tile_ready, release_ready, print_ready,
):
    chunks, length, pixels = print_source.shape
    group = blocks // chunks
    releases = length // group
    slots, padded, _ = sent.shape
    bins = padded - ROWS
    copies = [
        pltpu.make_async_copy(
            print_source.at[c], message.at[c, pl.ds(0, length)], print_ready.at[c]
        )
        for c in range(chunks)
    ]
    tile_copy = pltpu.make_async_copy(tile_source, tile_of, tile_ready)
    release_copy = pltpu.make_async_copy(release_source, release, release_ready)
    tile_copy.start()
    release_copy.start()
    for copy in copies:
        copy.start()
    sent[...] = jnp.full(sent.shape, -1.0, F32)
    release_copy.wait()
    value = release[...]
    rates = (jnp.maximum(value, 0.0) + jnp.log1p(jnp.exp(-jnp.abs(value)))).astype(BF16)
    tile_copy.wait()
    owner, rank = None, None
    for c in range(chunks):
        copies[c].wait()
        rows = []
        for j in range(group):
            k = c * group + j
            mine = lax.div(tile_of[k], tiles)
            rank = jnp.where(mine == owner, rank + 1, 0) if k else 0
            owner = mine
            target = owner * capacity + rank
            emission = lax.dot_general(
                rates,
                message[c, j * releases : (j + 1) * releases, :],
                (((1,), (0,)), ((), ())),
                preferred_element_type=F32,
            )
            local = lax.rem(tile_of[k], tiles).astype(F32)
            sent[target, :bins, :] = emission
            sent[target, bins:, :] = jnp.full((ROWS, pixels), local, F32)
            rows.append(jnp.full((1, pixels), target.astype(F32), F32))
        rows.append(jnp.full((2 * ROWS - group, pixels), -1.0, F32))
        message[c, length:, :] = jnp.concatenate(rows, 0).astype(BF16)


def residual_kernel(planes, capacity, arrived, observed, noise, mask, residual, back, weights):
    slots, padded, pixels = arrived.shape
    tiles, bins, _ = observed.shape
    share = bins // planes
    owners = slots // capacity

    def one_tile(t):
        def add(s, running):
            match = arrived[s, bins : bins + 1, :] == t.astype(F32)
            return running + jnp.where(match, arrived[s, :bins, :], 0.0)

        predicted = lax.fori_loop(0, slots, add, jnp.zeros((bins, pixels), F32), unroll=slots <= 8)
        weight = mask[pl.ds(t, 1), :].astype(F32) * noise[t]
        weights[t] = weight
        residual[t] = weight * (observed[t] - predicted)

    pl.loop(0, tiles, unroll=True)(one_tile)

    def one_owner(c):
        pieces = []
        for rank in range(capacity):
            s = c * capacity + rank
            place = arrived[s, bins : bins + 1, :]
            misfit = jnp.zeros((bins, pixels), F32)
            weight = jnp.zeros((bins, pixels), F32)
            for t in range(tiles):
                match = place == float(t)
                misfit = jnp.where(match, residual[t], misfit)
                weight = jnp.where(match, weights[t], weight)
            pieces.append((misfit, weight))
        for e in range(planes):
            rows = slice(e * share, (e + 1) * share)
            parts = [part[rows] for pair in pieces for part in pair]
            back[c * planes + e] = jnp.concatenate(parts, 0).astype(BF16)

    pl.loop(0, owners, unroll=owners <= 4)(one_owner)


def three_parts(values):
    high = values.astype(BF16).astype(F32)
    rest = values - high
    middle = rest.astype(BF16).astype(F32)
    return high, middle, rest - middle


def pivot_rows(rows, base, lane):
    width = lane.shape[1]
    inside = (lane >= base) & (lane < base + PIVOTS)
    out = [
        jnp.where(inside, jnp.where(lane == base + t, 1.0, 0.0), rows[t]) for t in range(PIVOTS)
    ]
    turned = [pltpu.roll(row, width - base, 1) for row in rows]
    block = [
        [jnp.broadcast_to(row[:, u : u + 1], lane.shape) for u in range(PIVOTS)] for row in turned
    ]
    for j in range(PIVOTS):
        inverse = 1.0 / block[j][j]
        out[j] = out[j] * inverse
        for u in range(j + 1, PIVOTS):
            block[j][u] = block[j][u] * inverse
        for i in range(PIVOTS):
            if i != j:
                factor = block[i][j]
                out[i] = out[i] - factor * out[j]
                for u in range(j + 1, PIVOTS):
                    block[i][u] = block[i][u] - factor * block[j][u]
    return [jnp.where(inside, -row, row) for row in out]


def sweep(matrix, panel, width):
    lane = lax.broadcasted_iota(jnp.int32, (ROWS, width), 1)
    thin = lax.broadcasted_iota(jnp.int32, (1, width), 1)

    def one_panel(step, carry):
        base = pl.multiple_of(step * PIVOTS, PIVOTS)
        rows = [matrix[pl.ds(base + t, ROWS, stride=width), :] for t in range(PIVOTS)]
        old = [matrix[pl.ds(b * width + base, PIVOTS), :] for b in range(ROWS)]
        new = pivot_rows(rows, base, lane)
        for t in range(PIVOTS):
            panel[pl.ds(t, ROWS, stride=PIVOTS), :] = new[t]
        inside = (thin >= base) & (thin < base + PIVOTS)
        mine = [panel[b * PIVOTS : (b + 1) * PIVOTS, :] for b in range(ROWS)]
        for b in range(ROWS):
            a1, a2, a3 = three_parts(old[b])
            b1, b2, b3 = three_parts(mine[b])
            left = jnp.concatenate([a1, a1, a2, a2, a1, a3], 0).astype(BF16)
            right = jnp.concatenate([b1, b2, b1, b2, b3, b1], 0).astype(BF16)
            change = lax.dot_general(
                left, right, (((0,), (0,)), ((), ())), preferred_element_type=F32
            )
            whole = slice(b * width, (b + 1) * width)
            matrix[whole, :] = jnp.where(inside, 0.0, matrix[whole, :]) - change
        for b in range(ROWS):
            matrix[pl.ds(b * width + base, PIVOTS), :] = mine[b]
        return carry

    lax.fori_loop(0, width // PIVOTS, one_panel, 0)


def minus_product(matrix, vector, width):
    total = [jnp.zeros(vector.shape, F32) for _ in range(4)]
    for k in range(width):
        factor = jnp.broadcast_to(vector[:, k : k + 1], vector.shape)
        total[k % 4] = total[k % 4] - factor * matrix[pl.ds(k, ROWS, stride=width), :]
    return (total[0] + total[1]) + (total[2] + total[3])


def newton_kernel(shifts, sides, capacity, group, plane, *refs):
    planes = len(shifts)
    messages, (back, release, mean, prior, out, left, gram, panel) = refs[:planes], refs[planes:]
    chunks, _, pixels = messages[0].shape
    owners = back.shape[0] // planes
    bins, releases = release.shape
    share = bins // planes
    pair = 2 * share
    top = share * releases
    gram[...] = jnp.zeros(gram.shape, F32)

    def one_chunk(prints, e, chunk):
        targets = prints[chunk, group * releases :, :].astype(F32)
        values = []
        for o in range(owners):
            block = back[o * planes + e].astype(F32)
            values.extend(block[r * pair : (r + 1) * pair] for r in range(capacity))
        for j in range(group):
            picked = jnp.zeros((pair, pixels), F32)
            for s, value in enumerate(values):
                picked = jnp.where(targets[j : j + 1] == float(s), value, picked)
            columns = slice(j * pixels, (j + 1) * pixels)
            block = prints[chunk, j * releases : (j + 1) * releases, :]
            for b in range(share):
                weight = jnp.broadcast_to(picked[share + b : share + b + 1], (2 * ROWS, pixels))
                weight = weight.astype(BF16)
                for r in range(0, releases, 2 * ROWS):
                    rows = slice(b * releases + r, b * releases + r + 2 * ROWS)
                    left[rows, columns] = block[r : r + 2 * ROWS] * weight
            if pair < 2 * ROWS:
                picked = jnp.concatenate([picked, jnp.zeros((2 * ROWS - pair, pixels), F32)], 0)
            left[top:, columns] = picked.astype(BF16)
        right = jnp.concatenate(
            [prints[chunk, j * releases : (j + 1) * releases, :] for j in range(group)], 1
        )
        gram[: top + 2 * ROWS, :] += lax.dot_general(
            left[...], right, (((1,), (1,)), ((), ())), preferred_element_type=F32
        )

    along, across = lax.div(plane[0], sides[1]), lax.rem(plane[0], sides[1])
    for prints, (far, near) in zip(messages, shifts):
        e = lax.rem(along + far, sides[0]) * sides[1] + lax.rem(across + near, sides[1])
        pl.loop(0, chunks, unroll=chunks == 1)(functools.partial(one_chunk, prints, e))

    def own(array):
        rows = array[...]
        mine = rows[:share]
        for e in range(1, planes):
            mine = jnp.where(plane[0] == e, rows[e * share : (e + 1) * share], mine)
        if share < ROWS:
            mine = jnp.concatenate([mine, jnp.zeros((ROWS - share, releases), F32)], 0)
        return mine

    log_release, prior_mean, prior_weight = own(release), own(mean), own(prior)
    unslope = 1.0 + jnp.exp(-log_release)
    gradient = gram[top : top + ROWS, :]
    right_side = gradient - prior_weight * (log_release - prior_mean) * unslope
    diagonal = prior_weight * unslope * unslope
    row = lax.broadcasted_iota(jnp.int32, (releases, releases), 0)
    column = lax.broadcasted_iota(jnp.int32, (releases, releases), 1)
    for b in range(ROWS):
        block = slice(b * releases, (b + 1) * releases)
        if b < share:
            matrix = gram[block, :]
            matrix = 0.5 * (matrix + matrix.T)
            gram[block, :] = matrix + jnp.where(row == column, diagonal[b : b + 1], 0.0)
        else:
            gram[block, :] = jnp.where(row == column, 1.0, 0.0)
    sweep(gram, panel, releases)
    update = log_release + unslope * minus_product(gram, right_side, releases)
    out[...] = update[:share]


def shifted(array, axis, distance):
    if not distance:
        return array
    size = lax.axis_size(axis)
    return lax.ppermute(array, axis, [((i + distance) % size, i) for i in range(size)])


def params():
    return pltpu.CompilerParams(vmem_limit_bytes=LIMIT)


def body(
    footprint, block_tile, log_release, prior_mean, prior_weight, observed, noise_weight, pixel_mask
):
    blocks, releases, pixels = footprint.shape
    owners = lax.axis_size("rel")
    planes = lax.axis_size(("bin", "rep"))
    tiles, bins, _ = observed.shape
    capacity = blocks * 4 // 3 // owners
    slots = owners * capacity
    share = bins // planes
    group = math.gcd(blocks, 6)
    chunks = blocks // group
    scalars = pl.BlockSpec(memory_space=pltpu.SMEM)
    local = pl.BlockSpec(memory_space=pltpu.VMEM)
    remote = pl.BlockSpec(memory_space=pltpu.HBM)
    release, mean, prior = log_release.T, prior_mean.T, prior_weight.T

    sent, message = pl.pallas_call(
        functools.partial(emission_kernel, tiles, capacity, blocks),
        out_shape=(
            jax.ShapeDtypeStruct((slots, bins + ROWS, pixels), F32),
            jax.ShapeDtypeStruct((chunks, group * releases + 2 * ROWS, pixels), BF16),
        ),
        in_specs=[remote] * 3,
        out_specs=(local, local),
        scratch_shapes=[
            pltpu.SMEM(block_tile.shape, jnp.int32),
            pltpu.VMEM(release.shape, F32),
            pltpu.SemaphoreType.DMA,
            pltpu.SemaphoreType.DMA,
            pltpu.SemaphoreType.DMA((chunks,)),
        ],
    )(block_tile, release, footprint.reshape(chunks, group * releases, pixels))
    arrived = lax.all_to_all(sent, "rel", split_axis=0, concat_axis=0, tiled=True)
    sides = (lax.axis_size("bin"), lax.axis_size("rep"))
    shifts, messages = [], []
    for far in range(sides[0]):
        moved = shifted(message, "bin", far)
        for near in range(sides[1]):
            shifts.append((far, near))
            messages.append(shifted(moved, "rep", near))

    residual, back = pl.pallas_call(
        functools.partial(residual_kernel, planes, capacity),
        out_shape=(
            jax.ShapeDtypeStruct(observed.shape, F32),
            jax.ShapeDtypeStruct((owners * planes, capacity * 2 * share, pixels), BF16),
        ),
        in_specs=[local] * 4,
        out_specs=(local, local),
        scratch_shapes=[pltpu.VMEM(observed.shape, F32)],
        compiler_params=params(),
    )(arrived, observed, noise_weight, pixel_mask)
    back = lax.all_to_all(back, ("rel", "bin", "rep"), split_axis=0, concat_axis=0, tiled=True)

    plane = lax.axis_index(("bin", "rep")).astype(jnp.int32).reshape(1)
    height = share * releases + 2 * ROWS
    release_new = pl.pallas_call(
        functools.partial(newton_kernel, shifts, sides, capacity, group),
        out_shape=jax.ShapeDtypeStruct((share, releases), F32),
        in_specs=[scalars] + [local] * (planes + 4),
        out_specs=local,
        scratch_shapes=[
            pltpu.VMEM((height, group * pixels), BF16),
            pltpu.VMEM((max(height, ROWS * releases), releases), F32),
            pltpu.VMEM((ROWS * PIVOTS, releases), F32),
        ],
        compiler_params=params(),
    )(plane, *messages, back, release, mean, prior)
    return (release_new.T, residual)


def solution(mesh):
    in_specs = (
        P(("groups", "rel", "bin", "rep"), None, None),
        P(("groups", "rel", "bin", "rep")),
        P(("groups", "rel"), None),
        P(("groups", "rel"), None),
        P(("groups", "rel"), None),
        P(("groups", "rel", "bin", "rep"), None, None),
        P(("groups", "rel", "bin", "rep"), None, None),
        P(("groups", "rel", "bin", "rep"), None),
    )
    out_specs = (
        P(("groups", "rel"), ("bin", "rep")),
        P(("groups", "rel", "bin", "rep"), None, None),
    )
    return jax.shard_map(body, mesh=mesh, in_specs=in_specs, out_specs=out_specs, check_vma=False)
```

```python
import functools
import math

import jax
import jax.numpy as jnp
from jax import lax
from jax.experimental import pallas as pl
from jax.experimental.pallas import tpu as pltpu
from jax.sharding import PartitionSpec as P

PIVOTS = 8
ROWS = 8
TOGETHER = 2
LIMIT = 48 << 20
F32 = jnp.float32
BF16 = jnp.bfloat16


def emission_kernel(
    tiles, capacity, blocks, tile_source, release_source, print_source, sent, message,
    tile_of, release, tile_ready, release_ready, print_ready,
):
    chunks, length, pixels = print_source.shape
    group = blocks // chunks
    releases = length // group
    slots, padded, _ = sent.shape
    bins = padded - ROWS
    copies = [
        pltpu.make_async_copy(
            print_source.at[c], message.at[c, pl.ds(0, length)], print_ready.at[c]
        )
        for c in range(chunks)
    ]
    tile_copy = pltpu.make_async_copy(tile_source, tile_of, tile_ready)
    release_copy = pltpu.make_async_copy(release_source, release, release_ready)
    tile_copy.start()
    release_copy.start()
    for copy in copies:
        copy.start()
    sent[...] = jnp.full(sent.shape, -1.0, F32)
    release_copy.wait()
    value = release[...]
    rates = (jnp.maximum(value, 0.0) + jnp.log1p(jnp.exp(-jnp.abs(value)))).astype(BF16)
    tile_copy.wait()
    owner, rank = None, None
    for c in range(chunks):
        copies[c].wait()
        rows = []
        for j in range(group):
            k = c * group + j
            mine = lax.div(tile_of[k], tiles)
            rank = jnp.where(mine == owner, rank + 1, 0) if k else 0
            owner = mine
            target = owner * capacity + rank
            emission = lax.dot_general(
                rates,
                message[c, j * releases : (j + 1) * releases, :],
                (((1,), (0,)), ((), ())),
                preferred_element_type=F32,
            )
            local = lax.rem(tile_of[k], tiles).astype(F32)
            sent[target, :bins, :] = emission
            sent[target, bins:, :] = jnp.full((ROWS, pixels), local, F32)
            rows.append(jnp.full((1, pixels), target.astype(F32), F32))
        rows.append(jnp.full((2 * ROWS - group, pixels), -1.0, F32))
        message[c, length:, :] = jnp.concatenate(rows, 0).astype(BF16)


def residual_kernel(planes, capacity, arrived, observed, noise, mask, residual, back, weights):
    slots, padded, pixels = arrived.shape
    tiles, bins, _ = observed.shape
    share = bins // planes
    owners = slots // capacity

    def one_tile(t):
        def add(s, running):
            match = arrived[s, bins : bins + 1, :] == t.astype(F32)
            return running + jnp.where(match, arrived[s, :bins, :], 0.0)

        predicted = lax.fori_loop(0, slots, add, jnp.zeros((bins, pixels), F32), unroll=slots <= 8)
        weight = mask[pl.ds(t, 1), :].astype(F32) * noise[t]
        weights[t] = weight
        residual[t] = weight * (observed[t] - predicted)

    pl.loop(0, tiles, unroll=True)(one_tile)

    def one_owner(c):
        pieces = []
        for rank in range(capacity):
            s = c * capacity + rank
            place = arrived[s, bins : bins + 1, :]
            misfit = jnp.zeros((bins, pixels), F32)
            weight = jnp.zeros((bins, pixels), F32)
            for t in range(tiles):
                match = place == float(t)
                misfit = jnp.where(match, residual[t], misfit)
                weight = jnp.where(match, weights[t], weight)
            pieces.append((misfit, weight))
        for e in range(planes):
            rows = slice(e * share, (e + 1) * share)
            parts = [part[rows] for pair in pieces for part in pair]
            back[c * planes + e] = jnp.concatenate(parts, 0).astype(BF16)

    pl.loop(0, owners, unroll=owners <= 4)(one_owner)


def three_parts(values):
    high = values.astype(BF16).astype(F32)
    rest = values - high
    middle = rest.astype(BF16).astype(F32)
    return high, middle, rest - middle


def spread(row, base, count):
    turned = pltpu.roll(row, row.shape[1] - base, 1)
    return [jnp.broadcast_to(turned[:, u : u + 1], row.shape) for u in range(count)]


def minus_products(start, factors, rows):
    terms = [factor * row for factor, row in zip(factors, rows)]
    while len(terms) > 1:
        terms = [sum(terms[i : i + 2]) for i in range(0, len(terms), 2)]
    return start - terms[0]


def pivot_rows(rows, base, lane):
    inside = (lane >= base) & (lane < base + PIVOTS)
    out = [
        jnp.where(inside, jnp.where(lane == base + t, 1.0, 0.0), rows[t]) for t in range(PIVOTS)
    ]
    turned = [pltpu.roll(row, lane.shape[1] - base, 1) for row in rows]
    block = [[None] * PIVOTS for _ in range(PIVOTS)]
    for u in range(PIVOTS):
        for t in range(u + 1):
            block[t][u] = jnp.broadcast_to(turned[t][:, u : u + 1], lane.shape)
    for j in range(PIVOTS):
        inverse = 1.0 / block[j][j]
        raw = list(block[j])
        out[j] = out[j] * inverse
        for u in range(j + 1, PIVOTS):
            block[j][u] = raw[u] * inverse
        for i in range(j + 1, PIVOTS):
            for u in range(i, PIVOTS):
                block[i][u] = block[i][u] - raw[i] * block[j][u]
            out[i] = out[i] - raw[i] * out[j]
    for j in range(PIVOTS - 1, 0, -1):
        for i in range(j):
            out[i] = out[i] - block[i][j] * out[j]
    return [jnp.where(inside, -row, row) for row in out]


def eliminate(matrix, ahead, panel, right_side):
    width = matrix.shape[1]
    steps = width // PIVOTS
    lane = lax.broadcasted_iota(jnp.int32, (ROWS, width), 1)
    thin = lax.broadcasted_iota(jnp.int32, (1, width), 1)
    def load(base):
        return [matrix[pl.ds(base + t, ROWS, stride=width), :] for t in range(PIVOTS)]

    def look_ahead(rows, base):
        turned = [pltpu.roll(row, width - base, 1) for row in rows]
        for t in range(PIVOTS):
            for u in range(PIVOTS):
                ahead[t * PIVOTS + u] = jnp.broadcast_to(turned[u][:, t : t + 1], lane.shape)

    def apply(vector, base, new):
        inside = (lane >= base) & (lane < base + PIVOTS)
        return minus_products(jnp.where(inside, 0.0, vector), spread(vector, base, PIVOTS), new)

    def one_panel(first, step, carry):
        new, vector = list(carry[:-1]), carry[-1]
        base = pl.multiple_of(step * PIVOTS, PIVOTS)
        following = pl.multiple_of(base + PIVOTS, PIVOTS)
        inside = (lane >= base) & (lane < base + PIVOTS)
        rows = [
            minus_products(
                jnp.where(inside, 0.0, row), [ahead[t * PIVOTS + u] for u in range(PIVOTS)], new
            )
            for t, row in enumerate(load(following))
        ]
        for t in range(PIVOTS):
            panel[pl.ds(t, ROWS, stride=PIVOTS), :] = new[t]
        old = [matrix[pl.ds(b * width + base, PIVOTS), :] for b in range(ROWS)]
        mine = [panel[b * PIVOTS : (b + 1) * PIVOTS, :] for b in range(ROWS)]
        within = (thin >= base) & (thin < base + PIVOTS)
        for group in range(0, ROWS, TOGETHER):
            left, right = [], []
            for b in range(TOGETHER):
                a1, a2, a3 = three_parts(old[group + b])
                b1, b2, b3 = three_parts(mine[group + b])
                left.extend([a1, a1, a2, a2, a1, a3])
                parts = jnp.concatenate([b1, b2, b1, b2, b3, b1], 0).astype(BF16)
                blank = jnp.zeros_like(parts)
                right.append(
                    jnp.concatenate([parts if i == b else blank for i in range(TOGETHER)], 1)
                )
            turned = jnp.concatenate(left, 0).astype(BF16).T[first:]
            change = jnp.dot(turned, jnp.concatenate(right, 0), preferred_element_type=F32)
            for b in range(TOGETHER):
                rest = slice((group + b) * width + first, (group + b + 1) * width)
                matrix[rest, :] = (
                    jnp.where(within, 0.0, matrix[rest, :]) - change[:, b * width : (b + 1) * width]
                )
        newer = pivot_rows(rows, following, lane)
        look_ahead(rows, following + PIVOTS)
        return (*newer, apply(vector, base, new))

    rows = load(0)
    carry = (*pivot_rows(rows, 0, lane), right_side)
    look_ahead(rows, PIVOTS)
    phases = 4 if steps % 4 == 0 else 1
    length = steps // phases
    for phase in range(phases):
        low, high = max(phase * length - 1, 0), (phase + 1) * length - 1
        step = functools.partial(one_panel, phase * length * PIVOTS)
        carry = lax.fori_loop(low, high, step, carry)
    return apply(carry[-1], width - PIVOTS, list(carry[:-1]))


def newton_kernel(shifts, sides, capacity, group, plane, *refs):
    planes = len(shifts)
    messages, (back, release, mean, prior, out, left, gram, ahead, panel) = refs[:planes], refs[planes:]
    chunks, _, pixels = messages[0].shape
    owners = back.shape[0] // planes
    bins, releases = release.shape
    share = bins // planes
    pair = 2 * share
    top = share * releases
    gram[...] = jnp.zeros(gram.shape, F32)

    def one_chunk(prints, e, chunk):
        targets = prints[chunk, group * releases :, :].astype(F32)
        values = []
        for o in range(owners):
            block = back[o * planes + e].astype(F32)
            values.extend(block[r * pair : (r + 1) * pair] for r in range(capacity))
        for j in range(group):
            picked = jnp.zeros((pair, pixels), F32)
            for s, value in enumerate(values):
                picked = jnp.where(targets[j : j + 1] == float(s), value, picked)
            columns = slice(j * pixels, (j + 1) * pixels)
            block = prints[chunk, j * releases : (j + 1) * releases, :]
            for b in range(share):
                weight = jnp.broadcast_to(picked[share + b : share + b + 1], (2 * ROWS, pixels))
                weight = weight.astype(BF16)
                for r in range(0, releases, 2 * ROWS):
                    rows = slice(b * releases + r, b * releases + r + 2 * ROWS)
                    left[rows, columns] = block[r : r + 2 * ROWS] * weight
            if pair < 2 * ROWS:
                picked = jnp.concatenate([picked, jnp.zeros((2 * ROWS - pair, pixels), F32)], 0)
            left[top:, columns] = picked.astype(BF16)
        right = jnp.concatenate(
            [prints[chunk, j * releases : (j + 1) * releases, :] for j in range(group)], 1
        )
        gram[: top + 2 * ROWS, :] += lax.dot_general(
            left[...], right, (((1,), (1,)), ((), ())), preferred_element_type=F32
        )

    along, across = lax.div(plane[0], sides[1]), lax.rem(plane[0], sides[1])
    for prints, (far, near) in zip(messages, shifts):
        e = lax.rem(along + far, sides[0]) * sides[1] + lax.rem(across + near, sides[1])
        pl.loop(0, chunks, unroll=chunks == 1)(functools.partial(one_chunk, prints, e))

    def own(array):
        rows = array[...]
        mine = rows[:share]
        for e in range(1, planes):
            mine = jnp.where(plane[0] == e, rows[e * share : (e + 1) * share], mine)
        if share < ROWS:
            mine = jnp.concatenate([mine, jnp.zeros((ROWS - share, releases), F32)], 0)
        return mine

    log_release, prior_mean, prior_weight = own(release), own(mean), own(prior)
    unslope = 1.0 + jnp.exp(-log_release)
    gradient = gram[top : top + ROWS, :]
    right_side = gradient - prior_weight * (log_release - prior_mean) * unslope
    diagonal = prior_weight * unslope * unslope
    row = lax.broadcasted_iota(jnp.int32, (releases, releases), 0)
    column = lax.broadcasted_iota(jnp.int32, (releases, releases), 1)
    for b in range(ROWS):
        block = slice(b * releases, (b + 1) * releases)
        if b < share:
            matrix = gram[block, :]
            matrix = 0.5 * (matrix + matrix.T)
            gram[block, :] = matrix + jnp.where(row == column, diagonal[b : b + 1], 0.0)
        else:
            gram[block, :] = jnp.where(row == column, 1.0, 0.0)
    systems = gram.at[pl.ds(0, ROWS * releases)]
    update = log_release + unslope * eliminate(systems, ahead, panel, right_side)
    out[...] = update[:share]


def newton_scratch(share, group, releases, pixels):
    height = share * releases + 2 * ROWS
    return [
        pltpu.VMEM((height, group * pixels), BF16),
        pltpu.VMEM((max(height, ROWS * releases), releases), F32),
        pltpu.VMEM((PIVOTS * PIVOTS, ROWS, releases), F32),
        pltpu.VMEM((ROWS * PIVOTS, releases), F32),
    ]


def shifted(array, axis, distance):
    if not distance:
        return array
    size = lax.axis_size(axis)
    return lax.ppermute(array, axis, [((i + distance) % size, i) for i in range(size)])


def params():
    return pltpu.CompilerParams(vmem_limit_bytes=LIMIT)


def body(
    footprint, block_tile, log_release, prior_mean, prior_weight, observed, noise_weight, pixel_mask
):
    blocks, releases, pixels = footprint.shape
    owners = lax.axis_size("rel")
    planes = lax.axis_size(("bin", "rep"))
    tiles, bins, _ = observed.shape
    capacity = blocks * 4 // 3 // owners
    slots = owners * capacity
    share = bins // planes
    group = math.gcd(blocks, 6)
    chunks = blocks // group
    scalars = pl.BlockSpec(memory_space=pltpu.SMEM)
    local = pl.BlockSpec(memory_space=pltpu.VMEM)
    remote = pl.BlockSpec(memory_space=pltpu.HBM)
    release, mean, prior = log_release.T, prior_mean.T, prior_weight.T

    sent, message = pl.pallas_call(
        functools.partial(emission_kernel, tiles, capacity, blocks),
        out_shape=(
            jax.ShapeDtypeStruct((slots, bins + ROWS, pixels), F32),
            jax.ShapeDtypeStruct((chunks, group * releases + 2 * ROWS, pixels), BF16),
        ),
        in_specs=[remote] * 3,
        out_specs=(local, local),
        scratch_shapes=[
            pltpu.SMEM(block_tile.shape, jnp.int32),
            pltpu.VMEM(release.shape, F32),
            pltpu.SemaphoreType.DMA,
            pltpu.SemaphoreType.DMA,
            pltpu.SemaphoreType.DMA((chunks,)),
        ],
    )(block_tile, release, footprint.reshape(chunks, group * releases, pixels))
    arrived = lax.all_to_all(sent, "rel", split_axis=0, concat_axis=0, tiled=True)
    sides = (lax.axis_size("bin"), lax.axis_size("rep"))
    shifts, messages = [], []
    for far in range(sides[0]):
        moved = shifted(message, "bin", far)
        for near in range(sides[1]):
            shifts.append((far, near))
            messages.append(shifted(moved, "rep", near))

    residual, back = pl.pallas_call(
        functools.partial(residual_kernel, planes, capacity),
        out_shape=(
            jax.ShapeDtypeStruct(observed.shape, F32),
            jax.ShapeDtypeStruct((owners * planes, capacity * 2 * share, pixels), BF16),
        ),
        in_specs=[local] * 4,
        out_specs=(local, local),
        scratch_shapes=[pltpu.VMEM(observed.shape, F32)],
        compiler_params=params(),
    )(arrived, observed, noise_weight, pixel_mask)
    back = lax.all_to_all(back, ("rel", "bin", "rep"), split_axis=0, concat_axis=0, tiled=True)

    plane = lax.axis_index(("bin", "rep")).astype(jnp.int32).reshape(1)
    release_new = pl.pallas_call(
        functools.partial(newton_kernel, shifts, sides, capacity, group),
        out_shape=jax.ShapeDtypeStruct((share, releases), F32),
        in_specs=[scalars] + [local] * (planes + 4),
        out_specs=local,
        scratch_shapes=newton_scratch(share, group, releases, pixels),
        compiler_params=params(),
    )(plane, *messages, back, release, mean, prior)
    return (release_new.T, residual)


def solution(mesh):
    in_specs = (
        P(("groups", "rel", "bin", "rep"), None, None),
        P(("groups", "rel", "bin", "rep")),
        P(("groups", "rel"), None),
        P(("groups", "rel"), None),
        P(("groups", "rel"), None),
        P(("groups", "rel", "bin", "rep"), None, None),
        P(("groups", "rel", "bin", "rep"), None, None),
        P(("groups", "rel", "bin", "rep"), None),
    )
    out_specs = (
        P(("groups", "rel"), ("bin", "rep")),
        P(("groups", "rel", "bin", "rep"), None, None),
    )
    return jax.shard_map(body, mesh=mesh, in_specs=in_specs, out_specs=out_specs, check_vma=False)
```

```python
import functools
import math

import jax
import jax.numpy as jnp
from jax import lax
from jax.experimental import pallas as pl
from jax.experimental.pallas import tpu as pltpu
from jax.sharding import PartitionSpec as P

PIVOTS = 8
ROWS = 8
TOGETHER = 2
LIMIT = 48 << 20
F32 = jnp.float32
BF16 = jnp.bfloat16


def emission_kernel(
    tiles, capacity, blocks, tile_source, release_source, print_source, sent, message,
    tile_of, release, tile_ready, release_ready, print_ready,
):
    chunks, length, pixels = print_source.shape
    group = blocks // chunks
    releases = length // group
    slots, padded, _ = sent.shape
    bins = padded - ROWS
    copies = [
        pltpu.make_async_copy(
            print_source.at[c], message.at[c, pl.ds(0, length)], print_ready.at[c]
        )
        for c in range(chunks)
    ]
    tile_copy = pltpu.make_async_copy(tile_source, tile_of, tile_ready)
    release_copy = pltpu.make_async_copy(release_source, release, release_ready)
    tile_copy.start()
    release_copy.start()
    for copy in copies:
        copy.start()
    sent[...] = jnp.full(sent.shape, -1.0, F32)
    release_copy.wait()
    value = release[...]
    rates = (jnp.maximum(value, 0.0) + jnp.log1p(jnp.exp(-jnp.abs(value)))).astype(BF16)
    tile_copy.wait()
    owner, rank = None, None
    for c in range(chunks):
        copies[c].wait()
        rows = []
        for j in range(group):
            k = c * group + j
            mine = lax.div(tile_of[k], tiles)
            rank = jnp.where(mine == owner, rank + 1, 0) if k else 0
            owner = mine
            target = owner * capacity + rank
            emission = lax.dot_general(
                rates,
                message[c, j * releases : (j + 1) * releases, :],
                (((1,), (0,)), ((), ())),
                preferred_element_type=F32,
            )
            local = lax.rem(tile_of[k], tiles).astype(F32)
            sent[target, :bins, :] = emission
            sent[target, bins:, :] = jnp.full((ROWS, pixels), local, F32)
            rows.append(jnp.full((1, pixels), target.astype(F32), F32))
        rows.append(jnp.full((2 * ROWS - group, pixels), -1.0, F32))
        message[c, length:, :] = jnp.concatenate(rows, 0).astype(BF16)


def residual_kernel(planes, capacity, arrived, observed, noise, mask, residual, back, weights):
    slots, padded, pixels = arrived.shape
    tiles, bins, _ = observed.shape
    share = bins // planes
    owners = slots // capacity

    def one_tile(t):
        def add(s, running):
            match = arrived[s, bins : bins + 1, :] == t.astype(F32)
            return running + jnp.where(match, arrived[s, :bins, :], 0.0)

        predicted = lax.fori_loop(0, slots, add, jnp.zeros((bins, pixels), F32), unroll=slots <= 8)
        weight = mask[pl.ds(t, 1), :].astype(F32) * noise[t]
        weights[t] = weight
        residual[t] = weight * (observed[t] - predicted)

    pl.loop(0, tiles, unroll=True)(one_tile)

    def one_owner(c):
        pieces = []
        for rank in range(capacity):
            s = c * capacity + rank
            place = arrived[s, bins : bins + 1, :]
            misfit = jnp.zeros((bins, pixels), F32)
            weight = jnp.zeros((bins, pixels), F32)
            for t in range(tiles):
                match = place == float(t)
                misfit = jnp.where(match, residual[t], misfit)
                weight = jnp.where(match, weights[t], weight)
            pieces.append((misfit, weight))
        for e in range(planes):
            rows = slice(e * share, (e + 1) * share)
            parts = [part[rows] for pair in pieces for part in pair]
            back[c * planes + e] = jnp.concatenate(parts, 0).astype(BF16)

    pl.loop(0, owners, unroll=owners <= 4)(one_owner)


def three_parts(values):
    high = values.astype(BF16).astype(F32)
    rest = values - high
    middle = rest.astype(BF16).astype(F32)
    return high, middle, rest - middle


def spread(row, base, count):
    turned = pltpu.roll(row, row.shape[1] - base, 1)
    return [jnp.broadcast_to(turned[:, u : u + 1], row.shape) for u in range(count)]


def minus_products(start, factors, rows):
    terms = [factor * row for factor, row in zip(factors, rows)]
    while len(terms) > 1:
        terms = [sum(terms[i : i + 2]) for i in range(0, len(terms), 2)]
    return start - terms[0]


def pivot_rows(rows, base, lane):
    inside = (lane >= base) & (lane < base + PIVOTS)
    out = [
        jnp.where(inside, jnp.where(lane == base + t, 1.0, 0.0), rows[t]) for t in range(PIVOTS)
    ]
    turned = [pltpu.roll(row, lane.shape[1] - base, 1) for row in rows]
    block = [[None] * PIVOTS for _ in range(PIVOTS)]
    for u in range(PIVOTS):
        for t in range(u + 1):
            block[t][u] = jnp.broadcast_to(turned[t][:, u : u + 1], lane.shape)
    for j in range(PIVOTS):
        inverse = 1.0 / block[j][j]
        raw = list(block[j])
        out[j] = out[j] * inverse
        for u in range(j + 1, PIVOTS):
            block[j][u] = raw[u] * inverse
        for i in range(j + 1, PIVOTS):
            for u in range(i, PIVOTS):
                block[i][u] = block[i][u] - raw[i] * block[j][u]
            out[i] = out[i] - raw[i] * out[j]
    for j in range(PIVOTS - 1, 0, -1):
        for i in range(j):
            out[i] = out[i] - block[i][j] * out[j]
    return [jnp.where(inside, -row, row) for row in out]


def eliminate(matrix, ahead, panel, right_side):
    width = matrix.shape[1]
    steps = width // PIVOTS
    lane = lax.broadcasted_iota(jnp.int32, (ROWS, width), 1)
    thin = lax.broadcasted_iota(jnp.int32, (1, width), 1)
    def load(base):
        return [matrix[pl.ds(base + t, ROWS, stride=width), :] for t in range(PIVOTS)]

    def look_ahead(rows, base):
        turned = [pltpu.roll(row, width - base, 1) for row in rows]
        for t in range(PIVOTS):
            for u in range(PIVOTS):
                ahead[t * PIVOTS + u] = jnp.broadcast_to(turned[u][:, t : t + 1], lane.shape)

    def apply(vector, base, new):
        inside = (lane >= base) & (lane < base + PIVOTS)
        return minus_products(jnp.where(inside, 0.0, vector), spread(vector, base, PIVOTS), new)

    def one_panel(first, step, carry):
        new, vector = list(carry[:-1]), carry[-1]
        base = pl.multiple_of(step * PIVOTS, PIVOTS)
        following = pl.multiple_of(base + PIVOTS, PIVOTS)
        inside = (lane >= base) & (lane < base + PIVOTS)
        rows = [
            minus_products(
                jnp.where(inside, 0.0, row), [ahead[t * PIVOTS + u] for u in range(PIVOTS)], new
            )
            for t, row in enumerate(load(following))
        ]
        for t in range(PIVOTS):
            panel[pl.ds(t, ROWS, stride=PIVOTS), :] = new[t]
        old = [matrix[pl.ds(b * width + base, PIVOTS), :] for b in range(ROWS)]
        mine = [panel[b * PIVOTS : (b + 1) * PIVOTS, :] for b in range(ROWS)]
        within = (thin >= base) & (thin < base + PIVOTS)
        for group in range(0, ROWS, TOGETHER):
            left, right = [], []
            for b in range(TOGETHER):
                a1, a2, a3 = three_parts(old[group + b])
                b1, b2, b3 = three_parts(mine[group + b])
                left.extend([a1, a1, a2, a2, a1, a3])
                parts = jnp.concatenate([b1, b2, b1, b2, b3, b1], 0).astype(BF16)
                blank = jnp.zeros_like(parts)
                right.append(
                    jnp.concatenate([parts if i == b else blank for i in range(TOGETHER)], 1)
                )
            turned = jnp.concatenate(left, 0).astype(BF16).T[first:]
            change = jnp.dot(turned, jnp.concatenate(right, 0), preferred_element_type=F32)
            for b in range(TOGETHER):
                rest = slice((group + b) * width + first, (group + b + 1) * width)
                matrix[rest, :] = (
                    jnp.where(within, 0.0, matrix[rest, :]) - change[:, b * width : (b + 1) * width]
                )
        newer = pivot_rows(rows, following, lane)
        look_ahead(rows, following + PIVOTS)
        return (*newer, apply(vector, base, new))

    rows = load(0)
    carry = (*pivot_rows(rows, 0, lane), right_side)
    look_ahead(rows, PIVOTS)
    phases = 4 if steps % 4 == 0 else 1
    length = steps // phases
    for phase in range(phases):
        low, high = max(phase * length - 1, 0), (phase + 1) * length - 1
        step = functools.partial(one_panel, phase * length * PIVOTS)
        carry = lax.fori_loop(low, high, step, carry)
    return apply(carry[-1], width - PIVOTS, list(carry[:-1]))


def newton_kernel(shifts, sides, capacity, group, plane, *refs):
    planes = len(shifts)
    messages, (back, release, mean, prior, out, halves, gram, ahead, panel) = refs[:planes], refs[planes:]
    chunks, _, pixels = messages[0].shape
    owners = back.shape[0] // planes
    bins, releases = release.shape
    share = bins // planes
    pair = 2 * share
    top = share * releases
    if chunks > 1:
        gram[...] = jnp.zeros(gram.shape, F32)

    def one_chunk(prints, e, i, chunk):
        left = halves.at[i % 2]
        targets = prints[chunk, group * releases :, :].astype(F32)
        values = []
        for o in range(owners):
            block = back[o * planes + e].astype(F32)
            values.extend(block[r * pair : (r + 1) * pair] for r in range(capacity))
        for j in range(group):
            picked = jnp.zeros((pair, pixels), F32)
            for s, value in enumerate(values):
                picked = jnp.where(targets[j : j + 1] == float(s), value, picked)
            columns = slice(j * pixels, (j + 1) * pixels)
            block = prints[chunk, j * releases : (j + 1) * releases, :]
            for b in range(share):
                weight = jnp.broadcast_to(picked[share + b : share + b + 1], (2 * ROWS, pixels))
                weight = weight.astype(BF16)
                for r in range(0, releases, 2 * ROWS):
                    rows = slice(b * releases + r, b * releases + r + 2 * ROWS)
                    left[rows, columns] = block[r : r + 2 * ROWS] * weight
            if pair < 2 * ROWS:
                picked = jnp.concatenate([picked, jnp.zeros((2 * ROWS - pair, pixels), F32)], 0)
            left[top:, columns] = picked.astype(BF16)
        right = jnp.concatenate(
            [prints[chunk, j * releases : (j + 1) * releases, :] for j in range(group)], 1
        )
        product = lax.dot_general(
            left[...], right, (((1,), (1,)), ((), ())), preferred_element_type=F32
        )
        if i or chunks > 1:
            product += gram[: top + 2 * ROWS, :]
        gram[: top + 2 * ROWS, :] = product

    along, across = lax.div(plane[0], sides[1]), lax.rem(plane[0], sides[1])
    for i, (prints, (far, near)) in enumerate(zip(messages, shifts)):
        e = lax.rem(along + far, sides[0]) * sides[1] + lax.rem(across + near, sides[1])
        pl.loop(0, chunks, unroll=chunks == 1)(functools.partial(one_chunk, prints, e, i))

    def own(array):
        rows = array[...]
        mine = rows[:share]
        for e in range(1, planes):
            mine = jnp.where(plane[0] == e, rows[e * share : (e + 1) * share], mine)
        if share < ROWS:
            mine = jnp.concatenate([mine, jnp.zeros((ROWS - share, releases), F32)], 0)
        return mine

    log_release, prior_mean, prior_weight = own(release), own(mean), own(prior)
    unslope = 1.0 + jnp.exp(-log_release)
    gradient = gram[top : top + ROWS, :]
    right_side = gradient - prior_weight * (log_release - prior_mean) * unslope
    diagonal = prior_weight * unslope * unslope
    row = lax.broadcasted_iota(jnp.int32, (releases, releases), 0)
    column = lax.broadcasted_iota(jnp.int32, (releases, releases), 1)
    for b in range(ROWS):
        block = slice(b * releases, (b + 1) * releases)
        if b < share:
            matrix = gram[block, :]
            matrix = 0.5 * (matrix + matrix.T)
            gram[block, :] = matrix + jnp.where(row == column, diagonal[b : b + 1], 0.0)
        else:
            gram[block, :] = jnp.where(row == column, 1.0, 0.0)
    systems = gram.at[pl.ds(0, ROWS * releases)]
    update = log_release + unslope * eliminate(systems, ahead, panel, right_side)
    out[...] = update[:share]


def newton_scratch(share, group, releases, pixels):
    height = share * releases + 2 * ROWS
    return [
        pltpu.VMEM((2, height, group * pixels), BF16),
        pltpu.VMEM((max(height, ROWS * releases), releases), F32),
        pltpu.VMEM((PIVOTS * PIVOTS, ROWS, releases), F32),
        pltpu.VMEM((ROWS * PIVOTS, releases), F32),
    ]


def shifted(array, axis, distance):
    if not distance:
        return array
    size = lax.axis_size(axis)
    return lax.ppermute(array, axis, [((i + distance) % size, i) for i in range(size)])


def params():
    return pltpu.CompilerParams(vmem_limit_bytes=LIMIT)


def body(
    footprint, block_tile, log_release, prior_mean, prior_weight, observed, noise_weight, pixel_mask
):
    blocks, releases, pixels = footprint.shape
    owners = lax.axis_size("rel")
    planes = lax.axis_size(("bin", "rep"))
    tiles, bins, _ = observed.shape
    capacity = blocks * 4 // 3 // owners
    slots = owners * capacity
    share = bins // planes
    group = math.gcd(blocks, 6)
    chunks = blocks // group
    scalars = pl.BlockSpec(memory_space=pltpu.SMEM)
    local = pl.BlockSpec(memory_space=pltpu.VMEM)
    remote = pl.BlockSpec(memory_space=pltpu.HBM)
    release, mean, prior = log_release.T, prior_mean.T, prior_weight.T

    sent, message = pl.pallas_call(
        functools.partial(emission_kernel, tiles, capacity, blocks),
        out_shape=(
            jax.ShapeDtypeStruct((slots, bins + ROWS, pixels), F32),
            jax.ShapeDtypeStruct((chunks, group * releases + 2 * ROWS, pixels), BF16),
        ),
        in_specs=[remote] * 3,
        out_specs=(local, local),
        scratch_shapes=[
            pltpu.SMEM(block_tile.shape, jnp.int32),
            pltpu.VMEM(release.shape, F32),
            pltpu.SemaphoreType.DMA,
            pltpu.SemaphoreType.DMA,
            pltpu.SemaphoreType.DMA((chunks,)),
        ],
    )(block_tile, release, footprint.reshape(chunks, group * releases, pixels))
    arrived = lax.all_to_all(sent, "rel", split_axis=0, concat_axis=0, tiled=True)
    sides = (lax.axis_size("bin"), lax.axis_size("rep"))
    shifts, messages = [], []
    for far in range(sides[0]):
        moved = shifted(message, "bin", far)
        for near in range(sides[1]):
            shifts.append((far, near))
            messages.append(shifted(moved, "rep", near))
    arrived, *messages = lax.optimization_barrier((arrived, *messages))

    residual, back = pl.pallas_call(
        functools.partial(residual_kernel, planes, capacity),
        out_shape=(
            jax.ShapeDtypeStruct(observed.shape, F32),
            jax.ShapeDtypeStruct((owners * planes, capacity * 2 * share, pixels), BF16),
        ),
        in_specs=[local] * 4,
        out_specs=(local, local),
        scratch_shapes=[pltpu.VMEM(observed.shape, F32)],
        compiler_params=params(),
    )(arrived, observed, noise_weight, pixel_mask)
    back = lax.all_to_all(back, ("rel", "bin", "rep"), split_axis=0, concat_axis=0, tiled=True)

    plane = lax.axis_index(("bin", "rep")).astype(jnp.int32).reshape(1)
    release_new = pl.pallas_call(
        functools.partial(newton_kernel, shifts, sides, capacity, group),
        out_shape=jax.ShapeDtypeStruct((share, releases), F32),
        in_specs=[scalars] + [local] * (planes + 4),
        out_specs=local,
        scratch_shapes=newton_scratch(share, group, releases, pixels),
        compiler_params=params(),
    )(plane, *messages, back, release, mean, prior)
    return (release_new.T, residual)


def solution(mesh):
    in_specs = (
        P(("groups", "rel", "bin", "rep"), None, None),
        P(("groups", "rel", "bin", "rep")),
        P(("groups", "rel"), None),
        P(("groups", "rel"), None),
        P(("groups", "rel"), None),
        P(("groups", "rel", "bin", "rep"), None, None),
        P(("groups", "rel", "bin", "rep"), None, None),
        P(("groups", "rel", "bin", "rep"), None),
    )
    out_specs = (
        P(("groups", "rel"), ("bin", "rep")),
        P(("groups", "rel", "bin", "rep"), None, None),
    )
    return jax.shard_map(body, mesh=mesh, in_specs=in_specs, out_specs=out_specs, check_vma=False)
```

```python
import functools
import math

import jax
import jax.numpy as jnp
from jax import lax
from jax.experimental import pallas as pl
from jax.experimental.pallas import tpu as pltpu
from jax.sharding import PartitionSpec as P

PIVOTS = 8
ROWS = 8
TOGETHER = 2
LIMIT = 48 << 20
F32 = jnp.float32
BF16 = jnp.bfloat16


def emission_kernel(
    tiles, capacity, blocks, tile_source, release_source, print_source, message, *refs
):
    owners = len(refs) - 6
    pieces, (sent, tile_of, release, tile_ready, release_ready, print_ready) = (
        refs[:owners],
        refs[owners:],
    )
    here = lax.axis_index("rel")
    chunks, length, pixels = print_source.shape
    group = blocks // chunks
    releases = length // group
    slots, padded, _ = sent.shape
    bins = padded - ROWS
    copies = [
        pltpu.make_async_copy(
            print_source.at[c], message.at[c, pl.ds(0, length)], print_ready.at[c]
        )
        for c in range(chunks)
    ]
    tile_copy = pltpu.make_async_copy(tile_source, tile_of, tile_ready)
    release_copy = pltpu.make_async_copy(release_source, release, release_ready)
    tile_copy.start()
    release_copy.start()
    for copy in copies:
        copy.start()
    sent[...] = jnp.full(sent.shape, -1.0, F32)
    release_copy.wait()
    value = release[...]
    rates = (jnp.maximum(value, 0.0) + jnp.log1p(jnp.exp(-jnp.abs(value)))).astype(BF16)
    tile_copy.wait()
    owner, rank = None, None
    for c in range(chunks):
        copies[c].wait()
        rows = []
        for j in range(group):
            k = c * group + j
            mine = lax.div(tile_of[k], tiles)
            rank = jnp.where(mine == owner, rank + 1, 0) if k else 0
            owner = mine
            target = owner * capacity + rank
            emission = lax.dot_general(
                rates,
                message[c, j * releases : (j + 1) * releases, :],
                (((1,), (0,)), ((), ())),
                preferred_element_type=F32,
            )
            local = lax.rem(tile_of[k], tiles).astype(F32)
            place = lax.rem(owner + (owners - here), owners) * capacity + rank
            sent[place, :bins, :] = emission
            sent[place, bins:, :] = jnp.full((ROWS, pixels), local, F32)
            rows.append(jnp.full((1, pixels), target.astype(F32), F32))
        rows.append(jnp.full((2 * ROWS - group, pixels), -1.0, F32))
        message[c, length:, :] = jnp.concatenate(rows, 0).astype(BF16)
    for d, piece in enumerate(pieces):
        piece[...] = sent[d * capacity : (d + 1) * capacity]


def residual_kernel(planes, owners, observed, noise, mask, *refs):
    arrived, (residual, back, weights) = refs[:owners], refs[owners:]
    capacity, padded, pixels = arrived[0].shape
    tiles, bins, _ = observed.shape
    share = bins // planes
    here = lax.axis_index("rel")

    def one_tile(t):
        predicted = jnp.zeros((bins, pixels), F32)
        for piece in arrived:
            for rank in range(capacity):
                match = piece[rank, bins : bins + 1, :] == t.astype(F32)
                predicted = predicted + jnp.where(match, piece[rank, :bins, :], 0.0)
        weight = mask[pl.ds(t, 1), :].astype(F32) * noise[t]
        weights[t] = weight
        residual[t] = weight * (observed[t] - predicted)

    pl.loop(0, tiles, unroll=True)(one_tile)

    for d, piece in enumerate(arrived):
        source = lax.rem(here + (owners - d), owners)
        pieces = []
        for rank in range(capacity):
            place = piece[rank, bins : bins + 1, :]
            misfit = jnp.zeros((bins, pixels), F32)
            weight = jnp.zeros((bins, pixels), F32)
            for t in range(tiles):
                match = place == float(t)
                misfit = jnp.where(match, residual[t], misfit)
                weight = jnp.where(match, weights[t], weight)
            pieces.append((misfit, weight))
        for e in range(planes):
            rows = slice(e * share, (e + 1) * share)
            parts = [part[rows] for pair in pieces for part in pair]
            back[source * planes + e] = jnp.concatenate(parts, 0).astype(BF16)


def three_parts(values):
    high = values.astype(BF16).astype(F32)
    rest = values - high
    middle = rest.astype(BF16).astype(F32)
    return high, middle, rest - middle


def spread(row, base, count):
    turned = pltpu.roll(row, row.shape[1] - base, 1)
    return [jnp.broadcast_to(turned[:, u : u + 1], row.shape) for u in range(count)]


def minus_products(start, factors, rows):
    terms = [factor * row for factor, row in zip(factors, rows)]
    while len(terms) > 1:
        terms = [sum(terms[i : i + 2]) for i in range(0, len(terms), 2)]
    return start - terms[0]


def pivot_rows(rows, base, lane):
    inside = (lane >= base) & (lane < base + PIVOTS)
    out = [
        jnp.where(inside, jnp.where(lane == base + t, 1.0, 0.0), rows[t]) for t in range(PIVOTS)
    ]
    turned = [pltpu.roll(row, lane.shape[1] - base, 1) for row in rows]
    block = [[None] * PIVOTS for _ in range(PIVOTS)]
    for u in range(PIVOTS):
        for t in range(u + 1):
            block[t][u] = jnp.broadcast_to(turned[t][:, u : u + 1], lane.shape)
    for j in range(PIVOTS):
        inverse = 1.0 / block[j][j]
        raw = list(block[j])
        out[j] = out[j] * inverse
        for u in range(j + 1, PIVOTS):
            block[j][u] = raw[u] * inverse
        for i in range(j + 1, PIVOTS):
            for u in range(i, PIVOTS):
                block[i][u] = block[i][u] - raw[i] * block[j][u]
            out[i] = out[i] - raw[i] * out[j]
    for j in range(PIVOTS - 1, 0, -1):
        for i in range(j):
            out[i] = out[i] - block[i][j] * out[j]
    return [jnp.where(inside, -row, row) for row in out]


def eliminate(matrix, ahead, panel, right_side):
    width = matrix.shape[1]
    steps = width // PIVOTS
    lane = lax.broadcasted_iota(jnp.int32, (ROWS, width), 1)
    thin = lax.broadcasted_iota(jnp.int32, (1, width), 1)
    def load(base):
        return [matrix[pl.ds(base + t, ROWS, stride=width), :] for t in range(PIVOTS)]

    def look_ahead(rows, base):
        turned = [pltpu.roll(row, width - base, 1) for row in rows]
        for t in range(PIVOTS):
            for u in range(PIVOTS):
                ahead[t * PIVOTS + u] = jnp.broadcast_to(turned[u][:, t : t + 1], lane.shape)

    def apply(vector, base, new):
        inside = (lane >= base) & (lane < base + PIVOTS)
        return minus_products(jnp.where(inside, 0.0, vector), spread(vector, base, PIVOTS), new)

    def one_panel(first, step, carry):
        new, vector = list(carry[:-1]), carry[-1]
        base = pl.multiple_of(step * PIVOTS, PIVOTS)
        following = pl.multiple_of(base + PIVOTS, PIVOTS)
        inside = (lane >= base) & (lane < base + PIVOTS)
        rows = [
            minus_products(
                jnp.where(inside, 0.0, row), [ahead[t * PIVOTS + u] for u in range(PIVOTS)], new
            )
            for t, row in enumerate(load(following))
        ]
        for t in range(PIVOTS):
            panel[pl.ds(t, ROWS, stride=PIVOTS), :] = new[t]
        old = [matrix[pl.ds(b * width + base, PIVOTS), :] for b in range(ROWS)]
        mine = [panel[b * PIVOTS : (b + 1) * PIVOTS, :] for b in range(ROWS)]
        within = (thin >= base) & (thin < base + PIVOTS)
        for group in range(0, ROWS, TOGETHER):
            left, right = [], []
            for b in range(TOGETHER):
                a1, a2, a3 = three_parts(old[group + b])
                b1, b2, b3 = three_parts(mine[group + b])
                left.extend([a1, a1, a2, a2, a1, a3])
                parts = jnp.concatenate([b1, b2, b1, b2, b3, b1], 0).astype(BF16)
                blank = jnp.zeros_like(parts)
                right.append(
                    jnp.concatenate([parts if i == b else blank for i in range(TOGETHER)], 1)
                )
            turned = jnp.concatenate(left, 0).astype(BF16).T[first:]
            change = jnp.dot(turned, jnp.concatenate(right, 0), preferred_element_type=F32)
            for b in range(TOGETHER):
                rest = slice((group + b) * width + first, (group + b + 1) * width)
                matrix[rest, :] = (
                    jnp.where(within, 0.0, matrix[rest, :]) - change[:, b * width : (b + 1) * width]
                )
        newer = pivot_rows(rows, following, lane)
        look_ahead(rows, following + PIVOTS)
        return (*newer, apply(vector, base, new))

    rows = load(0)
    carry = (*pivot_rows(rows, 0, lane), right_side)
    look_ahead(rows, PIVOTS)
    phases = 4 if steps % 4 == 0 else 1
    length = steps // phases
    for phase in range(phases):
        low, high = max(phase * length - 1, 0), (phase + 1) * length - 1
        step = functools.partial(one_panel, phase * length * PIVOTS)
        carry = lax.fori_loop(low, high, step, carry)
    return apply(carry[-1], width - PIVOTS, list(carry[:-1]))


def newton_kernel(shifts, sides, capacity, group, plane, *refs):
    planes = len(shifts)
    messages, (back, release, mean, prior, out, halves, gram, ahead, panel) = refs[:planes], refs[planes:]
    chunks, _, pixels = messages[0].shape
    owners = back.shape[0] // planes
    bins, releases = release.shape
    share = bins // planes
    pair = 2 * share
    top = share * releases
    if chunks > 1:
        gram[...] = jnp.zeros(gram.shape, F32)

    def one_chunk(prints, e, i, chunk):
        left = halves.at[i % 2]
        targets = prints[chunk, group * releases :, :].astype(F32)
        values = []
        for o in range(owners):
            block = back[o * planes + e].astype(F32)
            values.extend(block[r * pair : (r + 1) * pair] for r in range(capacity))
        for j in range(group):
            picked = jnp.zeros((pair, pixels), F32)
            for s, value in enumerate(values):
                picked = jnp.where(targets[j : j + 1] == float(s), value, picked)
            columns = slice(j * pixels, (j + 1) * pixels)
            block = prints[chunk, j * releases : (j + 1) * releases, :]
            for b in range(share):
                weight = jnp.broadcast_to(picked[share + b : share + b + 1], (2 * ROWS, pixels))
                weight = weight.astype(BF16)
                for r in range(0, releases, 2 * ROWS):
                    rows = slice(b * releases + r, b * releases + r + 2 * ROWS)
                    left[rows, columns] = block[r : r + 2 * ROWS] * weight
            if pair < 2 * ROWS:
                picked = jnp.concatenate([picked, jnp.zeros((2 * ROWS - pair, pixels), F32)], 0)
            left[top:, columns] = picked.astype(BF16)
        right = jnp.concatenate(
            [prints[chunk, j * releases : (j + 1) * releases, :] for j in range(group)], 1
        )
        product = lax.dot_general(
            left[...], right, (((1,), (1,)), ((), ())), preferred_element_type=F32
        )
        if i or chunks > 1:
            product += gram[: top + 2 * ROWS, :]
        gram[: top + 2 * ROWS, :] = product

    along, across = lax.div(plane[0], sides[1]), lax.rem(plane[0], sides[1])
    for i, (prints, (far, near)) in enumerate(zip(messages, shifts)):
        e = lax.rem(along + far, sides[0]) * sides[1] + lax.rem(across + near, sides[1])
        pl.loop(0, chunks, unroll=chunks == 1)(functools.partial(one_chunk, prints, e, i))

    def own(array):
        rows = array[...]
        mine = rows[:share]
        for e in range(1, planes):
            mine = jnp.where(plane[0] == e, rows[e * share : (e + 1) * share], mine)
        if share < ROWS:
            mine = jnp.concatenate([mine, jnp.zeros((ROWS - share, releases), F32)], 0)
        return mine

    log_release, prior_mean, prior_weight = own(release), own(mean), own(prior)
    unslope = 1.0 + jnp.exp(-log_release)
    gradient = gram[top : top + ROWS, :]
    right_side = gradient - prior_weight * (log_release - prior_mean) * unslope
    diagonal = prior_weight * unslope * unslope
    row = lax.broadcasted_iota(jnp.int32, (releases, releases), 0)
    column = lax.broadcasted_iota(jnp.int32, (releases, releases), 1)
    for b in range(ROWS):
        block = slice(b * releases, (b + 1) * releases)
        if b < share:
            matrix = gram[block, :]
            matrix = 0.5 * (matrix + matrix.T)
            gram[block, :] = matrix + jnp.where(row == column, diagonal[b : b + 1], 0.0)
        else:
            gram[block, :] = jnp.where(row == column, 1.0, 0.0)
    systems = gram.at[pl.ds(0, ROWS * releases)]
    update = log_release + unslope * eliminate(systems, ahead, panel, right_side)
    out[...] = update[:share]


def newton_scratch(share, group, releases, pixels):
    height = share * releases + 2 * ROWS
    return [
        pltpu.VMEM((2, height, group * pixels), BF16),
        pltpu.VMEM((max(height, ROWS * releases), releases), F32),
        pltpu.VMEM((PIVOTS * PIVOTS, ROWS, releases), F32),
        pltpu.VMEM((ROWS * PIVOTS, releases), F32),
    ]


def shifted(array, axis, distance):
    if not distance:
        return array
    size = lax.axis_size(axis)
    return lax.ppermute(array, axis, [((i + distance) % size, i) for i in range(size)])


def params():
    return pltpu.CompilerParams(vmem_limit_bytes=LIMIT)


def body(
    footprint, block_tile, log_release, prior_mean, prior_weight, observed, noise_weight, pixel_mask
):
    blocks, releases, pixels = footprint.shape
    owners = lax.axis_size("rel")
    planes = lax.axis_size(("bin", "rep"))
    tiles, bins, _ = observed.shape
    capacity = blocks * 4 // 3 // owners
    slots = owners * capacity
    share = bins // planes
    group = math.gcd(blocks, 6)
    chunks = blocks // group
    scalars = pl.BlockSpec(memory_space=pltpu.SMEM)
    local = pl.BlockSpec(memory_space=pltpu.VMEM)
    remote = pl.BlockSpec(memory_space=pltpu.HBM)
    release, mean, prior = log_release.T, prior_mean.T, prior_weight.T

    message, *sent = pl.pallas_call(
        functools.partial(emission_kernel, tiles, capacity, blocks),
        out_shape=(
            jax.ShapeDtypeStruct((chunks, group * releases + 2 * ROWS, pixels), BF16),
            *[jax.ShapeDtypeStruct((capacity, bins + ROWS, pixels), F32)] * owners,
        ),
        in_specs=[remote] * 3,
        out_specs=(local,) * (1 + owners),
        scratch_shapes=[
            pltpu.VMEM((slots, bins + ROWS, pixels), F32),
            pltpu.SMEM(block_tile.shape, jnp.int32),
            pltpu.VMEM(release.shape, F32),
            pltpu.SemaphoreType.DMA,
            pltpu.SemaphoreType.DMA,
            pltpu.SemaphoreType.DMA((chunks,)),
        ],
    )(block_tile, release, footprint.reshape(chunks, group * releases, pixels))
    arrived = [shifted(piece, "rel", owners - d if d else 0) for d, piece in enumerate(sent)]
    sides = (lax.axis_size("bin"), lax.axis_size("rep"))
    shifts, messages = [], []
    for far in range(sides[0]):
        moved = shifted(message, "bin", far)
        for near in range(sides[1]):
            shifts.append((far, near))
            messages.append(shifted(moved, "rep", near))

    residual, back = pl.pallas_call(
        functools.partial(residual_kernel, planes, owners),
        out_shape=(
            jax.ShapeDtypeStruct(observed.shape, F32),
            jax.ShapeDtypeStruct((owners * planes, capacity * 2 * share, pixels), BF16),
        ),
        in_specs=[local] * (3 + owners),
        out_specs=(local, local),
        scratch_shapes=[pltpu.VMEM(observed.shape, F32)],
        compiler_params=params(),
    )(observed, noise_weight, pixel_mask, *arrived)
    back = lax.all_to_all(back, ("rel", "bin", "rep"), split_axis=0, concat_axis=0, tiled=True)

    plane = lax.axis_index(("bin", "rep")).astype(jnp.int32).reshape(1)
    release_new = pl.pallas_call(
        functools.partial(newton_kernel, shifts, sides, capacity, group),
        out_shape=jax.ShapeDtypeStruct((share, releases), F32),
        in_specs=[scalars] + [local] * (planes + 4),
        out_specs=local,
        scratch_shapes=newton_scratch(share, group, releases, pixels),
        compiler_params=params(),
    )(plane, *messages, back, release, mean, prior)
    return (release_new.T, residual)


def solution(mesh):
    in_specs = (
        P(("groups", "rel", "bin", "rep"), None, None),
        P(("groups", "rel", "bin", "rep")),
        P(("groups", "rel"), None),
        P(("groups", "rel"), None),
        P(("groups", "rel"), None),
        P(("groups", "rel", "bin", "rep"), None, None),
        P(("groups", "rel", "bin", "rep"), None, None),
        P(("groups", "rel", "bin", "rep"), None),
    )
    out_specs = (
        P(("groups", "rel"), ("bin", "rep")),
        P(("groups", "rel", "bin", "rep"), None, None),
    )
    return jax.shard_map(body, mesh=mesh, in_specs=in_specs, out_specs=out_specs, check_vma=False)
```

```python
import functools
import math

import jax
import jax.numpy as jnp
from jax import lax
from jax.experimental import pallas as pl
from jax.experimental.pallas import tpu as pltpu
from jax.sharding import PartitionSpec as P

PIVOTS = 8
ROWS = 8
TOGETHER = 2
LIMIT = 48 << 20
F32 = jnp.float32
BF16 = jnp.bfloat16


def emission_kernel(
    tiles, capacity, blocks, tile_source, release_source, print_source, message, *refs
):
    owners = len(refs) - 6
    pieces, (sent, tile_of, release, tile_ready, release_ready, print_ready) = (
        refs[:owners],
        refs[owners:],
    )
    here = lax.axis_index("rel")
    chunks, length, pixels = print_source.shape
    group = blocks // chunks
    releases = length // group
    slots, padded, _ = sent.shape
    bins = padded - ROWS
    copies = [
        pltpu.make_async_copy(
            print_source.at[c], message.at[c, pl.ds(0, length)], print_ready.at[c]
        )
        for c in range(chunks)
    ]
    tile_copy = pltpu.make_async_copy(tile_source, tile_of, tile_ready)
    release_copy = pltpu.make_async_copy(release_source, release, release_ready)
    tile_copy.start()
    release_copy.start()
    for copy in copies:
        copy.start()
    sent[...] = jnp.full(sent.shape, -1.0, F32)
    release_copy.wait()
    value = release[...]
    rates = (jnp.maximum(value, 0.0) + jnp.log1p(jnp.exp(-jnp.abs(value)))).astype(BF16)
    tile_copy.wait()
    owner, rank = None, None
    for c in range(chunks):
        copies[c].wait()
        rows = []
        for j in range(group):
            k = c * group + j
            mine = lax.div(tile_of[k], tiles)
            rank = jnp.where(mine == owner, rank + 1, 0) if k else 0
            owner = mine
            target = owner * capacity + rank
            emission = lax.dot_general(
                rates,
                message[c, j * releases : (j + 1) * releases, :],
                (((1,), (0,)), ((), ())),
                preferred_element_type=F32,
            )
            local = lax.rem(tile_of[k], tiles).astype(F32)
            place = lax.rem(owner + (owners - here), owners) * capacity + rank
            sent[place, :bins, :] = emission
            sent[place, bins:, :] = jnp.full((ROWS, pixels), local, F32)
            rows.append(jnp.full((1, pixels), target.astype(F32), F32))
        rows.append(jnp.full((2 * ROWS - group, pixels), -1.0, F32))
        message[c, length:, :] = jnp.concatenate(rows, 0).astype(BF16)
    for d, piece in enumerate(pieces):
        piece[...] = sent[d * capacity : (d + 1) * capacity]


def add_emissions(start, piece, bins, tile):
    for rank in range(piece.shape[0]):
        match = piece[rank, bins : bins + 1, :] == float(tile)
        start = start - jnp.where(match, piece[rank, :bins, :], 0.0)
    return start


def prepare_kernel(observed, noise, mask, own, remaining, weights):
    tiles, bins, _ = observed.shape
    for t in range(tiles):
        weights[t] = mask[t : t + 1, :].astype(F32) * noise[t]
        remaining[t] = add_emissions(observed[t], own, bins, t)


def residual_kernel(planes, owners, remaining, weights, *refs):
    arrived, (residual, back) = refs[:owners], refs[owners:]
    capacity, padded, pixels = arrived[0].shape
    tiles, bins, _ = remaining.shape
    share = bins // planes
    here = lax.axis_index("rel")

    for t in range(tiles):
        left = remaining[t]
        for piece in arrived[1:]:
            left = add_emissions(left, piece, bins, t)
        residual[t] = weights[t] * left

    for d, piece in enumerate(arrived):
        source = lax.rem(here + (owners - d), owners)
        pieces = []
        for rank in range(capacity):
            place = piece[rank, bins : bins + 1, :]
            misfit = jnp.zeros((bins, pixels), F32)
            weight = jnp.zeros((bins, pixels), F32)
            for t in range(tiles):
                match = place == float(t)
                misfit = jnp.where(match, residual[t], misfit)
                weight = jnp.where(match, weights[t], weight)
            pieces.append((misfit, weight))
        for e in range(planes):
            rows = slice(e * share, (e + 1) * share)
            parts = [part[rows] for pair in pieces for part in pair]
            back[source * planes + e] = jnp.concatenate(parts, 0).astype(BF16)


def three_parts(values):
    high = values.astype(BF16).astype(F32)
    rest = values - high
    middle = rest.astype(BF16).astype(F32)
    return high, middle, rest - middle


def spread(row, base, count):
    turned = pltpu.roll(row, row.shape[1] - base, 1)
    return [jnp.broadcast_to(turned[:, u : u + 1], row.shape) for u in range(count)]


def minus_products(start, factors, rows):
    terms = [factor * row for factor, row in zip(factors, rows)]
    while len(terms) > 1:
        terms = [sum(terms[i : i + 2]) for i in range(0, len(terms), 2)]
    return start - terms[0]


def pivot_rows(rows, base, lane):
    inside = (lane >= base) & (lane < base + PIVOTS)
    out = [
        jnp.where(inside, jnp.where(lane == base + t, 1.0, 0.0), rows[t]) for t in range(PIVOTS)
    ]
    turned = [pltpu.roll(row, lane.shape[1] - base, 1) for row in rows]
    block = [[None] * PIVOTS for _ in range(PIVOTS)]
    for u in range(PIVOTS):
        for t in range(u + 1):
            block[t][u] = jnp.broadcast_to(turned[t][:, u : u + 1], lane.shape)
    for j in range(PIVOTS):
        inverse = 1.0 / block[j][j]
        raw = list(block[j])
        out[j] = out[j] * inverse
        for u in range(j + 1, PIVOTS):
            block[j][u] = raw[u] * inverse
        for i in range(j + 1, PIVOTS):
            for u in range(i, PIVOTS):
                block[i][u] = block[i][u] - raw[i] * block[j][u]
            out[i] = out[i] - raw[i] * out[j]
    for j in range(PIVOTS - 1, 0, -1):
        for i in range(j):
            out[i] = out[i] - block[i][j] * out[j]
    return [jnp.where(inside, -row, row) for row in out]


def eliminate(matrix, ahead, panel, right_side):
    width = matrix.shape[1]
    steps = width // PIVOTS
    lane = lax.broadcasted_iota(jnp.int32, (ROWS, width), 1)
    thin = lax.broadcasted_iota(jnp.int32, (1, width), 1)
    def load(base):
        return [matrix[pl.ds(base + t, ROWS, stride=width), :] for t in range(PIVOTS)]

    def look_ahead(rows, base):
        turned = [pltpu.roll(row, width - base, 1) for row in rows]
        for t in range(PIVOTS):
            for u in range(PIVOTS):
                ahead[t * PIVOTS + u] = jnp.broadcast_to(turned[u][:, t : t + 1], lane.shape)

    def apply(vector, base, new):
        inside = (lane >= base) & (lane < base + PIVOTS)
        return minus_products(jnp.where(inside, 0.0, vector), spread(vector, base, PIVOTS), new)

    def one_panel(first, step, carry):
        new, vector = list(carry[:-1]), carry[-1]
        base = pl.multiple_of(step * PIVOTS, PIVOTS)
        following = pl.multiple_of(base + PIVOTS, PIVOTS)
        inside = (lane >= base) & (lane < base + PIVOTS)
        rows = [
            minus_products(
                jnp.where(inside, 0.0, row), [ahead[t * PIVOTS + u] for u in range(PIVOTS)], new
            )
            for t, row in enumerate(load(following))
        ]
        for t in range(PIVOTS):
            panel[pl.ds(t, ROWS, stride=PIVOTS), :] = new[t]
        old = [matrix[pl.ds(b * width + base, PIVOTS), :] for b in range(ROWS)]
        mine = [panel[b * PIVOTS : (b + 1) * PIVOTS, :] for b in range(ROWS)]
        within = (thin >= base) & (thin < base + PIVOTS)
        for group in range(0, ROWS, TOGETHER):
            left, right = [], []
            for b in range(TOGETHER):
                a1, a2, a3 = three_parts(old[group + b])
                b1, b2, b3 = three_parts(mine[group + b])
                left.extend([a1, a1, a2, a2, a1, a3])
                parts = jnp.concatenate([b1, b2, b1, b2, b3, b1], 0).astype(BF16)
                blank = jnp.zeros_like(parts)
                right.append(
                    jnp.concatenate([parts if i == b else blank for i in range(TOGETHER)], 1)
                )
            turned = jnp.concatenate(left, 0).astype(BF16).T[first:]
            change = jnp.dot(turned, jnp.concatenate(right, 0), preferred_element_type=F32)
            for b in range(TOGETHER):
                rest = slice((group + b) * width + first, (group + b + 1) * width)
                matrix[rest, :] = (
                    jnp.where(within, 0.0, matrix[rest, :]) - change[:, b * width : (b + 1) * width]
                )
        newer = pivot_rows(rows, following, lane)
        look_ahead(rows, following + PIVOTS)
        return (*newer, apply(vector, base, new))

    rows = load(0)
    carry = (*pivot_rows(rows, 0, lane), right_side)
    look_ahead(rows, PIVOTS)
    phases = 4 if steps % 4 == 0 else 1
    length = steps // phases
    for phase in range(phases):
        low, high = max(phase * length - 1, 0), (phase + 1) * length - 1
        step = functools.partial(one_panel, phase * length * PIVOTS)
        carry = lax.fori_loop(low, high, step, carry)
    return apply(carry[-1], width - PIVOTS, list(carry[:-1]))


def newton_kernel(shifts, sides, capacity, group, *refs):
    plane = lax.axis_index(("bin", "rep"))
    planes = len(shifts)
    messages, (back, release, mean, prior, out, halves, gram, ahead, panel) = refs[:planes], refs[planes:]
    chunks, _, pixels = messages[0].shape
    owners = back.shape[0] // planes
    bins, releases = release.shape
    share = bins // planes
    pair = 2 * share
    top = share * releases
    if chunks > 1:
        gram[...] = jnp.zeros(gram.shape, F32)

    def one_chunk(prints, e, i, chunk):
        left = halves.at[i % 2]
        targets = prints[chunk, group * releases :, :].astype(F32)
        values = []
        for o in range(owners):
            block = back[o * planes + e].astype(F32)
            values.extend(block[r * pair : (r + 1) * pair] for r in range(capacity))
        for j in range(group):
            picked = jnp.zeros((pair, pixels), F32)
            for s, value in enumerate(values):
                picked = jnp.where(targets[j : j + 1] == float(s), value, picked)
            columns = slice(j * pixels, (j + 1) * pixels)
            block = prints[chunk, j * releases : (j + 1) * releases, :]
            for b in range(share):
                weight = jnp.broadcast_to(picked[share + b : share + b + 1], (2 * ROWS, pixels))
                weight = weight.astype(BF16)
                for r in range(0, releases, 2 * ROWS):
                    rows = slice(b * releases + r, b * releases + r + 2 * ROWS)
                    left[rows, columns] = block[r : r + 2 * ROWS] * weight
            if pair < 2 * ROWS:
                picked = jnp.concatenate([picked, jnp.zeros((2 * ROWS - pair, pixels), F32)], 0)
            left[top:, columns] = picked.astype(BF16)
        right = jnp.concatenate(
            [prints[chunk, j * releases : (j + 1) * releases, :] for j in range(group)], 1
        )
        product = lax.dot_general(
            left[...], right, (((1,), (1,)), ((), ())), preferred_element_type=F32
        )
        if i or chunks > 1:
            product += gram[: top + 2 * ROWS, :]
        gram[: top + 2 * ROWS, :] = product

    along, across = lax.div(plane, sides[1]), lax.rem(plane, sides[1])
    for i, (prints, (far, near)) in enumerate(zip(messages, shifts)):
        e = lax.rem(along + far, sides[0]) * sides[1] + lax.rem(across + near, sides[1])
        pl.loop(0, chunks, unroll=chunks == 1)(functools.partial(one_chunk, prints, e, i))

    def own(array):
        rows = array[...]
        mine = rows[:share]
        for e in range(1, planes):
            mine = jnp.where(plane == e, rows[e * share : (e + 1) * share], mine)
        if share < ROWS:
            mine = jnp.concatenate([mine, jnp.zeros((ROWS - share, releases), F32)], 0)
        return mine

    log_release, prior_mean, prior_weight = own(release), own(mean), own(prior)
    unslope = 1.0 + jnp.exp(-log_release)
    gradient = gram[top : top + ROWS, :]
    right_side = gradient - prior_weight * (log_release - prior_mean) * unslope
    diagonal = prior_weight * unslope * unslope
    row = lax.broadcasted_iota(jnp.int32, (releases, releases), 0)
    column = lax.broadcasted_iota(jnp.int32, (releases, releases), 1)
    for b in range(ROWS):
        block = slice(b * releases, (b + 1) * releases)
        if b < share:
            matrix = gram[block, :]
            matrix = 0.5 * (matrix + matrix.T)
            gram[block, :] = matrix + jnp.where(row == column, diagonal[b : b + 1], 0.0)
        else:
            gram[block, :] = jnp.where(row == column, 1.0, 0.0)
    systems = gram.at[pl.ds(0, ROWS * releases)]
    update = log_release + unslope * eliminate(systems, ahead, panel, right_side)
    out[...] = update[:share]


def newton_scratch(share, group, releases, pixels):
    height = share * releases + 2 * ROWS
    return [
        pltpu.VMEM((2, height, group * pixels), BF16),
        pltpu.VMEM((max(height, ROWS * releases), releases), F32),
        pltpu.VMEM((PIVOTS * PIVOTS, ROWS, releases), F32),
        pltpu.VMEM((ROWS * PIVOTS, releases), F32),
    ]


def shifted(array, axis, distance):
    if not distance:
        return array
    size = lax.axis_size(axis)
    return lax.ppermute(array, axis, [((i + distance) % size, i) for i in range(size)])


def params():
    return pltpu.CompilerParams(vmem_limit_bytes=LIMIT)


def body(
    footprint, block_tile, log_release, prior_mean, prior_weight, observed, noise_weight, pixel_mask
):
    blocks, releases, pixels = footprint.shape
    owners = lax.axis_size("rel")
    planes = lax.axis_size(("bin", "rep"))
    tiles, bins, _ = observed.shape
    capacity = blocks * 4 // 3 // owners
    slots = owners * capacity
    share = bins // planes
    group = math.gcd(blocks, 6)
    chunks = blocks // group
    local = pl.BlockSpec(memory_space=pltpu.VMEM)
    remote = pl.BlockSpec(memory_space=pltpu.HBM)
    release, mean, prior = log_release.T, prior_mean.T, prior_weight.T

    message, *sent = pl.pallas_call(
        functools.partial(emission_kernel, tiles, capacity, blocks),
        out_shape=(
            jax.ShapeDtypeStruct((chunks, group * releases + 2 * ROWS, pixels), BF16),
            *[jax.ShapeDtypeStruct((capacity, bins + ROWS, pixels), F32)] * owners,
        ),
        in_specs=[remote] * 3,
        out_specs=(local,) * (1 + owners),
        scratch_shapes=[
            pltpu.VMEM((slots, bins + ROWS, pixels), F32),
            pltpu.SMEM(block_tile.shape, jnp.int32),
            pltpu.VMEM(release.shape, F32),
            pltpu.SemaphoreType.DMA,
            pltpu.SemaphoreType.DMA,
            pltpu.SemaphoreType.DMA((chunks,)),
        ],
    )(block_tile, release, footprint.reshape(chunks, group * releases, pixels))
    arrived = [shifted(piece, "rel", owners - d if d else 0) for d, piece in enumerate(sent)]
    sides = (lax.axis_size("bin"), lax.axis_size("rep"))
    shifts, messages = [], []
    for far in range(sides[0]):
        moved = shifted(message, "bin", far)
        for near in range(sides[1]):
            shifts.append((far, near))
            messages.append(shifted(moved, "rep", near))

    remaining, weights = pl.pallas_call(
        prepare_kernel,
        out_shape=(jax.ShapeDtypeStruct(observed.shape, F32),) * 2,
        in_specs=[local] * 4,
        out_specs=(local, local),
        compiler_params=params(),
    )(observed, noise_weight, pixel_mask, arrived[0])
    arrived[1:], messages[1:-1] = lax.optimization_barrier((arrived[1:], messages[1:-1]))
    residual, back = pl.pallas_call(
        functools.partial(residual_kernel, planes, owners),
        out_shape=(
            jax.ShapeDtypeStruct(observed.shape, F32),
            jax.ShapeDtypeStruct((owners * planes, capacity * 2 * share, pixels), BF16),
        ),
        in_specs=[local] * (2 + owners),
        out_specs=(local, local),
        compiler_params=params(),
    )(remaining, weights, *arrived)
    back = lax.all_to_all(back, ("rel", "bin", "rep"), split_axis=0, concat_axis=0, tiled=True)

    release_new = pl.pallas_call(
        functools.partial(newton_kernel, shifts, sides, capacity, group),
        out_shape=jax.ShapeDtypeStruct((share, releases), F32),
        in_specs=[local] * (planes + 4),
        out_specs=local,
        scratch_shapes=newton_scratch(share, group, releases, pixels),
        compiler_params=params(),
    )(*messages, back, release, mean, prior)
    return (release_new.T, residual)


def solution(mesh):
    in_specs = (
        P(("groups", "rel", "bin", "rep"), None, None),
        P(("groups", "rel", "bin", "rep")),
        P(("groups", "rel"), None),
        P(("groups", "rel"), None),
        P(("groups", "rel"), None),
        P(("groups", "rel", "bin", "rep"), None, None),
        P(("groups", "rel", "bin", "rep"), None, None),
        P(("groups", "rel", "bin", "rep"), None),
    )
    out_specs = (
        P(("groups", "rel"), ("bin", "rep")),
        P(("groups", "rel", "bin", "rep"), None, None),
    )
    return jax.shard_map(body, mesh=mesh, in_specs=in_specs, out_specs=out_specs, check_vma=False)
```

```python
import functools
import math

import jax
import jax.numpy as jnp
from jax import lax
from jax.experimental import pallas as pl
from jax.experimental.pallas import tpu as pltpu
from jax.sharding import PartitionSpec as P

PIVOTS = 8
ROWS = 8
TOGETHER = 4
LIMIT = 48 << 20
F32 = jnp.float32
BF16 = jnp.bfloat16


def emission_kernel(
    tiles, capacity, blocks, tile_source, release_source, print_source, message, *refs
):
    owners = len(refs) - 6
    pieces, (sent, tile_of, release, tile_ready, release_ready, print_ready) = (
        refs[:owners],
        refs[owners:],
    )
    here = lax.axis_index("rel")
    chunks, length, pixels = print_source.shape
    group = blocks // chunks
    releases = length // group
    slots, padded, _ = sent.shape
    bins = padded - ROWS
    copies = [
        pltpu.make_async_copy(
            print_source.at[c], message.at[c, pl.ds(0, length)], print_ready.at[c]
        )
        for c in range(chunks)
    ]
    tile_copy = pltpu.make_async_copy(tile_source, tile_of, tile_ready)
    release_copy = pltpu.make_async_copy(release_source, release, release_ready)
    tile_copy.start()
    release_copy.start()
    for copy in copies:
        copy.start()
    sent[...] = jnp.full(sent.shape, -1.0, F32)
    release_copy.wait()
    value = release[...]
    rates = (jnp.maximum(value, 0.0) + jnp.log1p(jnp.exp(-jnp.abs(value)))).astype(BF16)
    tile_copy.wait()
    owner, rank = None, None
    for c in range(chunks):
        copies[c].wait()
        rows = []
        for j in range(group):
            k = c * group + j
            mine = lax.div(tile_of[k], tiles)
            rank = jnp.where(mine == owner, rank + 1, 0) if k else 0
            owner = mine
            target = owner * capacity + rank
            emission = lax.dot_general(
                rates,
                message[c, j * releases : (j + 1) * releases, :],
                (((1,), (0,)), ((), ())),
                preferred_element_type=F32,
            )
            local = lax.rem(tile_of[k], tiles).astype(F32)
            place = lax.rem(owner + (owners - here), owners) * capacity + rank
            sent[place, :bins, :] = emission
            sent[place, bins:, :] = jnp.full((ROWS, pixels), local, F32)
            rows.append(jnp.full((1, pixels), target.astype(F32), F32))
        rows.append(jnp.full((2 * ROWS - group, pixels), -1.0, F32))
        message[c, length:, :] = jnp.concatenate(rows, 0).astype(BF16)
    for d, piece in enumerate(pieces):
        piece[...] = sent[d * capacity : (d + 1) * capacity]


def add_emissions(start, piece, bins, tile):
    for rank in range(piece.shape[0]):
        match = piece[rank, bins : bins + 1, :] == float(tile)
        start = start - jnp.where(match, piece[rank, :bins, :], 0.0)
    return start


def prepare_kernel(observed, noise, mask, own, remaining, weights):
    tiles, bins, _ = observed.shape
    for t in range(tiles):
        weights[t] = mask[t : t + 1, :].astype(F32) * noise[t]
        remaining[t] = add_emissions(observed[t], own, bins, t)


def residual_kernel(planes, owners, remaining, weights, *refs):
    arrived, (residual, back) = refs[:owners], refs[owners:]
    capacity, padded, pixels = arrived[0].shape
    tiles, bins, _ = remaining.shape
    share = bins // planes
    here = lax.axis_index("rel")

    for t in range(tiles):
        left = remaining[t]
        for piece in arrived[1:]:
            left = add_emissions(left, piece, bins, t)
        residual[t] = weights[t] * left

    for d, piece in enumerate(arrived):
        source = lax.rem(here + (owners - d), owners)
        pieces = []
        for rank in range(capacity):
            place = piece[rank, bins : bins + 1, :]
            misfit = jnp.zeros((bins, pixels), F32)
            weight = jnp.zeros((bins, pixels), F32)
            for t in range(tiles):
                match = place == float(t)
                misfit = jnp.where(match, residual[t], misfit)
                weight = jnp.where(match, weights[t], weight)
            pieces.append((misfit, weight))
        for e in range(planes):
            rows = slice(e * share, (e + 1) * share)
            parts = [part[rows] for pair in pieces for part in pair]
            back[source * planes + e] = jnp.concatenate(parts, 0).astype(BF16)


def three_parts(values):
    high = values.astype(BF16).astype(F32)
    rest = values - high
    middle = rest.astype(BF16).astype(F32)
    return high, middle, rest - middle


def spread(row, base, count):
    turned = pltpu.roll(row, row.shape[1] - base, 1)
    return [jnp.broadcast_to(turned[:, u : u + 1], row.shape) for u in range(count)]


def minus_products(start, factors, rows):
    terms = [factor * row for factor, row in zip(factors, rows)]
    while len(terms) > 1:
        terms = [sum(terms[i : i + 2]) for i in range(0, len(terms), 2)]
    return start - terms[0]


def beside_zeros(rows, place):
    zeros = jnp.zeros_like(rows)
    pair = jnp.concatenate([zeros, rows] if place % 2 else [rows, zeros], 0).astype(BF16)
    blank = jnp.zeros_like(pair)
    return jnp.concatenate([pair if i == place // 2 else blank for i in range(TOGETHER // 2)], 0)


def pivot_rows(rows, base, lane):
    inside = (lane >= base) & (lane < base + PIVOTS)
    out = [
        jnp.where(inside, jnp.where(lane == base + t, 1.0, 0.0), rows[t]) for t in range(PIVOTS)
    ]
    turned = [pltpu.roll(row, lane.shape[1] - base, 1) for row in rows]
    block = [[None] * PIVOTS for _ in range(PIVOTS)]
    for u in range(PIVOTS):
        for t in range(u + 1):
            block[t][u] = jnp.broadcast_to(turned[t][:, u : u + 1], lane.shape)
    for j in range(PIVOTS):
        inverse = 1.0 / block[j][j]
        raw = list(block[j])
        out[j] = out[j] * inverse
        for u in range(j + 1, PIVOTS):
            block[j][u] = raw[u] * inverse
        for i in range(j + 1, PIVOTS):
            for u in range(i, PIVOTS):
                block[i][u] = block[i][u] - raw[i] * block[j][u]
            out[i] = out[i] - raw[i] * out[j]
    for j in range(PIVOTS - 1, 0, -1):
        for i in range(j):
            out[i] = out[i] - block[i][j] * out[j]
    return [jnp.where(inside, -row, row) for row in out]


def eliminate(matrix, ahead, panel, right_side):
    width = matrix.shape[1]
    steps = width // PIVOTS
    lane = lax.broadcasted_iota(jnp.int32, (ROWS, width), 1)
    thin = lax.broadcasted_iota(jnp.int32, (1, width), 1)
    def load(base):
        return [matrix[pl.ds(base + t, ROWS, stride=width), :] for t in range(PIVOTS)]

    def look_ahead(rows, base):
        turned = [pltpu.roll(row, width - base, 1) for row in rows]
        for t in range(PIVOTS):
            for u in range(PIVOTS):
                ahead[t * PIVOTS + u] = jnp.broadcast_to(turned[u][:, t : t + 1], lane.shape)

    def apply(vector, base, new):
        inside = (lane >= base) & (lane < base + PIVOTS)
        return minus_products(jnp.where(inside, 0.0, vector), spread(vector, base, PIVOTS), new)

    def one_panel(first, step, carry):
        new, vector = list(carry[:-1]), carry[-1]
        base = pl.multiple_of(step * PIVOTS, PIVOTS)
        following = pl.multiple_of(base + PIVOTS, PIVOTS)
        inside = (lane >= base) & (lane < base + PIVOTS)
        rows = [
            minus_products(
                jnp.where(inside, 0.0, row), [ahead[t * PIVOTS + u] for u in range(PIVOTS)], new
            )
            for t, row in enumerate(load(following))
        ]
        for t in range(PIVOTS):
            panel[pl.ds(t, ROWS, stride=PIVOTS), :] = new[t]
        old = [matrix[pl.ds(b * width + base, PIVOTS), :] for b in range(ROWS)]
        mine = [panel[b * PIVOTS : (b + 1) * PIVOTS, :] for b in range(ROWS)]
        within = (thin >= base) & (thin < base + PIVOTS)
        for group in range(0, ROWS, TOGETHER):
            thirds = zip(*[three_parts(row) for row in old[group : group + TOGETHER]])
            a1, a2, a3 = [jnp.concatenate(third, 0).astype(BF16) for third in thirds]
            turned = jnp.concatenate([a1, a2, a3, a1], 0).T[first:]
            right = []
            for b in range(TOGETHER):
                b1, b2, b3 = [beside_zeros(part, b) for part in three_parts(mine[group + b])]
                blank = jnp.zeros_like(b1)
                right.append(jnp.concatenate([b1, b1, b1, b3, b2, b2, blank, blank], 0))
            change = jnp.dot(
                jnp.concatenate([turned, turned], 1),
                jnp.concatenate(right, 1),
                preferred_element_type=F32,
            )
            for b in range(TOGETHER):
                rest = slice((group + b) * width + first, (group + b + 1) * width)
                matrix[rest, :] = (
                    jnp.where(within, 0.0, matrix[rest, :]) - change[:, b * width : (b + 1) * width]
                )
        newer = pivot_rows(rows, following, lane)
        look_ahead(rows, following + PIVOTS)
        return (*newer, apply(vector, base, new))

    rows = load(0)
    carry = (*pivot_rows(rows, 0, lane), right_side)
    look_ahead(rows, PIVOTS)
    phases = 4 if steps % 4 == 0 else 1
    length = steps // phases
    for phase in range(phases):
        low, high = max(phase * length - 1, 0), (phase + 1) * length - 1
        step = functools.partial(one_panel, phase * length * PIVOTS)
        carry = lax.fori_loop(low, high, step, carry)
    return apply(carry[-1], width - PIVOTS, list(carry[:-1]))


def newton_kernel(shifts, sides, capacity, group, *refs):
    plane = lax.axis_index(("bin", "rep"))
    planes = len(shifts)
    messages, (back, release, mean, prior, out, halves, gram, ahead, panel) = refs[:planes], refs[planes:]
    chunks, _, pixels = messages[0].shape
    owners = back.shape[0] // planes
    bins, releases = release.shape
    share = bins // planes
    pair = 2 * share
    top = share * releases
    if chunks > 1:
        gram[...] = jnp.zeros(gram.shape, F32)

    def one_chunk(prints, e, i, chunk):
        left = halves.at[i % 2]
        targets = prints[chunk, group * releases :, :].astype(F32)
        values = []
        for o in range(owners):
            block = back[o * planes + e].astype(F32)
            values.extend(block[r * pair : (r + 1) * pair] for r in range(capacity))
        for j in range(group):
            picked = jnp.zeros((pair, pixels), F32)
            for s, value in enumerate(values):
                picked = jnp.where(targets[j : j + 1] == float(s), value, picked)
            columns = slice(j * pixels, (j + 1) * pixels)
            block = prints[chunk, j * releases : (j + 1) * releases, :]
            for b in range(share):
                weight = jnp.broadcast_to(picked[share + b : share + b + 1], (2 * ROWS, pixels))
                weight = weight.astype(BF16)
                for r in range(0, releases, 2 * ROWS):
                    rows = slice(b * releases + r, b * releases + r + 2 * ROWS)
                    left[rows, columns] = block[r : r + 2 * ROWS] * weight
            if pair < 2 * ROWS:
                picked = jnp.concatenate([picked, jnp.zeros((2 * ROWS - pair, pixels), F32)], 0)
            left[top:, columns] = picked.astype(BF16)
        right = jnp.concatenate(
            [prints[chunk, j * releases : (j + 1) * releases, :] for j in range(group)], 1
        )
        product = lax.dot_general(
            left[...], right, (((1,), (1,)), ((), ())), preferred_element_type=F32
        )
        if i or chunks > 1:
            product += gram[: top + 2 * ROWS, :]
        gram[: top + 2 * ROWS, :] = product

    along, across = lax.div(plane, sides[1]), lax.rem(plane, sides[1])
    for i, (prints, (far, near)) in enumerate(zip(messages, shifts)):
        e = lax.rem(along + far, sides[0]) * sides[1] + lax.rem(across + near, sides[1])
        pl.loop(0, chunks, unroll=chunks == 1)(functools.partial(one_chunk, prints, e, i))

    def own(array):
        rows = array[...]
        mine = rows[:share]
        for e in range(1, planes):
            mine = jnp.where(plane == e, rows[e * share : (e + 1) * share], mine)
        if share < ROWS:
            mine = jnp.concatenate([mine, jnp.zeros((ROWS - share, releases), F32)], 0)
        return mine

    log_release, prior_mean, prior_weight = own(release), own(mean), own(prior)
    unslope = 1.0 + jnp.exp(-log_release)
    gradient = gram[top : top + ROWS, :]
    right_side = gradient - prior_weight * (log_release - prior_mean) * unslope
    diagonal = prior_weight * unslope * unslope
    row = lax.broadcasted_iota(jnp.int32, (releases, releases), 0)
    column = lax.broadcasted_iota(jnp.int32, (releases, releases), 1)
    for b in range(ROWS):
        block = slice(b * releases, (b + 1) * releases)
        if b < share:
            matrix = gram[block, :]
            matrix = 0.5 * (matrix + matrix.T)
            gram[block, :] = matrix + jnp.where(row == column, diagonal[b : b + 1], 0.0)
        else:
            gram[block, :] = jnp.where(row == column, 1.0, 0.0)
    systems = gram.at[pl.ds(0, ROWS * releases)]
    update = log_release + unslope * eliminate(systems, ahead, panel, right_side)
    out[...] = update[:share]


def newton_scratch(share, group, releases, pixels):
    height = share * releases + 2 * ROWS
    return [
        pltpu.VMEM((2, height, group * pixels), BF16),
        pltpu.VMEM((max(height, ROWS * releases), releases), F32),
        pltpu.VMEM((PIVOTS * PIVOTS, ROWS, releases), F32),
        pltpu.VMEM((ROWS * PIVOTS, releases), F32),
    ]


def shifted(array, axis, distance):
    if not distance:
        return array
    size = lax.axis_size(axis)
    return lax.ppermute(array, axis, [((i + distance) % size, i) for i in range(size)])


def params():
    return pltpu.CompilerParams(vmem_limit_bytes=LIMIT)


def body(
    footprint, block_tile, log_release, prior_mean, prior_weight, observed, noise_weight, pixel_mask
):
    blocks, releases, pixels = footprint.shape
    owners = lax.axis_size("rel")
    planes = lax.axis_size(("bin", "rep"))
    tiles, bins, _ = observed.shape
    capacity = blocks * 4 // 3 // owners
    slots = owners * capacity
    share = bins // planes
    group = math.gcd(blocks, 6)
    chunks = blocks // group
    local = pl.BlockSpec(memory_space=pltpu.VMEM)
    remote = pl.BlockSpec(memory_space=pltpu.HBM)
    release, mean, prior = log_release.T, prior_mean.T, prior_weight.T

    message, *sent = pl.pallas_call(
        functools.partial(emission_kernel, tiles, capacity, blocks),
        out_shape=(
            jax.ShapeDtypeStruct((chunks, group * releases + 2 * ROWS, pixels), BF16),
            *[jax.ShapeDtypeStruct((capacity, bins + ROWS, pixels), F32)] * owners,
        ),
        in_specs=[remote] * 3,
        out_specs=(local,) * (1 + owners),
        scratch_shapes=[
            pltpu.VMEM((slots, bins + ROWS, pixels), F32),
            pltpu.SMEM(block_tile.shape, jnp.int32),
            pltpu.VMEM(release.shape, F32),
            pltpu.SemaphoreType.DMA,
            pltpu.SemaphoreType.DMA,
            pltpu.SemaphoreType.DMA((chunks,)),
        ],
    )(block_tile, release, footprint.reshape(chunks, group * releases, pixels))
    arrived = [shifted(piece, "rel", owners - d if d else 0) for d, piece in enumerate(sent)]
    sides = (lax.axis_size("bin"), lax.axis_size("rep"))
    shifts, messages = [], []
    for far in range(sides[0]):
        moved = shifted(message, "bin", far)
        for near in range(sides[1]):
            shifts.append((far, near))
            messages.append(shifted(moved, "rep", near))

    remaining, weights = pl.pallas_call(
        prepare_kernel,
        out_shape=(jax.ShapeDtypeStruct(observed.shape, F32),) * 2,
        in_specs=[local] * 4,
        out_specs=(local, local),
        compiler_params=params(),
    )(observed, noise_weight, pixel_mask, arrived[0])
    arrived[1:], messages[1:-1] = lax.optimization_barrier((arrived[1:], messages[1:-1]))
    residual, back = pl.pallas_call(
        functools.partial(residual_kernel, planes, owners),
        out_shape=(
            jax.ShapeDtypeStruct(observed.shape, F32),
            jax.ShapeDtypeStruct((owners * planes, capacity * 2 * share, pixels), BF16),
        ),
        in_specs=[local] * (2 + owners),
        out_specs=(local, local),
        compiler_params=params(),
    )(remaining, weights, *arrived)
    back = lax.all_to_all(back, ("rel", "bin", "rep"), split_axis=0, concat_axis=0, tiled=True)

    release_new = pl.pallas_call(
        functools.partial(newton_kernel, shifts, sides, capacity, group),
        out_shape=jax.ShapeDtypeStruct((share, releases), F32),
        in_specs=[local] * (planes + 4),
        out_specs=local,
        scratch_shapes=newton_scratch(share, group, releases, pixels),
        compiler_params=params(),
    )(*messages, back, release, mean, prior)
    return (release_new.T, residual)


def solution(mesh):
    in_specs = (
        P(("groups", "rel", "bin", "rep"), None, None),
        P(("groups", "rel", "bin", "rep")),
        P(("groups", "rel"), None),
        P(("groups", "rel"), None),
        P(("groups", "rel"), None),
        P(("groups", "rel", "bin", "rep"), None, None),
        P(("groups", "rel", "bin", "rep"), None, None),
        P(("groups", "rel", "bin", "rep"), None),
    )
    out_specs = (
        P(("groups", "rel"), ("bin", "rep")),
        P(("groups", "rel", "bin", "rep"), None, None),
    )
    return jax.shard_map(body, mesh=mesh, in_specs=in_specs, out_specs=out_specs, check_vma=False)
```

```python
import functools
import math

import jax
import jax.numpy as jnp
from jax import lax
from jax.experimental import pallas as pl
from jax.experimental.pallas import tpu as pltpu
from jax.sharding import PartitionSpec as P

PIVOTS = 8
ROWS = 8
TOGETHER = 4
LIMIT = 48 << 20
F32 = jnp.float32
BF16 = jnp.bfloat16


def emission_kernel(tiles, capacity, tile_source, release_source, print_source, *refs):
    pieces, scratch = refs[:-7], refs[-7:]
    sent, tile_of, release, prints, tile_ready, release_ready, print_ready = scratch
    blocks, _, pixels = prints.shape
    owners = len(pieces)
    bins = release.shape[0]
    here = lax.axis_index("rel")
    tile_copy = pltpu.make_async_copy(tile_source, tile_of, tile_ready)
    release_copy = pltpu.make_async_copy(release_source, release, release_ready)
    print_copies = [
        pltpu.make_async_copy(print_source.at[k], prints.at[k], print_ready.at[k])
        for k in range(blocks)
    ]
    for copy in [tile_copy, release_copy, *print_copies]:
        copy.start()
    sent[...] = jnp.full(sent.shape, -1.0, F32)
    release_copy.wait()
    value = release[...]
    rates = (jnp.maximum(value, 0.0) + jnp.log1p(jnp.exp(-jnp.abs(value)))).astype(BF16)
    tile_copy.wait()
    owner, rank = None, None
    for k in range(blocks):
        mine = lax.div(tile_of[k], tiles)
        rank = jnp.where(mine == owner, rank + 1, 0) if k else 0
        owner = mine
        place = lax.rem(owner + (owners - here), owners) * capacity + rank
        print_copies[k].wait()
        sent[place, :bins, :] = lax.dot_general(
            rates, prints[k], (((1,), (0,)), ((), ())), preferred_element_type=F32
        )
        local = lax.rem(tile_of[k], tiles).astype(F32)
        sent[place, bins:, :] = jnp.full((ROWS, pixels), local, F32)
    for d, piece in enumerate(pieces):
        piece[...] = sent[d * capacity : (d + 1) * capacity]


def add_emissions(start, piece, bins, tile):
    for rank in range(piece.shape[0]):
        match = piece[rank, bins : bins + 1, :] == float(tile)
        start = start - jnp.where(match, piece[rank, :bins, :], 0.0)
    return start


def prepare_kernel(observed, noise, mask, own, remaining, weights):
    tiles, bins, _ = observed.shape
    for t in range(tiles):
        weights[t] = mask[t : t + 1, :].astype(F32) * noise[t]
        remaining[t] = add_emissions(observed[t], own, bins, t)


def residual_kernel(planes, owners, remaining, weights, *refs):
    arrived, (residual, back) = refs[:owners], refs[owners:]
    capacity, padded, pixels = arrived[0].shape
    tiles, bins, _ = remaining.shape
    share = bins // planes
    here = lax.axis_index("rel")

    for t in range(tiles):
        left = remaining[t]
        for piece in arrived[1:]:
            left = add_emissions(left, piece, bins, t)
        residual[t] = weights[t] * left

    for d, piece in enumerate(arrived):
        source = lax.rem(here + (owners - d), owners)
        pieces = []
        for rank in range(capacity):
            place = piece[rank, bins : bins + 1, :]
            misfit = jnp.zeros((bins, pixels), F32)
            weight = jnp.full((bins, pixels), -1.0, F32)
            for t in range(tiles):
                match = place == float(t)
                misfit = jnp.where(match, residual[t], misfit)
                weight = jnp.where(match, weights[t], weight)
            pieces.append((misfit, weight))
        for e in range(planes):
            rows = slice(e * share, (e + 1) * share)
            parts = [part[rows] for pair in pieces for part in pair]
            back[source * planes + e] = jnp.concatenate(parts, 0).astype(BF16)


def three_parts(values):
    high = values.astype(BF16).astype(F32)
    rest = values - high
    middle = rest.astype(BF16).astype(F32)
    return high, middle, rest - middle


def spread(row, base, count):
    turned = pltpu.roll(row, row.shape[1] - base, 1)
    return [jnp.broadcast_to(turned[:, u : u + 1], row.shape) for u in range(count)]


def minus_products(start, factors, rows):
    terms = [factor * row for factor, row in zip(factors, rows)]
    while len(terms) > 1:
        terms = [sum(terms[i : i + 2]) for i in range(0, len(terms), 2)]
    return start - terms[0]


def beside_zeros(rows, place):
    zeros = jnp.zeros_like(rows)
    pair = jnp.concatenate([zeros, rows] if place % 2 else [rows, zeros], 0).astype(BF16)
    blank = jnp.zeros_like(pair)
    return jnp.concatenate([pair if i == place // 2 else blank for i in range(TOGETHER // 2)], 0)


def pivot_rows(rows, base, lane):
    inside = (lane >= base) & (lane < base + PIVOTS)
    out = [
        jnp.where(inside, jnp.where(lane == base + t, 1.0, 0.0), rows[t]) for t in range(PIVOTS)
    ]
    turned = [pltpu.roll(row, lane.shape[1] - base, 1) for row in rows]
    block = [[None] * PIVOTS for _ in range(PIVOTS)]
    for u in range(PIVOTS):
        for t in range(u + 1):
            block[t][u] = jnp.broadcast_to(turned[t][:, u : u + 1], lane.shape)
    for j in range(PIVOTS):
        inverse = 1.0 / block[j][j]
        raw = list(block[j])
        out[j] = out[j] * inverse
        for u in range(j + 1, PIVOTS):
            block[j][u] = raw[u] * inverse
        for i in range(j + 1, PIVOTS):
            for u in range(i, PIVOTS):
                block[i][u] = block[i][u] - raw[i] * block[j][u]
            out[i] = out[i] - raw[i] * out[j]
    for j in range(PIVOTS - 1, 0, -1):
        for i in range(j):
            out[i] = out[i] - block[i][j] * out[j]
    return [jnp.where(inside, -row, row) for row in out]


def eliminate(matrix, ahead, panel, right_side):
    width = matrix.shape[1]
    steps = width // PIVOTS
    lane = lax.broadcasted_iota(jnp.int32, (ROWS, width), 1)
    thin = lax.broadcasted_iota(jnp.int32, (1, width), 1)
    def load(base):
        return [matrix[pl.ds(base + t, ROWS, stride=width), :] for t in range(PIVOTS)]

    def look_ahead(rows, base):
        turned = [pltpu.roll(row, width - base, 1) for row in rows]
        for t in range(PIVOTS):
            for u in range(PIVOTS):
                ahead[t * PIVOTS + u] = jnp.broadcast_to(turned[u][:, t : t + 1], lane.shape)

    def apply(vector, base, new):
        inside = (lane >= base) & (lane < base + PIVOTS)
        return minus_products(jnp.where(inside, 0.0, vector), spread(vector, base, PIVOTS), new)

    def one_panel(first, step, carry):
        new, vector = list(carry[:-1]), carry[-1]
        base = pl.multiple_of(step * PIVOTS, PIVOTS)
        following = pl.multiple_of(base + PIVOTS, PIVOTS)
        inside = (lane >= base) & (lane < base + PIVOTS)
        rows = [
            minus_products(
                jnp.where(inside, 0.0, row), [ahead[t * PIVOTS + u] for u in range(PIVOTS)], new
            )
            for t, row in enumerate(load(following))
        ]
        for t in range(PIVOTS):
            panel[pl.ds(t, ROWS, stride=PIVOTS), :] = new[t]
        old = [matrix[pl.ds(b * width + base, PIVOTS), :] for b in range(ROWS)]
        mine = [panel[b * PIVOTS : (b + 1) * PIVOTS, :] for b in range(ROWS)]
        within = (thin >= base) & (thin < base + PIVOTS)
        for group in range(0, ROWS, TOGETHER):
            thirds = zip(*[three_parts(row) for row in old[group : group + TOGETHER]])
            a1, a2, a3 = [jnp.concatenate(third, 0).astype(BF16) for third in thirds]
            turned = jnp.concatenate([a1, a2, a3, a1], 0).T[first:]
            right = []
            for b in range(TOGETHER):
                b1, b2, b3 = [beside_zeros(part, b) for part in three_parts(mine[group + b])]
                blank = jnp.zeros_like(b1)
                right.append(jnp.concatenate([b1, b1, b1, b3, b2, b2, blank, blank], 0))
            change = jnp.dot(
                jnp.concatenate([turned, turned], 1),
                jnp.concatenate(right, 1),
                preferred_element_type=F32,
            )
            for b in range(TOGETHER):
                rest = slice((group + b) * width + first, (group + b + 1) * width)
                matrix[rest, :] = (
                    jnp.where(within, 0.0, matrix[rest, :]) - change[:, b * width : (b + 1) * width]
                )
        newer = pivot_rows(rows, following, lane)
        look_ahead(rows, following + PIVOTS)
        return (*newer, apply(vector, base, new))

    rows = load(0)
    carry = (*pivot_rows(rows, 0, lane), right_side)
    look_ahead(rows, PIVOTS)
    phases = 4 if steps % 4 == 0 else 1
    length = steps // phases
    for phase in range(phases):
        low, high = max(phase * length - 1, 0), (phase + 1) * length - 1
        step = functools.partial(one_panel, phase * length * PIVOTS)
        carry = lax.fori_loop(low, high, step, carry)
    return apply(carry[-1], width - PIVOTS, list(carry[:-1]))


def newton_kernel(shifts, sides, capacity, group, *refs):
    plane = lax.axis_index(("bin", "rep"))
    planes = len(shifts)
    messages, (back, release, mean, prior, out, halves, gram, ahead, panel) = refs[:planes], refs[planes:]
    chunks, _, pixels = messages[0].shape
    owners = back.shape[0] // planes
    bins, releases = release.shape
    share = bins // planes
    pair = 2 * share
    top = share * releases
    if chunks > 1:
        gram[...] = jnp.zeros(gram.shape, F32)

    def one_chunk(prints, e, i, chunk):
        left = halves.at[i % 2]
        slots = []
        count = jnp.zeros((1, pixels), F32) - (chunk * group).astype(F32)
        for o in range(owners):
            block = back[o * planes + e].astype(F32)
            for r in range(capacity):
                value = block[r * pair : (r + 1) * pair]
                used = value[share : share + 1] >= 0.0
                slots.append((jnp.where(used, count, -1.0), value))
                count = count + jnp.where(used, 1.0, 0.0)
        for j in range(group):
            picked = jnp.zeros((pair, pixels), F32)
            for index, value in slots:
                picked = jnp.where(index == float(j), value, picked)
            columns = slice(j * pixels, (j + 1) * pixels)
            block = prints[chunk, j * releases : (j + 1) * releases, :]
            for b in range(share):
                weight = jnp.broadcast_to(picked[share + b : share + b + 1], (2 * ROWS, pixels))
                weight = weight.astype(BF16)
                for r in range(0, releases, 2 * ROWS):
                    rows = slice(b * releases + r, b * releases + r + 2 * ROWS)
                    left[rows, columns] = block[r : r + 2 * ROWS] * weight
            if pair < 2 * ROWS:
                picked = jnp.concatenate([picked, jnp.zeros((2 * ROWS - pair, pixels), F32)], 0)
            left[top:, columns] = picked.astype(BF16)
        right = jnp.concatenate(
            [prints[chunk, j * releases : (j + 1) * releases, :] for j in range(group)], 1
        )
        product = lax.dot_general(
            left[...], right, (((1,), (1,)), ((), ())), preferred_element_type=F32
        )
        if i or chunks > 1:
            product += gram[: top + 2 * ROWS, :]
        gram[: top + 2 * ROWS, :] = product

    along, across = lax.div(plane, sides[1]), lax.rem(plane, sides[1])
    for i, (prints, (far, near)) in enumerate(zip(messages, shifts)):
        e = lax.rem(along + far, sides[0]) * sides[1] + lax.rem(across + near, sides[1])
        pl.loop(0, chunks, unroll=chunks == 1)(functools.partial(one_chunk, prints, e, i))

    def own(array):
        rows = array[...]
        mine = rows[:share]
        for e in range(1, planes):
            mine = jnp.where(plane == e, rows[e * share : (e + 1) * share], mine)
        if share < ROWS:
            mine = jnp.concatenate([mine, jnp.zeros((ROWS - share, releases), F32)], 0)
        return mine

    log_release, prior_mean, prior_weight = own(release), own(mean), own(prior)
    unslope = 1.0 + jnp.exp(-log_release)
    gradient = gram[top : top + ROWS, :]
    right_side = gradient - prior_weight * (log_release - prior_mean) * unslope
    diagonal = prior_weight * unslope * unslope
    row = lax.broadcasted_iota(jnp.int32, (releases, releases), 0)
    column = lax.broadcasted_iota(jnp.int32, (releases, releases), 1)
    for b in range(ROWS):
        block = slice(b * releases, (b + 1) * releases)
        if b < share:
            matrix = gram[block, :]
            matrix = 0.5 * (matrix + matrix.T)
            gram[block, :] = matrix + jnp.where(row == column, diagonal[b : b + 1], 0.0)
        else:
            gram[block, :] = jnp.where(row == column, 1.0, 0.0)
    systems = gram.at[pl.ds(0, ROWS * releases)]
    update = log_release + unslope * eliminate(systems, ahead, panel, right_side)
    out[...] = update[:share]


def newton_scratch(share, group, releases, pixels):
    height = share * releases + 2 * ROWS
    return [
        pltpu.VMEM((2, height, group * pixels), BF16),
        pltpu.VMEM((max(height, ROWS * releases), releases), F32),
        pltpu.VMEM((PIVOTS * PIVOTS, ROWS, releases), F32),
        pltpu.VMEM((ROWS * PIVOTS, releases), F32),
    ]


def shifted(array, axis, distance):
    if not distance:
        return array
    size = lax.axis_size(axis)
    return lax.ppermute(array, axis, [((i + distance) % size, i) for i in range(size)])


def params():
    return pltpu.CompilerParams(vmem_limit_bytes=LIMIT)


def body(
    footprint, block_tile, log_release, prior_mean, prior_weight, observed, noise_weight, pixel_mask
):
    blocks, releases, pixels = footprint.shape
    owners = lax.axis_size("rel")
    planes = lax.axis_size(("bin", "rep"))
    tiles, bins, _ = observed.shape
    capacity = blocks * 4 // 3 // owners
    slots = owners * capacity
    share = bins // planes
    group = math.gcd(blocks, 6)
    chunks = blocks // group
    local = pl.BlockSpec(memory_space=pltpu.VMEM)
    remote = pl.BlockSpec(memory_space=pltpu.HBM)
    release, mean, prior = log_release.T, prior_mean.T, prior_weight.T

    message = footprint.reshape(chunks, group * releases, pixels)
    sent = pl.pallas_call(
        functools.partial(emission_kernel, tiles, capacity),
        out_shape=[jax.ShapeDtypeStruct((capacity, bins + ROWS, pixels), F32)] * owners,
        in_specs=[remote] * 3,
        out_specs=[local] * owners,
        scratch_shapes=[
            pltpu.VMEM((slots, bins + ROWS, pixels), F32),
            pltpu.SMEM(block_tile.shape, jnp.int32),
            pltpu.VMEM(release.shape, F32),
            pltpu.VMEM(footprint.shape, BF16),
            pltpu.SemaphoreType.DMA,
            pltpu.SemaphoreType.DMA,
            pltpu.SemaphoreType.DMA((blocks,)),
        ],
    )(block_tile, release, footprint)
    arrived = [shifted(piece, "rel", owners - d if d else 0) for d, piece in enumerate(sent)]
    sides = (lax.axis_size("bin"), lax.axis_size("rep"))
    shifts, messages = [], []
    for far in range(sides[0]):
        moved = shifted(message, "bin", far)
        for near in range(sides[1]):
            shifts.append((far, near))
            messages.append(shifted(moved, "rep", near))

    remaining, weights = pl.pallas_call(
        prepare_kernel,
        out_shape=(jax.ShapeDtypeStruct(observed.shape, F32),) * 2,
        in_specs=[local] * 4,
        out_specs=(local, local),
        compiler_params=params(),
    )(observed, noise_weight, pixel_mask, arrived[0])
    arrived[1:], messages[1:-1] = lax.optimization_barrier((arrived[1:], messages[1:-1]))
    residual, back = pl.pallas_call(
        functools.partial(residual_kernel, planes, owners),
        out_shape=(
            jax.ShapeDtypeStruct(observed.shape, F32),
            jax.ShapeDtypeStruct((owners * planes, capacity * 2 * share, pixels), BF16),
        ),
        in_specs=[local] * (2 + owners),
        out_specs=(local, local),
        compiler_params=params(),
    )(remaining, weights, *arrived)
    back = lax.all_to_all(back, ("rel", "bin", "rep"), split_axis=0, concat_axis=0, tiled=True)

    release_new = pl.pallas_call(
        functools.partial(newton_kernel, shifts, sides, capacity, group),
        out_shape=jax.ShapeDtypeStruct((share, releases), F32),
        in_specs=[local] * (planes + 4),
        out_specs=local,
        scratch_shapes=newton_scratch(share, group, releases, pixels),
        compiler_params=params(),
    )(*messages, back, release, mean, prior)
    return (release_new.T, residual)


def solution(mesh):
    in_specs = (
        P(("groups", "rel", "bin", "rep"), None, None),
        P(("groups", "rel", "bin", "rep")),
        P(("groups", "rel"), None),
        P(("groups", "rel"), None),
        P(("groups", "rel"), None),
        P(("groups", "rel", "bin", "rep"), None, None),
        P(("groups", "rel", "bin", "rep"), None, None),
        P(("groups", "rel", "bin", "rep"), None),
    )
    out_specs = (
        P(("groups", "rel"), ("bin", "rep")),
        P(("groups", "rel", "bin", "rep"), None, None),
    )
    return jax.shard_map(body, mesh=mesh, in_specs=in_specs, out_specs=out_specs, check_vma=False)
```

```python
import functools
import math

import jax
import jax.numpy as jnp
from jax import lax
from jax.experimental import pallas as pl
from jax.experimental.pallas import tpu as pltpu
from jax.sharding import PartitionSpec as P

PIVOTS = 8
ROWS = 8
TOGETHER = 4
LIMIT = 48 << 20
F32 = jnp.float32
BF16 = jnp.bfloat16


def emission_kernel(
    tiles, capacity, blocks, tile_source, release_source, print_source, message, *refs
):
    owners = len(refs) - 6
    pieces, (sent, tile_of, release, tile_ready, release_ready, print_ready) = (
        refs[:owners],
        refs[owners:],
    )
    here = lax.axis_index("rel")
    chunks, length, pixels = print_source.shape
    group = blocks // chunks
    releases = length // group
    slots, padded, _ = sent.shape
    bins = padded - ROWS
    copies = [
        pltpu.make_async_copy(
            print_source.at[c], message.at[c, pl.ds(0, length)], print_ready.at[c]
        )
        for c in range(chunks)
    ]
    tile_copy = pltpu.make_async_copy(tile_source, tile_of, tile_ready)
    release_copy = pltpu.make_async_copy(release_source, release, release_ready)
    tile_copy.start()
    release_copy.start()
    for copy in copies:
        copy.start()
    sent[...] = jnp.full(sent.shape, -1.0, F32)
    release_copy.wait()
    value = release[...]
    rates = (jnp.maximum(value, 0.0) + jnp.log1p(jnp.exp(-jnp.abs(value)))).astype(BF16)
    tile_copy.wait()
    owner, rank = None, None
    for c in range(chunks):
        copies[c].wait()
        rows = []
        for j in range(group):
            k = c * group + j
            mine = lax.div(tile_of[k], tiles)
            rank = jnp.where(mine == owner, rank + 1, 0) if k else 0
            owner = mine
            target = owner * capacity + rank
            emission = lax.dot_general(
                rates,
                message[c, j * releases : (j + 1) * releases, :],
                (((1,), (0,)), ((), ())),
                preferred_element_type=F32,
            )
            local = lax.rem(tile_of[k], tiles).astype(F32)
            place = lax.rem(owner + (owners - here), owners) * capacity + rank
            sent[place, :bins, :] = emission
            sent[place, bins:, :] = jnp.full((ROWS, pixels), local, F32)
            rows.append(jnp.full((1, pixels), target.astype(F32), F32))
        rows.append(jnp.full((2 * ROWS - group, pixels), -1.0, F32))
        message[c, length:, :] = jnp.concatenate(rows, 0).astype(BF16)
    for d, piece in enumerate(pieces):
        piece[...] = sent[d * capacity : (d + 1) * capacity]


def add_emissions(start, piece, bins, tile):
    for rank in range(piece.shape[0]):
        match = piece[rank, bins : bins + 1, :] == float(tile)
        start = start - jnp.where(match, piece[rank, :bins, :], 0.0)
    return start


def prepare_kernel(observed, noise, mask, own, remaining, weights):
    tiles, bins, _ = observed.shape
    for t in range(tiles):
        weights[t] = mask[t : t + 1, :].astype(F32) * noise[t]
        remaining[t] = add_emissions(observed[t], own, bins, t)


def residual_kernel(planes, owners, remaining, weights, *refs):
    arrived, (residual, back) = refs[:owners], refs[owners:]
    capacity, padded, pixels = arrived[0].shape
    tiles, bins, _ = remaining.shape
    share = bins // planes
    here = lax.axis_index("rel")

    for t in range(tiles):
        left = remaining[t]
        for piece in arrived[1:]:
            left = add_emissions(left, piece, bins, t)
        residual[t] = weights[t] * left

    for d, piece in enumerate(arrived):
        source = lax.rem(here + (owners - d), owners)
        pieces = []
        for rank in range(capacity):
            place = piece[rank, bins : bins + 1, :]
            misfit = jnp.zeros((bins, pixels), F32)
            weight = jnp.zeros((bins, pixels), F32)
            for t in range(tiles):
                match = place == float(t)
                misfit = jnp.where(match, residual[t], misfit)
                weight = jnp.where(match, weights[t], weight)
            pieces.append((misfit, weight))
        for e in range(planes):
            rows = slice(e * share, (e + 1) * share)
            parts = [part[rows] for pair in pieces for part in pair]
            back[source * planes + e] = jnp.concatenate(parts, 0).astype(BF16)


def three_parts(values):
    high = values.astype(BF16).astype(F32)
    rest = values - high
    middle = rest.astype(BF16).astype(F32)
    return high, middle, rest - middle


def spread(row, base, count):
    turned = pltpu.roll(row, row.shape[1] - base, 1)
    return [jnp.broadcast_to(turned[:, u : u + 1], row.shape) for u in range(count)]


def minus_products(start, factors, rows):
    terms = [factor * row for factor, row in zip(factors, rows)]
    while len(terms) > 1:
        terms = [sum(terms[i : i + 2]) for i in range(0, len(terms), 2)]
    return start - terms[0]


def beside_zeros(rows, place):
    zeros = jnp.zeros_like(rows)
    pair = jnp.concatenate([zeros, rows] if place % 2 else [rows, zeros], 0).astype(BF16)
    blank = jnp.zeros_like(pair)
    return jnp.concatenate([pair if i == place // 2 else blank for i in range(TOGETHER // 2)], 0)


def pivot_rows(rows, base, lane):
    inside = (lane >= base) & (lane < base + PIVOTS)
    out = [
        jnp.where(inside, jnp.where(lane == base + t, 1.0, 0.0), rows[t]) for t in range(PIVOTS)
    ]
    turned = [pltpu.roll(row, lane.shape[1] - base, 1) for row in rows]
    block = [[None] * PIVOTS for _ in range(PIVOTS)]
    for u in range(PIVOTS):
        for t in range(u + 1):
            block[t][u] = jnp.broadcast_to(turned[t][:, u : u + 1], lane.shape)
    for j in range(PIVOTS):
        inverse = 1.0 / block[j][j]
        raw = list(block[j])
        out[j] = out[j] * inverse
        for u in range(j + 1, PIVOTS):
            block[j][u] = raw[u] * inverse
        for i in range(j + 1, PIVOTS):
            for u in range(i, PIVOTS):
                block[i][u] = block[i][u] - raw[i] * block[j][u]
            out[i] = out[i] - raw[i] * out[j]
    for j in range(PIVOTS - 1, 0, -1):
        for i in range(j):
            out[i] = out[i] - block[i][j] * out[j]
    return [jnp.where(inside, -row, row) for row in out]


def eliminate(matrix, ahead, panel, right_side):
    width = matrix.shape[1]
    steps = width // PIVOTS
    lane = lax.broadcasted_iota(jnp.int32, (ROWS, width), 1)
    thin = lax.broadcasted_iota(jnp.int32, (1, width), 1)
    def load(base):
        return [matrix[pl.ds(base + t, ROWS, stride=width), :] for t in range(PIVOTS)]

    def look_ahead(rows, base):
        turned = [pltpu.roll(row, width - base, 1) for row in rows]
        for t in range(PIVOTS):
            for u in range(PIVOTS):
                ahead[t * PIVOTS + u] = jnp.broadcast_to(turned[u][:, t : t + 1], lane.shape)

    def apply(vector, base, new):
        inside = (lane >= base) & (lane < base + PIVOTS)
        return minus_products(jnp.where(inside, 0.0, vector), spread(vector, base, PIVOTS), new)

    def one_panel(first, step, carry):
        new, vector = list(carry[:-1]), carry[-1]
        base = pl.multiple_of(step * PIVOTS, PIVOTS)
        following = pl.multiple_of(base + PIVOTS, PIVOTS)
        inside = (lane >= base) & (lane < base + PIVOTS)
        rows = [
            minus_products(
                jnp.where(inside, 0.0, row), [ahead[t * PIVOTS + u] for u in range(PIVOTS)], new
            )
            for t, row in enumerate(load(following))
        ]
        for t in range(PIVOTS):
            panel[pl.ds(t, ROWS, stride=PIVOTS), :] = new[t]
        old = [matrix[pl.ds(b * width + base, PIVOTS), :] for b in range(ROWS)]
        mine = [panel[b * PIVOTS : (b + 1) * PIVOTS, :] for b in range(ROWS)]
        within = (thin >= base) & (thin < base + PIVOTS)
        for group in range(0, ROWS, TOGETHER):
            thirds = zip(*[three_parts(row) for row in old[group : group + TOGETHER]])
            a1, a2, a3 = [jnp.concatenate(third, 0).astype(BF16) for third in thirds]
            turned = jnp.concatenate([a1, a2, a3, a1], 0).T[first:]
            right = []
            for b in range(TOGETHER):
                b1, b2, b3 = [beside_zeros(part, b) for part in three_parts(mine[group + b])]
                blank = jnp.zeros_like(b1)
                right.append(jnp.concatenate([b1, b1, b1, b3, b2, b2, blank, blank], 0))
            change = jnp.dot(
                jnp.concatenate([turned, turned], 1),
                jnp.concatenate(right, 1),
                preferred_element_type=F32,
            )
            for b in range(TOGETHER):
                rest = slice((group + b) * width + first, (group + b + 1) * width)
                matrix[rest, :] = (
                    jnp.where(within, 0.0, matrix[rest, :]) - change[:, b * width : (b + 1) * width]
                )
        newer = pivot_rows(rows, following, lane)
        look_ahead(rows, following + PIVOTS)
        return (*newer, apply(vector, base, new))

    rows = load(0)
    carry = (*pivot_rows(rows, 0, lane), right_side)
    look_ahead(rows, PIVOTS)
    phases = 4 if steps % 4 == 0 else 1
    length = steps // phases
    for phase in range(phases):
        low, high = max(phase * length - 1, 0), (phase + 1) * length - 1
        step = functools.partial(one_panel, phase * length * PIVOTS)
        carry = lax.fori_loop(low, high, step, carry)
    return apply(carry[-1], width - PIVOTS, list(carry[:-1]))


def newton_kernel(shifts, sides, capacity, group, *refs):
    plane = lax.axis_index(("bin", "rep"))
    planes = len(shifts)
    messages, (back, release, mean, prior, out, halves, gram, ahead, panel) = refs[:planes], refs[planes:]
    chunks, _, pixels = messages[0].shape
    owners = back.shape[0] // planes
    bins, releases = release.shape
    share = bins // planes
    pair = 2 * share
    top = share * releases
    if chunks > 1:
        gram[...] = jnp.zeros(gram.shape, F32)

    def one_chunk(prints, e, i, chunk):
        left = halves.at[i % 2]
        targets = prints[chunk, group * releases :, :].astype(F32)
        values = []
        for o in range(owners):
            block = back[o * planes + e].astype(F32)
            values.extend(block[r * pair : (r + 1) * pair] for r in range(capacity))
        for j in range(group):
            picked = jnp.zeros((pair, pixels), F32)
            for s, value in enumerate(values):
                picked = jnp.where(targets[j : j + 1] == float(s), value, picked)
            columns = slice(j * pixels, (j + 1) * pixels)
            block = prints[chunk, j * releases : (j + 1) * releases, :]
            for b in range(share):
                weight = jnp.broadcast_to(picked[share + b : share + b + 1], (2 * ROWS, pixels))
                weight = weight.astype(BF16)
                for r in range(0, releases, 2 * ROWS):
                    rows = slice(b * releases + r, b * releases + r + 2 * ROWS)
                    left[rows, columns] = block[r : r + 2 * ROWS] * weight
            if pair < 2 * ROWS:
                picked = jnp.concatenate([picked, jnp.zeros((2 * ROWS - pair, pixels), F32)], 0)
            left[top:, columns] = picked.astype(BF16)
        right = jnp.concatenate(
            [prints[chunk, j * releases : (j + 1) * releases, :] for j in range(group)], 1
        )
        product = lax.dot_general(
            left[...], right, (((1,), (1,)), ((), ())), preferred_element_type=F32
        )
        if i or chunks > 1:
            product += gram[: top + 2 * ROWS, :]
        gram[: top + 2 * ROWS, :] = product

    along, across = lax.div(plane, sides[1]), lax.rem(plane, sides[1])
    for i, (prints, (far, near)) in enumerate(zip(messages, shifts)):
        e = lax.rem(along + far, sides[0]) * sides[1] + lax.rem(across + near, sides[1])
        pl.loop(0, chunks, unroll=chunks == 1)(functools.partial(one_chunk, prints, e, i))

    def own(array):
        rows = array[...]
        mine = rows[:share]
        for e in range(1, planes):
            mine = jnp.where(plane == e, rows[e * share : (e + 1) * share], mine)
        if share < ROWS:
            mine = jnp.concatenate([mine, jnp.zeros((ROWS - share, releases), F32)], 0)
        return mine

    log_release, prior_mean, prior_weight = own(release), own(mean), own(prior)
    unslope = 1.0 + jnp.exp(-log_release)
    gradient = gram[top : top + ROWS, :]
    right_side = gradient - prior_weight * (log_release - prior_mean) * unslope
    diagonal = prior_weight * unslope * unslope
    row = lax.broadcasted_iota(jnp.int32, (releases, releases), 0)
    column = lax.broadcasted_iota(jnp.int32, (releases, releases), 1)
    for b in range(ROWS):
        block = slice(b * releases, (b + 1) * releases)
        if b < share:
            matrix = gram[block, :]
            matrix = 0.5 * (matrix + matrix.T)
            gram[block, :] = matrix + jnp.where(row == column, diagonal[b : b + 1], 0.0)
        else:
            gram[block, :] = jnp.where(row == column, 1.0, 0.0)
    systems = gram.at[pl.ds(0, ROWS * releases)]
    update = log_release + unslope * eliminate(systems, ahead, panel, right_side)
    out[...] = update[:share]


def newton_scratch(share, group, releases, pixels):
    height = share * releases + 2 * ROWS
    return [
        pltpu.VMEM((2, height, group * pixels), BF16),
        pltpu.VMEM((max(height, ROWS * releases), releases), F32),
        pltpu.VMEM((PIVOTS * PIVOTS, ROWS, releases), F32),
        pltpu.VMEM((ROWS * PIVOTS, releases), F32),
    ]


def shifted(array, axis, distance):
    if not distance:
        return array
    size = lax.axis_size(axis)
    return lax.ppermute(array, axis, [((i + distance) % size, i) for i in range(size)])


def params():
    return pltpu.CompilerParams(vmem_limit_bytes=LIMIT)


def body(
    footprint, block_tile, log_release, prior_mean, prior_weight, observed, noise_weight, pixel_mask
):
    blocks, releases, pixels = footprint.shape
    owners = lax.axis_size("rel")
    planes = lax.axis_size(("bin", "rep"))
    tiles, bins, _ = observed.shape
    capacity = blocks * 4 // 3 // owners
    slots = owners * capacity
    share = bins // planes
    group = math.gcd(blocks, 6)
    chunks = blocks // group
    local = pl.BlockSpec(memory_space=pltpu.VMEM)
    remote = pl.BlockSpec(memory_space=pltpu.HBM)
    release, mean, prior = log_release.T, prior_mean.T, prior_weight.T

    message, *sent = pl.pallas_call(
        functools.partial(emission_kernel, tiles, capacity, blocks),
        out_shape=(
            jax.ShapeDtypeStruct((chunks, group * releases + 2 * ROWS, pixels), BF16),
            *[jax.ShapeDtypeStruct((capacity, bins + ROWS, pixels), F32)] * owners,
        ),
        in_specs=[remote] * 3,
        out_specs=(local,) * (1 + owners),
        scratch_shapes=[
            pltpu.VMEM((slots, bins + ROWS, pixels), F32),
            pltpu.SMEM(block_tile.shape, jnp.int32),
            pltpu.VMEM(release.shape, F32),
            pltpu.SemaphoreType.DMA,
            pltpu.SemaphoreType.DMA,
            pltpu.SemaphoreType.DMA((chunks,)),
        ],
    )(block_tile, release, footprint.reshape(chunks, group * releases, pixels))
    arrived = [shifted(piece, "rel", owners - d if d else 0) for d, piece in enumerate(sent)]
    sides = (lax.axis_size("bin"), lax.axis_size("rep"))
    remaining, weights = pl.pallas_call(
        prepare_kernel,
        out_shape=(jax.ShapeDtypeStruct(observed.shape, F32),) * 2,
        in_specs=[local] * 4,
        out_specs=(local, local),
        compiler_params=params(),
    )(observed, noise_weight, pixel_mask, arrived[0])
    near = [shifted(message, "rep", d) for d in range(sides[1])]
    shifts, messages = [], []
    for far in range(sides[0]):
        moved = shifted(message, "bin", far)
        if far:
            moved, remaining, arrived[1:] = lax.optimization_barrier((moved, remaining, arrived[1:]))
        for d in range(sides[1]):
            shifts.append((far, d))
            messages.append(shifted(moved, "rep", d) if far else near[d])
    residual, back = pl.pallas_call(
        functools.partial(residual_kernel, planes, owners),
        out_shape=(
            jax.ShapeDtypeStruct(observed.shape, F32),
            jax.ShapeDtypeStruct((owners * planes, capacity * 2 * share, pixels), BF16),
        ),
        in_specs=[local] * (2 + owners),
        out_specs=(local, local),
        compiler_params=params(),
    )(remaining, weights, *arrived)
    back, messages = lax.optimization_barrier((back, messages))
    back = lax.all_to_all(back, ("rel", "bin", "rep"), split_axis=0, concat_axis=0, tiled=True)

    release_new = pl.pallas_call(
        functools.partial(newton_kernel, shifts, sides, capacity, group),
        out_shape=jax.ShapeDtypeStruct((share, releases), F32),
        in_specs=[local] * (planes + 4),
        out_specs=local,
        scratch_shapes=newton_scratch(share, group, releases, pixels),
        compiler_params=params(),
    )(*messages, back, release, mean, prior)
    return (release_new.T, residual)


def solution(mesh):
    in_specs = (
        P(("groups", "rel", "bin", "rep"), None, None),
        P(("groups", "rel", "bin", "rep")),
        P(("groups", "rel"), None),
        P(("groups", "rel"), None),
        P(("groups", "rel"), None),
        P(("groups", "rel", "bin", "rep"), None, None),
        P(("groups", "rel", "bin", "rep"), None, None),
        P(("groups", "rel", "bin", "rep"), None),
    )
    out_specs = (
        P(("groups", "rel"), ("bin", "rep")),
        P(("groups", "rel", "bin", "rep"), None, None),
    )
    return jax.shard_map(body, mesh=mesh, in_specs=in_specs, out_specs=out_specs, check_vma=False)
```

```python
import functools
import math

import jax
import jax.numpy as jnp
from jax import lax
from jax.experimental import pallas as pl
from jax.experimental.pallas import tpu as pltpu
from jax.sharding import PartitionSpec as P

PIVOTS = 8
ROWS = 8
TOGETHER = 4
LIMIT = 48 << 20
F32 = jnp.float32
BF16 = jnp.bfloat16


def emission_kernel(
    tiles, capacity, blocks, tile_source, release_source, print_source, message, *refs
):
    owners = len(refs) - 6
    pieces, (sent, tile_of, release, tile_ready, release_ready, print_ready) = (
        refs[:owners],
        refs[owners:],
    )
    here = lax.axis_index("rel")
    chunks, length, pixels = print_source.shape
    group = blocks // chunks
    releases = length // group
    slots, padded, _ = sent.shape
    bins = padded - ROWS
    copies = [
        pltpu.make_async_copy(
            print_source.at[c], message.at[c, pl.ds(0, length)], print_ready.at[c]
        )
        for c in range(chunks)
    ]
    tile_copy = pltpu.make_async_copy(tile_source, tile_of, tile_ready)
    release_copy = pltpu.make_async_copy(release_source, release, release_ready)
    tile_copy.start()
    release_copy.start()
    for copy in copies:
        copy.start()
    sent[...] = jnp.full(sent.shape, -1.0, F32)
    release_copy.wait()
    value = release[...]
    rates = (jnp.maximum(value, 0.0) + jnp.log1p(jnp.exp(-jnp.abs(value)))).astype(BF16)
    tile_copy.wait()
    owner, rank = None, None
    for c in range(chunks):
        copies[c].wait()
        rows = []
        for j in range(group):
            k = c * group + j
            mine = lax.div(tile_of[k], tiles)
            rank = jnp.where(mine == owner, rank + 1, 0) if k else 0
            owner = mine
            target = owner * capacity + rank
            emission = lax.dot_general(
                rates,
                message[c, j * releases : (j + 1) * releases, :],
                (((1,), (0,)), ((), ())),
                preferred_element_type=F32,
            )
            local = lax.rem(tile_of[k], tiles).astype(F32)
            place = lax.rem(owner + (owners - here), owners) * capacity + rank
            sent[place, :bins, :] = emission
            sent[place, bins:, :] = jnp.full((ROWS, pixels), local, F32)
            rows.append(jnp.full((1, pixels), target.astype(F32), F32))
        rows.append(jnp.full((2 * ROWS - group, pixels), -1.0, F32))
        message[c, length:, :] = jnp.concatenate(rows, 0).astype(BF16)
    for d, piece in enumerate(pieces):
        piece[...] = sent[d * capacity : (d + 1) * capacity]


def add_emissions(start, piece, bins, tile):
    for rank in range(piece.shape[0]):
        match = piece[rank, bins : bins + 1, :] == float(tile)
        start = start - jnp.where(match, piece[rank, :bins, :], 0.0)
    return start


def prepare_kernel(observed, noise, mask, own, remaining, weights):
    tiles, bins, _ = observed.shape
    for t in range(tiles):
        weights[t] = mask[t : t + 1, :].astype(F32) * noise[t]
        remaining[t] = add_emissions(observed[t], own, bins, t)


def residual_kernel(planes, owners, remaining, weights, *refs):
    arrived, (residual, back) = refs[:owners], refs[owners:]
    capacity, padded, pixels = arrived[0].shape
    tiles, bins, _ = remaining.shape
    share = bins // planes
    here = lax.axis_index("rel")

    for t in range(tiles):
        left = remaining[t]
        for piece in arrived[1:]:
            left = add_emissions(left, piece, bins, t)
        residual[t] = weights[t] * left

    for d, piece in enumerate(arrived):
        source = lax.rem(here + (owners - d), owners)
        pieces = []
        for rank in range(capacity):
            place = piece[rank, bins : bins + 1, :]
            misfit = jnp.zeros((bins, pixels), F32)
            weight = jnp.zeros((bins, pixels), F32)
            for t in range(tiles):
                match = place == float(t)
                misfit = jnp.where(match, residual[t], misfit)
                weight = jnp.where(match, weights[t], weight)
            pieces.append((misfit, weight))
        for e in range(planes):
            rows = slice(e * share, (e + 1) * share)
            parts = [part[rows] for pair in pieces for part in pair]
            back[source * planes + e] = jnp.concatenate(parts, 0).astype(BF16)


def three_parts(values):
    high = values.astype(BF16).astype(F32)
    rest = values - high
    middle = rest.astype(BF16).astype(F32)
    return high, middle, rest - middle


def spread(row, base, count):
    turned = pltpu.roll(row, row.shape[1] - base, 1)
    return [jnp.broadcast_to(turned[:, u : u + 1], row.shape) for u in range(count)]


def minus_products(start, factors, rows):
    terms = [factor * row for factor, row in zip(factors, rows)]
    while len(terms) > 1:
        terms = [sum(terms[i : i + 2]) for i in range(0, len(terms), 2)]
    return start - terms[0]


def beside_zeros(rows, place):
    zeros = jnp.zeros_like(rows)
    pair = jnp.concatenate([zeros, rows] if place % 2 else [rows, zeros], 0).astype(BF16)
    blank = jnp.zeros_like(pair)
    return jnp.concatenate([pair if i == place // 2 else blank for i in range(TOGETHER // 2)], 0)


def pivot_rows(rows, base, lane):
    inside = (lane >= base) & (lane < base + PIVOTS)
    out = [
        jnp.where(inside, jnp.where(lane == base + t, 1.0, 0.0), rows[t]) for t in range(PIVOTS)
    ]
    turned = [pltpu.roll(row, lane.shape[1] - base, 1) for row in rows]
    block = [[None] * PIVOTS for _ in range(PIVOTS)]
    for u in range(PIVOTS):
        for t in range(u + 1):
            block[t][u] = jnp.broadcast_to(turned[t][:, u : u + 1], lane.shape)
    for j in range(PIVOTS):
        inverse = 1.0 / block[j][j]
        raw = list(block[j])
        out[j] = out[j] * inverse
        for u in range(j + 1, PIVOTS):
            block[j][u] = raw[u] * inverse
        for i in range(j + 1, PIVOTS):
            for u in range(i, PIVOTS):
                block[i][u] = block[i][u] - raw[i] * block[j][u]
            out[i] = out[i] - raw[i] * out[j]
    for j in range(PIVOTS - 1, 0, -1):
        for i in range(j):
            out[i] = out[i] - block[i][j] * out[j]
    return [jnp.where(inside, -row, row) for row in out]


def eliminate(matrix, ahead, panel, right_side):
    width = matrix.shape[1]
    steps = width // PIVOTS
    lane = lax.broadcasted_iota(jnp.int32, (ROWS, width), 1)
    thin = lax.broadcasted_iota(jnp.int32, (1, width), 1)
    def load(base):
        return [matrix[pl.ds(base + t, ROWS, stride=width), :] for t in range(PIVOTS)]

    def look_ahead(rows, base):
        turned = [pltpu.roll(row, width - base, 1) for row in rows]
        for t in range(PIVOTS):
            for u in range(PIVOTS):
                ahead[t * PIVOTS + u] = jnp.broadcast_to(turned[u][:, t : t + 1], lane.shape)

    def apply(vector, base, new):
        inside = (lane >= base) & (lane < base + PIVOTS)
        return minus_products(jnp.where(inside, 0.0, vector), spread(vector, base, PIVOTS), new)

    def one_panel(first, step, carry):
        new, vector = list(carry[:-1]), carry[-1]
        base = pl.multiple_of(step * PIVOTS, PIVOTS)
        following = pl.multiple_of(base + PIVOTS, PIVOTS)
        inside = (lane >= base) & (lane < base + PIVOTS)
        rows = [
            minus_products(
                jnp.where(inside, 0.0, row), [ahead[t * PIVOTS + u] for u in range(PIVOTS)], new
            )
            for t, row in enumerate(load(following))
        ]
        for t in range(PIVOTS):
            panel[pl.ds(t, ROWS, stride=PIVOTS), :] = new[t]
        old = [matrix[pl.ds(b * width + base, PIVOTS), :] for b in range(ROWS)]
        mine = [panel[b * PIVOTS : (b + 1) * PIVOTS, :] for b in range(ROWS)]
        within = (thin >= base) & (thin < base + PIVOTS)
        for group in range(0, ROWS, TOGETHER):
            thirds = zip(*[three_parts(row) for row in old[group : group + TOGETHER]])
            a1, a2, a3 = [jnp.concatenate(third, 0).astype(BF16) for third in thirds]
            turned = jnp.concatenate([a1, a2, a3, a1], 0).T[first:]
            right = []
            for b in range(TOGETHER):
                b1, b2, b3 = [beside_zeros(part, b) for part in three_parts(mine[group + b])]
                blank = jnp.zeros_like(b1)
                right.append(jnp.concatenate([b1, b1, b1, b3, b2, b2, blank, blank], 0))
            change = jnp.dot(
                jnp.concatenate([turned, turned], 1),
                jnp.concatenate(right, 1),
                preferred_element_type=F32,
            )
            for b in range(TOGETHER):
                rest = slice((group + b) * width + first, (group + b + 1) * width)
                matrix[rest, :] = (
                    jnp.where(within, 0.0, matrix[rest, :]) - change[:, b * width : (b + 1) * width]
                )
        newer = pivot_rows(rows, following, lane)
        look_ahead(rows, following + PIVOTS)
        return (*newer, apply(vector, base, new))

    rows = load(0)
    carry = (*pivot_rows(rows, 0, lane), right_side)
    look_ahead(rows, PIVOTS)
    phases = 8 if steps % 8 == 0 else 1
    length = steps // phases
    for phase in range(phases):
        low, high = max(phase * length - 1, 0), (phase + 1) * length - 1
        step = functools.partial(one_panel, phase * length * PIVOTS)
        carry = lax.fori_loop(low, high, step, carry)
    return apply(carry[-1], width - PIVOTS, list(carry[:-1]))


def newton_kernel(shifts, sides, capacity, group, *refs):
    plane = lax.axis_index(("bin", "rep"))
    planes = len(shifts)
    messages, (back, release, mean, prior, out, scaled, gram, ahead, panel) = refs[:planes], refs[planes:]
    chunks, _, pixels = messages[0].shape
    owners = back.shape[0] // planes
    bins, releases = release.shape
    share = bins // planes
    pair = 2 * share
    top = share * releases
    if chunks > 1:
        gram[...] = jnp.zeros(gram.shape, F32)

    def one_chunk(prints, e, i, chunk):
        left = scaled.at[i]
        targets = prints[chunk, group * releases :, :].astype(F32)
        values = []
        for o in range(owners):
            block = back[o * planes + e].astype(F32)
            values.extend(block[r * pair : (r + 1) * pair] for r in range(capacity))
        for j in range(group):
            picked = jnp.zeros((pair, pixels), F32)
            for s, value in enumerate(values):
                picked = jnp.where(targets[j : j + 1] == float(s), value, picked)
            columns = slice(j * pixels, (j + 1) * pixels)
            block = prints[chunk, j * releases : (j + 1) * releases, :]
            for b in range(share):
                weight = jnp.broadcast_to(picked[share + b : share + b + 1], (2 * ROWS, pixels))
                weight = weight.astype(BF16)
                for r in range(0, releases, 2 * ROWS):
                    rows = slice(b * releases + r, b * releases + r + 2 * ROWS)
                    left[rows, columns] = block[r : r + 2 * ROWS] * weight
            if pair < 2 * ROWS:
                picked = jnp.concatenate([picked, jnp.zeros((2 * ROWS - pair, pixels), F32)], 0)
            left[top:, columns] = picked.astype(BF16)
        right = jnp.concatenate(
            [prints[chunk, j * releases : (j + 1) * releases, :] for j in range(group)], 1
        )
        product = lax.dot_general(
            left[...], right, (((1,), (1,)), ((), ())), preferred_element_type=F32
        )
        if i or chunks > 1:
            product += gram[: top + 2 * ROWS, :]
        gram[: top + 2 * ROWS, :] = product

    along, across = lax.div(plane, sides[1]), lax.rem(plane, sides[1])
    for i, (prints, (far, near)) in enumerate(zip(messages, shifts)):
        e = lax.rem(along + far, sides[0]) * sides[1] + lax.rem(across + near, sides[1])
        pl.loop(0, chunks, unroll=chunks == 1)(functools.partial(one_chunk, prints, e, i))

    def own(array):
        rows = array[...]
        mine = rows[:share]
        for e in range(1, planes):
            mine = jnp.where(plane == e, rows[e * share : (e + 1) * share], mine)
        if share < ROWS:
            mine = jnp.concatenate([mine, jnp.zeros((ROWS - share, releases), F32)], 0)
        return mine

    log_release, prior_mean, prior_weight = own(release), own(mean), own(prior)
    unslope = 1.0 + jnp.exp(-log_release)
    gradient = gram[top : top + ROWS, :]
    right_side = gradient - prior_weight * (log_release - prior_mean) * unslope
    diagonal = prior_weight * unslope * unslope
    row = lax.broadcasted_iota(jnp.int32, (releases, releases), 0)
    column = lax.broadcasted_iota(jnp.int32, (releases, releases), 1)
    for b in range(ROWS):
        block = slice(b * releases, (b + 1) * releases)
        if b < share:
            matrix = gram[block, :]
            matrix = 0.5 * (matrix + matrix.T)
            gram[block, :] = matrix + jnp.where(row == column, diagonal[b : b + 1], 0.0)
        else:
            gram[block, :] = jnp.where(row == column, 1.0, 0.0)
    systems = gram.at[pl.ds(0, ROWS * releases)]
    update = log_release + unslope * eliminate(systems, ahead, panel, right_side)
    out[...] = update[:share]


def newton_scratch(planes, share, group, releases, pixels):
    height = share * releases + 2 * ROWS
    return [
        pltpu.VMEM((planes, height, group * pixels), BF16),
        pltpu.VMEM((max(height, ROWS * releases), releases), F32),
        pltpu.VMEM((PIVOTS * PIVOTS, ROWS, releases), F32),
        pltpu.VMEM((ROWS * PIVOTS, releases), F32),
    ]


def shifted(array, axis, distance):
    if not distance:
        return array
    size = lax.axis_size(axis)
    return lax.ppermute(array, axis, [((i + distance) % size, i) for i in range(size)])


def params():
    return pltpu.CompilerParams(vmem_limit_bytes=LIMIT)


def body(
    footprint, block_tile, log_release, prior_mean, prior_weight, observed, noise_weight, pixel_mask
):
    blocks, releases, pixels = footprint.shape
    owners = lax.axis_size("rel")
    planes = lax.axis_size(("bin", "rep"))
    tiles, bins, _ = observed.shape
    capacity = blocks * 4 // 3 // owners
    slots = owners * capacity
    share = bins // planes
    group = math.gcd(blocks, 6)
    chunks = blocks // group
    local = pl.BlockSpec(memory_space=pltpu.VMEM)
    remote = pl.BlockSpec(memory_space=pltpu.HBM)
    release, mean, prior = log_release.T, prior_mean.T, prior_weight.T

    message, *sent = pl.pallas_call(
        functools.partial(emission_kernel, tiles, capacity, blocks),
        out_shape=(
            jax.ShapeDtypeStruct((chunks, group * releases + 2 * ROWS, pixels), BF16),
            *[jax.ShapeDtypeStruct((capacity, bins + ROWS, pixels), F32)] * owners,
        ),
        in_specs=[remote] * 3,
        out_specs=(local,) * (1 + owners),
        scratch_shapes=[
            pltpu.VMEM((slots, bins + ROWS, pixels), F32),
            pltpu.SMEM(block_tile.shape, jnp.int32),
            pltpu.VMEM(release.shape, F32),
            pltpu.SemaphoreType.DMA,
            pltpu.SemaphoreType.DMA,
            pltpu.SemaphoreType.DMA((chunks,)),
        ],
    )(block_tile, release, footprint.reshape(chunks, group * releases, pixels))
    arrived = [shifted(piece, "rel", owners - d if d else 0) for d, piece in enumerate(sent)]
    sides = (lax.axis_size("bin"), lax.axis_size("rep"))
    shifts, messages = [], []
    for far in range(sides[0]):
        moved = shifted(message, "bin", far)
        for near in range(sides[1]):
            shifts.append((far, near))
            messages.append(shifted(moved, "rep", near))

    remaining, weights = pl.pallas_call(
        prepare_kernel,
        out_shape=(jax.ShapeDtypeStruct(observed.shape, F32),) * 2,
        in_specs=[local] * 4,
        out_specs=(local, local),
        compiler_params=params(),
    )(observed, noise_weight, pixel_mask, arrived[0])
    arrived[1:], messages[1:-1] = lax.optimization_barrier((arrived[1:], messages[1:-1]))
    residual, back = pl.pallas_call(
        functools.partial(residual_kernel, planes, owners),
        out_shape=(
            jax.ShapeDtypeStruct(observed.shape, F32),
            jax.ShapeDtypeStruct((owners * planes, capacity * 2 * share, pixels), BF16),
        ),
        in_specs=[local] * (2 + owners),
        out_specs=(local, local),
        compiler_params=params(),
    )(remaining, weights, *arrived)
    back = lax.all_to_all(back, ("rel", "bin", "rep"), split_axis=0, concat_axis=0, tiled=True)

    release_new = pl.pallas_call(
        functools.partial(newton_kernel, shifts, sides, capacity, group),
        out_shape=jax.ShapeDtypeStruct((share, releases), F32),
        in_specs=[local] * (planes + 4),
        out_specs=local,
        scratch_shapes=newton_scratch(planes, share, group, releases, pixels),
        compiler_params=params(),
    )(*messages, back, release, mean, prior)
    return (release_new.T, residual)


def solution(mesh):
    in_specs = (
        P(("groups", "rel", "bin", "rep"), None, None),
        P(("groups", "rel", "bin", "rep")),
        P(("groups", "rel"), None),
        P(("groups", "rel"), None),
        P(("groups", "rel"), None),
        P(("groups", "rel", "bin", "rep"), None, None),
        P(("groups", "rel", "bin", "rep"), None, None),
        P(("groups", "rel", "bin", "rep"), None),
    )
    out_specs = (
        P(("groups", "rel"), ("bin", "rep")),
        P(("groups", "rel", "bin", "rep"), None, None),
    )
    return jax.shard_map(body, mesh=mesh, in_specs=in_specs, out_specs=out_specs, check_vma=False)
```

```python
import functools
import math

import jax
import jax.numpy as jnp
from jax import lax
from jax.experimental import pallas as pl
from jax.experimental.pallas import tpu as pltpu
from jax.sharding import PartitionSpec as P

PIVOTS = 8
ROWS = 8
TOGETHER = 4
LIMIT = 48 << 20
F32 = jnp.float32
BF16 = jnp.bfloat16


def emission_kernel(tiles, capacity, tile_source, release_source, print_source, *refs):
    pieces, scratch = refs[:-7], refs[-7:]
    sent, tile_of, release, prints, tile_ready, release_ready, print_ready = scratch
    blocks, _, pixels = prints.shape
    owners = len(pieces)
    bins = release.shape[0]
    here = lax.axis_index("rel")
    tile_copy = pltpu.make_async_copy(tile_source, tile_of, tile_ready)
    release_copy = pltpu.make_async_copy(release_source, release, release_ready)
    print_copy = pltpu.make_async_copy(print_source, prints, print_ready)
    for copy in [tile_copy, release_copy, print_copy]:
        copy.start()
    sent[...] = jnp.full(sent.shape, -1.0, F32)
    release_copy.wait()
    value = release[...]
    rates = (jnp.maximum(value, 0.0) + jnp.log1p(jnp.exp(-jnp.abs(value)))).astype(BF16)
    tile_copy.wait()
    print_copy.wait()
    owner, rank = None, None
    for k in range(blocks):
        mine = lax.div(tile_of[k], tiles)
        rank = jnp.where(mine == owner, rank + 1, 0) if k else 0
        owner = mine
        place = lax.rem(owner + (owners - here), owners) * capacity + rank
        sent[place, :bins, :] = lax.dot_general(
            rates, prints[k], (((1,), (0,)), ((), ())), preferred_element_type=F32
        )
        local = lax.rem(tile_of[k], tiles).astype(F32)
        sent[place, bins:, :] = jnp.full((ROWS, pixels), local, F32)
    for d, piece in enumerate(pieces):
        piece[...] = sent[d * capacity : (d + 1) * capacity]


def add_emissions(start, piece, bins, tile):
    for rank in range(piece.shape[0]):
        match = piece[rank, bins : bins + 1, :] == float(tile)
        start = start - jnp.where(match, piece[rank, :bins, :], 0.0)
    return start


def prepare_kernel(observed, noise, mask, own, remaining, weights):
    tiles, bins, _ = observed.shape
    for t in range(tiles):
        weights[t] = mask[t : t + 1, :].astype(F32) * noise[t]
        remaining[t] = add_emissions(observed[t], own, bins, t)


def residual_kernel(planes, owners, remaining, weights, *refs):
    arrived, (residual, back) = refs[:owners], refs[owners:]
    capacity, padded, pixels = arrived[0].shape
    tiles, bins, _ = remaining.shape
    share = bins // planes
    here = lax.axis_index("rel")

    for t in range(tiles):
        left = remaining[t]
        for piece in arrived[1:]:
            left = add_emissions(left, piece, bins, t)
        residual[t] = weights[t] * left

    for d, piece in enumerate(arrived):
        source = lax.rem(here + (owners - d), owners)
        pieces = []
        for rank in range(capacity):
            place = piece[rank, bins : bins + 1, :]
            misfit = jnp.zeros((bins, pixels), F32)
            weight = jnp.full((bins, pixels), -1.0, F32)
            for t in range(tiles):
                match = place == float(t)
                misfit = jnp.where(match, residual[t], misfit)
                weight = jnp.where(match, weights[t], weight)
            pieces.append((misfit, weight))
        for e in range(planes):
            rows = slice(e * share, (e + 1) * share)
            parts = [part[rows] for pair in pieces for part in pair]
            back[source * planes + e] = jnp.concatenate(parts, 0).astype(BF16)


def three_parts(values):
    high = values.astype(BF16).astype(F32)
    rest = values - high
    middle = rest.astype(BF16).astype(F32)
    return high, middle, rest - middle


def spread(row, base, count):
    turned = pltpu.roll(row, row.shape[1] - base, 1)
    return [jnp.broadcast_to(turned[:, u : u + 1], row.shape) for u in range(count)]


def minus_products(start, factors, rows):
    terms = [factor * row for factor, row in zip(factors, rows)]
    while len(terms) > 1:
        terms = [sum(terms[i : i + 2]) for i in range(0, len(terms), 2)]
    return start - terms[0]


def beside_zeros(rows, place):
    zeros = jnp.zeros_like(rows)
    pair = jnp.concatenate([zeros, rows] if place % 2 else [rows, zeros], 0).astype(BF16)
    blank = jnp.zeros_like(pair)
    return jnp.concatenate([pair if i == place // 2 else blank for i in range(TOGETHER // 2)], 0)


def pivot_rows(rows, base, lane):
    inside = (lane >= base) & (lane < base + PIVOTS)
    out = [
        jnp.where(inside, jnp.where(lane == base + t, 1.0, 0.0), rows[t]) for t in range(PIVOTS)
    ]
    turned = [pltpu.roll(row, lane.shape[1] - base, 1) for row in rows]
    block = [[None] * PIVOTS for _ in range(PIVOTS)]
    for u in range(PIVOTS):
        for t in range(u + 1):
            block[t][u] = jnp.broadcast_to(turned[t][:, u : u + 1], lane.shape)
    for j in range(PIVOTS):
        inverse = 1.0 / block[j][j]
        raw = list(block[j])
        out[j] = out[j] * inverse
        for u in range(j + 1, PIVOTS):
            block[j][u] = raw[u] * inverse
        for i in range(j + 1, PIVOTS):
            for u in range(i, PIVOTS):
                block[i][u] = block[i][u] - raw[i] * block[j][u]
            out[i] = out[i] - raw[i] * out[j]
    for j in range(PIVOTS - 1, 0, -1):
        for i in range(j):
            out[i] = out[i] - block[i][j] * out[j]
    return [jnp.where(inside, -row, row) for row in out]


def eliminate(matrix, ahead, panel, right_side):
    width = matrix.shape[1]
    steps = width // PIVOTS
    lane = lax.broadcasted_iota(jnp.int32, (ROWS, width), 1)
    thin = lax.broadcasted_iota(jnp.int32, (1, width), 1)
    def load(base):
        return [matrix[pl.ds(base + t, ROWS, stride=width), :] for t in range(PIVOTS)]

    def look_ahead(rows, base):
        turned = [pltpu.roll(row, width - base, 1) for row in rows]
        for t in range(PIVOTS):
            for u in range(PIVOTS):
                ahead[t * PIVOTS + u] = jnp.broadcast_to(turned[u][:, t : t + 1], lane.shape)

    def apply(vector, base, new):
        inside = (lane >= base) & (lane < base + PIVOTS)
        return minus_products(jnp.where(inside, 0.0, vector), spread(vector, base, PIVOTS), new)

    def one_panel(first, step, carry):
        new, vector = list(carry[:-1]), carry[-1]
        base = pl.multiple_of(step * PIVOTS, PIVOTS)
        following = pl.multiple_of(base + PIVOTS, PIVOTS)
        inside = (lane >= base) & (lane < base + PIVOTS)
        rows = [
            minus_products(
                jnp.where(inside, 0.0, row), [ahead[t * PIVOTS + u] for u in range(PIVOTS)], new
            )
            for t, row in enumerate(load(following))
        ]
        for t in range(PIVOTS):
            panel[pl.ds(t, ROWS, stride=PIVOTS), :] = new[t]
        old = [matrix[pl.ds(b * width + base, PIVOTS), :] for b in range(ROWS)]
        mine = [panel[b * PIVOTS : (b + 1) * PIVOTS, :] for b in range(ROWS)]
        within = (thin >= base) & (thin < base + PIVOTS)
        for group in range(0, ROWS, TOGETHER):
            thirds = zip(*[three_parts(row) for row in old[group : group + TOGETHER]])
            a1, a2, a3 = [jnp.concatenate(third, 0).astype(BF16) for third in thirds]
            turned = jnp.concatenate([a1, a2, a3, a1], 0).T[first:]
            right = []
            for b in range(TOGETHER):
                b1, b2, b3 = [beside_zeros(part, b) for part in three_parts(mine[group + b])]
                blank = jnp.zeros_like(b1)
                right.append(jnp.concatenate([b1, b1, b1, b3, b2, b2, blank, blank], 0))
            change = jnp.dot(
                jnp.concatenate([turned, turned], 1),
                jnp.concatenate(right, 1),
                preferred_element_type=F32,
            )
            for b in range(TOGETHER):
                rest = slice((group + b) * width + first, (group + b + 1) * width)
                matrix[rest, :] = (
                    jnp.where(within, 0.0, matrix[rest, :]) - change[:, b * width : (b + 1) * width]
                )
        newer = pivot_rows(rows, following, lane)
        look_ahead(rows, following + PIVOTS)
        return (*newer, apply(vector, base, new))

    rows = load(0)
    carry = (*pivot_rows(rows, 0, lane), right_side)
    look_ahead(rows, PIVOTS)
    phases = 8 if steps % 8 == 0 else 1
    length = steps // phases
    for phase in range(phases):
        low, high = max(phase * length - 1, 0), (phase + 1) * length - 1
        step = functools.partial(one_panel, phase * length * PIVOTS)
        carry = lax.fori_loop(low, high, step, carry)
    return apply(carry[-1], width - PIVOTS, list(carry[:-1]))


def newton_kernel(shifts, sides, capacity, group, *refs):
    plane = lax.axis_index(("bin", "rep"))
    planes = len(shifts)
    messages, (back, release, mean, prior, out, scaled, gram, ahead, panel) = refs[:planes], refs[planes:]
    chunks, _, pixels = messages[0].shape
    owners = back.shape[0] // planes
    bins, releases = release.shape
    share = bins // planes
    pair = 2 * share
    top = share * releases
    if chunks > 1:
        gram[...] = jnp.zeros(gram.shape, F32)

    def one_chunk(prints, e, i, chunk):
        left = scaled.at[i]
        slots = []
        count = jnp.zeros((1, pixels), F32) - (chunk * group).astype(F32)
        for o in range(owners):
            block = back[o * planes + e].astype(F32)
            for r in range(capacity):
                value = block[r * pair : (r + 1) * pair]
                used = value[share : share + 1] >= 0.0
                slots.append((jnp.where(used, count, -1.0), value))
                count = count + jnp.where(used, 1.0, 0.0)
        for j in range(group):
            picked = jnp.zeros((pair, pixels), F32)
            for index, value in slots:
                picked = jnp.where(index == float(j), value, picked)
            columns = slice(j * pixels, (j + 1) * pixels)
            block = prints[chunk, j * releases : (j + 1) * releases, :]
            for b in range(share):
                weight = jnp.broadcast_to(picked[share + b : share + b + 1], (2 * ROWS, pixels))
                weight = weight.astype(BF16)
                for r in range(0, releases, 2 * ROWS):
                    rows = slice(b * releases + r, b * releases + r + 2 * ROWS)
                    left[rows, columns] = block[r : r + 2 * ROWS] * weight
            if pair < 2 * ROWS:
                picked = jnp.concatenate([picked, jnp.zeros((2 * ROWS - pair, pixels), F32)], 0)
            left[top:, columns] = picked.astype(BF16)
        right = jnp.concatenate(
            [prints[chunk, j * releases : (j + 1) * releases, :] for j in range(group)], 1
        )
        product = lax.dot_general(
            left[...], right, (((1,), (1,)), ((), ())), preferred_element_type=F32
        )
        if i or chunks > 1:
            product += gram[: top + 2 * ROWS, :]
        gram[: top + 2 * ROWS, :] = product

    along, across = lax.div(plane, sides[1]), lax.rem(plane, sides[1])
    for i, (prints, (far, near)) in enumerate(zip(messages, shifts)):
        e = lax.rem(along + far, sides[0]) * sides[1] + lax.rem(across + near, sides[1])
        pl.loop(0, chunks, unroll=chunks == 1)(functools.partial(one_chunk, prints, e, i))

    def own(array):
        rows = array[...]
        mine = rows[:share]
        for e in range(1, planes):
            mine = jnp.where(plane == e, rows[e * share : (e + 1) * share], mine)
        if share < ROWS:
            mine = jnp.concatenate([mine, jnp.zeros((ROWS - share, releases), F32)], 0)
        return mine

    log_release, prior_mean, prior_weight = own(release), own(mean), own(prior)
    unslope = 1.0 + jnp.exp(-log_release)
    gradient = gram[top : top + ROWS, :]
    right_side = gradient - prior_weight * (log_release - prior_mean) * unslope
    diagonal = prior_weight * unslope * unslope
    row = lax.broadcasted_iota(jnp.int32, (releases, releases), 0)
    column = lax.broadcasted_iota(jnp.int32, (releases, releases), 1)
    for b in range(ROWS):
        block = slice(b * releases, (b + 1) * releases)
        if b < share:
            matrix = gram[block, :]
            matrix = 0.5 * (matrix + matrix.T)
            gram[block, :] = matrix + jnp.where(row == column, diagonal[b : b + 1], 0.0)
        else:
            gram[block, :] = jnp.where(row == column, 1.0, 0.0)
    systems = gram.at[pl.ds(0, ROWS * releases)]
    update = log_release + unslope * eliminate(systems, ahead, panel, right_side)
    out[...] = update[:share]


def newton_scratch(planes, share, group, releases, pixels):
    height = share * releases + 2 * ROWS
    return [
        pltpu.VMEM((planes, height, group * pixels), BF16),
        pltpu.VMEM((max(height, ROWS * releases), releases), F32),
        pltpu.VMEM((PIVOTS * PIVOTS, ROWS, releases), F32),
        pltpu.VMEM((ROWS * PIVOTS, releases), F32),
    ]


def shifted(array, axis, distance):
    if not distance:
        return array
    size = lax.axis_size(axis)
    return lax.ppermute(array, axis, [((i + distance) % size, i) for i in range(size)])


def params():
    return pltpu.CompilerParams(vmem_limit_bytes=LIMIT)


def body(
    footprint, block_tile, log_release, prior_mean, prior_weight, observed, noise_weight, pixel_mask
):
    blocks, releases, pixels = footprint.shape
    owners = lax.axis_size("rel")
    planes = lax.axis_size(("bin", "rep"))
    tiles, bins, _ = observed.shape
    capacity = blocks * 4 // 3 // owners
    slots = owners * capacity
    share = bins // planes
    group = math.gcd(blocks, 6)
    chunks = blocks // group
    local = pl.BlockSpec(memory_space=pltpu.VMEM)
    remote = pl.BlockSpec(memory_space=pltpu.HBM)
    release, mean, prior = log_release.T, prior_mean.T, prior_weight.T

    message = footprint.reshape(chunks, group * releases, pixels)
    sent = pl.pallas_call(
        functools.partial(emission_kernel, tiles, capacity),
        out_shape=[jax.ShapeDtypeStruct((capacity, bins + ROWS, pixels), F32)] * owners,
        in_specs=[remote] * 3,
        out_specs=[local] * owners,
        scratch_shapes=[
            pltpu.VMEM((slots, bins + ROWS, pixels), F32),
            pltpu.SMEM(block_tile.shape, jnp.int32),
            pltpu.VMEM(release.shape, F32),
            pltpu.VMEM(footprint.shape, BF16),
            pltpu.SemaphoreType.DMA,
            pltpu.SemaphoreType.DMA,
            pltpu.SemaphoreType.DMA,
        ],
    )(block_tile, release, footprint)
    message, sent = lax.optimization_barrier((message, sent))
    arrived = [shifted(piece, "rel", owners - d if d else 0) for d, piece in enumerate(sent)]
    sides = (lax.axis_size("bin"), lax.axis_size("rep"))
    shifts, messages = [], []
    for far in range(sides[0]):
        moved = shifted(message, "bin", far)
        for near in range(sides[1]):
            shifts.append((far, near))
            messages.append(shifted(moved, "rep", near))

    remaining, weights = pl.pallas_call(
        prepare_kernel,
        out_shape=(jax.ShapeDtypeStruct(observed.shape, F32),) * 2,
        in_specs=[local] * 4,
        out_specs=(local, local),
        compiler_params=params(),
    )(observed, noise_weight, pixel_mask, arrived[0])
    arrived[1:], messages[1:-1] = lax.optimization_barrier((arrived[1:], messages[1:-1]))
    residual, back = pl.pallas_call(
        functools.partial(residual_kernel, planes, owners),
        out_shape=(
            jax.ShapeDtypeStruct(observed.shape, F32),
            jax.ShapeDtypeStruct((owners * planes, capacity * 2 * share, pixels), BF16),
        ),
        in_specs=[local] * (2 + owners),
        out_specs=(local, local),
        compiler_params=params(),
    )(remaining, weights, *arrived)
    back = lax.all_to_all(back, ("rel", "bin", "rep"), split_axis=0, concat_axis=0, tiled=True)

    release_new = pl.pallas_call(
        functools.partial(newton_kernel, shifts, sides, capacity, group),
        out_shape=jax.ShapeDtypeStruct((share, releases), F32),
        in_specs=[local] * (planes + 4),
        out_specs=local,
        scratch_shapes=newton_scratch(planes, share, group, releases, pixels),
        compiler_params=params(),
    )(*messages, back, release, mean, prior)
    return (release_new.T, residual)


def solution(mesh):
    in_specs = (
        P(("groups", "rel", "bin", "rep"), None, None),
        P(("groups", "rel", "bin", "rep")),
        P(("groups", "rel"), None),
        P(("groups", "rel"), None),
        P(("groups", "rel"), None),
        P(("groups", "rel", "bin", "rep"), None, None),
        P(("groups", "rel", "bin", "rep"), None, None),
        P(("groups", "rel", "bin", "rep"), None),
    )
    out_specs = (
        P(("groups", "rel"), ("bin", "rep")),
        P(("groups", "rel", "bin", "rep"), None, None),
    )
    return jax.shard_map(body, mesh=mesh, in_specs=in_specs, out_specs=out_specs, check_vma=False)
```
